32 devices in a mesh: shard: 4 (over z), ctx: 2 (over x), tp: 4 (over y, core).
Axes of the slice: x: 2, y: 2, z: 4, core: 2. Of those that a mesh axis runs over, the one named last changes fastest.
Arguments:
- tokens: bfloat16 [4, 1024, 768], P('shard', 'ctx'), may hold values from -6 to 6
- segment_ids: int32 [4, 1024], P('shard', 'ctx'), may hold values from 0 to 15, never falling along the last dimension, each value on 1 to 512 neighbouring positions
- valid_mask: int32 [4, 1024], P('shard', 'ctx'), may hold values from 0 to 1, as said below
- qkv_weight: bfloat16 [3, 768, 768], P(None, ('shard', 'ctx'), 'tp'), may hold values from -0.21875 to 0.21875
- qv_bias: float32 [2, 768], P(None, 'tp'), may hold values from -0.4375 to 0.4375
- out_weight: bfloat16 [768, 768], P('tp', ('shard', 'ctx')), may hold values from -2.5 to 2.5
- out_bias: float32 [768], replicated, may hold values from -1.5 to 1.5
- norm1_gain: float32 [768], replicated, may hold values from 0.5 to 1.5
- norm1_shift: float32 [768], replicated, may hold values from -1.5 to 1.5
- in_weight: bfloat16 [768, 3072], P(('shard', 'ctx'), 'tp'), may hold values from -0.21875 to 0.21875
- in_bias: float32 [3072], P('tp'), may hold values from -4 to 4
- down_weight: bfloat16 [3072, 768], P('tp', ('shard', 'ctx')), may hold values from -0.109375 to 0.109375
- down_bias: float32 [768], replicated, may hold values from -1.5 to 1.5
- norm2_gain: float32 [768], replicated, may hold values from 0.5 to 1.5
- norm2_shift: float32 [768], replicated, may hold values from -1.5 to 1.5
- out_cotangent: float32 [4, 1024, 768], P('shard', 'ctx'), may hold values from -6 to 6
Outputs:
- layer_out: bfloat16 [4, 1024, 768], P('shard', 'ctx')
- tokens_grad: float32 [4, 1024, 768], P('shard', 'ctx')
- qkv_weight_grad: float32 [3, 768, 768], P(None, ('shard', 'ctx'), 'tp')
- qv_bias_grad: float32 [2, 768], P(None, 'tp')
- out_weight_grad: float32 [768, 768], P('tp', ('shard', 'ctx'))
- out_bias_grad: float32 [768], replicated
- norm1_gain_grad: float32 [768], replicated
- norm1_shift_grad: float32 [768], replicated
- in_weight_grad: float32 [768, 3072], P(('shard', 'ctx'), 'tp')
- in_bias_grad: float32 [3072], P('tp')
- down_weight_grad: float32 [3072, 768], P('tp', ('shard', 'ctx'))
- down_bias_grad: float32 [768], replicated
- norm2_gain_grad: float32 [768], replicated
- norm2_shift_grad: float32 [768], replicated
- stream_rms: float32 [3], replicated
The draws below stay inside these ranges and needn't reach their ends.
Inputs may be any that keep to these rules, and one draw needn't show every extreme that they name: `segment_ids`: in each sequence the document numbers never fall; each of the 16 documents holds 1 to 512 tokens, and one holds exactly 512. In each sequence the tokens with valid_mask 1 are a leading run of 512 to 1024 positions.
All inputs are finite; a program needn't handle non-finite values.
Results may differ from the reference program's by a relative error of at most 0.012.
Values may be sent and summed in bfloat16 or wider, within the bound.
A program may use at most 128 MiB of HBM per device.

```python
import math
import jax
import jax.numpy as jnp
import numpy as np
from jax import lax

D = 768
HEADS = 12
HEAD_DIM = 64
FF = 3072
DOCS = 16
SEQ_LEN = 1024
SEQS = 4


def draw_valid_mask(key, part):
    lengths = jax.random.randint(key, (SEQS,), SEQ_LEN // 2, SEQ_LEN + 1)
    positions = lax.broadcasted_iota(jnp.int32, (SEQS, SEQ_LEN), 1)
    return (positions < lengths[:, None]).astype(jnp.int32)


def shard_levels(own_key, dims, pieces, least, top_value):
    def one(position, blocks):
        heights = jax.random.uniform(jax.random.fold_in(jax.random.fold_in(own_key, 6), position), (blocks,), jnp.float32, least / len(pieces), top_value / len(pieces))
        return jnp.repeat(jnp.exp(heights), dims[position] // blocks).reshape((-1,) + (1,) * (len(dims) - position - 1))

    level = one(*pieces[0])
    for cut in pieces[1:]:
        level = level * one(*cut)
    return level


def length_profile(count, total, bound, lean):
    portions = [(1 << 20) // math.isqrt(standing ** lean) + 1 for standing in range(2, count + 1)]
    spare, counts = total - bound - (count - 1), [1] * (count - 1)
    while spare > 0:
        free = [i for i in range(count - 1) if counts[i] < bound]
        whole, remaining = sum([portions[i] for i in free]), spare
        for i in free:
            extra = min(bound - counts[i], max(1, remaining * portions[i] // whole), spare)
            counts[i] = counts[i] + extra
            spare = spare - extra
    return np.array([bound] + counts)


def uneven(key, amount, total, limit, skew):
    if amount == 2:
        one = jax.random.randint(key, (), max(1, total - limit), min(limit, total - 1) + 1)
        return jnp.stack([one, total - one])
    sizes = jnp.asarray(length_profile(amount, total, limit, skew), jnp.int32)
    pairs = (amount - 1) // 2
    source_of, receiver = sizes[1:1 + 2 * pairs:2], sizes[2:2 + 2 * pairs:2]
    slack = jnp.minimum(source_of - 1, limit - receiver)
    passed = jax.random.randint(jax.random.fold_in(key, 1), (pairs,), 0, 1 << 20) % (slack + 1)
    sizes = sizes.at[1:1 + 2 * pairs:2].set(source_of - passed).at[2:2 + 2 * pairs:2].set(receiver + passed)
    return sizes[jax.random.permutation(jax.random.fold_in(key, 2), amount)]


def bell_draw(key, extent, width, bound, cuts=(), kind=jnp.bfloat16):
    result = jax.random.normal(key, extent, jnp.float32) * width
    if len(cuts) > 0:
        result = shard_levels(key, extent, cuts, -0.22, 0.18) * result
    return jnp.clip(result, min=-bound, max=bound).astype(kind)


def setup_inputs(seed: int = 0) -> dict:
    seeds = jax.random.split(jax.random.key(seed), 17)
    tokens = bell_draw(seeds[0], (SEQS, SEQ_LEN, D), 1.0, 6.0, ((0, 4), (1, 2)))
    segment_ids = jax.vmap(lambda own: jnp.searchsorted(jnp.cumsum(uneven(own, DOCS, SEQ_LEN, SEQ_LEN // 2, 2)), jnp.arange(SEQ_LEN), side="right"))(jax.random.split(seeds[1], SEQS)).reshape((SEQS, SEQ_LEN)).astype(jnp.int32)
    valid_mask = draw_valid_mask(jax.random.fold_in(seeds[16], 71), 0)
    qkv_weight = bell_draw(seeds[3], (3, D, D), D ** -0.5, 0.21875, ((1, 8), (2, 4)))
    qv_bias = bell_draw(seeds[4], (2, D), 0.03, 0.4375, ((1, 4),), jnp.float32)
    out_weight = bell_draw(seeds[5], (D, D), (max(D // 128, 2)) ** -0.5, 2.5, ((0, 4), (1, 8)))
    out_bias = bell_draw(seeds[6], (D,), 0.1, 1.5, (), jnp.float32)
    norm1_gain = jnp.clip(1.0 + 0.1 * jax.random.normal(seeds[7], (D,), jnp.float32), 0.5, 1.5)
    norm1_shift = bell_draw(seeds[8], (D,), 0.1, 1.5, (), jnp.float32)
    in_weight = bell_draw(seeds[9], (D, FF), D ** -0.5, 0.21875, ((0, 8), (1, 4)))
    in_bias = bell_draw(seeds[10], (FF,), 0.3, 4.0, ((0, 4),), jnp.float32)
    down_weight = bell_draw(seeds[11], (FF, D), FF ** -0.5, 0.109375, ((0, 4), (1, 8)))
    down_bias = bell_draw(seeds[12], (D,), 0.1, 1.5, (), jnp.float32)
    norm2_gain = jnp.clip(1.0 + 0.1 * jax.random.normal(seeds[13], (D,), jnp.float32), 0.5, 1.5)
    norm2_shift = bell_draw(seeds[14], (D,), 0.1, 1.5, (), jnp.float32)
    out_cotangent = bell_draw(seeds[15], (SEQS, SEQ_LEN, D), 1.0, 6.0, ((0, 4), (1, 2)), jnp.float32)
    return dict(tokens=tokens, segment_ids=segment_ids, valid_mask=valid_mask, qkv_weight=qkv_weight, qv_bias=qv_bias, out_weight=out_weight, out_bias=out_bias, norm1_gain=norm1_gain, norm1_shift=norm1_shift, in_weight=in_weight, in_bias=in_bias, down_weight=down_weight, down_bias=down_bias, norm2_gain=norm2_gain, norm2_shift=norm2_shift, out_cotangent=out_cotangent)


@jax.custom_vjp
def low(v):
    return lax.optimization_barrier(v.astype(jnp.bfloat16)).astype(jnp.float32)

@jax.custom_vjp
def low_back(v):
    return v

def low_keep(v):
    return (low(v), None)

def low_pass(kept, grad):
    return (grad,)

def back_keep(v):
    return (v, None)

def back_low(kept, grad):
    return (low(grad),)
low.defvjp(low_keep, low_pass)
low_back.defvjp(back_keep, back_low)
norm_eps = 1e-12
masked_score = -1e+30

def layer_norm(rows, gain, shift):
    mean = lax.optimization_barrier(jnp.mean(rows, axis=-1, keepdims=True))
    centred = rows - mean
    spread = lax.optimization_barrier(jnp.mean(centred * centred, axis=-1, keepdims=True))
    return centred * lax.rsqrt(spread + norm_eps) * gain + shift

def gelu_tanh(value):
    return jax.nn.gelu(value, approximate=True)

def allowed_pairs(query_seg, query_pos, key_seg, key_valid, key_pos):
    same = query_seg[:, None] == key_seg[None, :]
    usable = (key_valid[None, :] == 1) | (query_pos[:, None] == key_pos[None, :])
    return same & usable

def product(left, right):
    return jnp.dot(left, right, precision=lax.Precision.HIGHEST, preferred_element_type=jnp.float32)

def attend(queries, keys, values, seg, valid):
    length = queries.shape[0]
    block = min(512, length)
    count = length // block
    positions = lax.iota(jnp.int32, length)
    key_heads = keys.reshape(length, HEADS, HEAD_DIM)
    value_heads = values.reshape(length, HEADS, HEAD_DIM)

    def one_block(inputs):
        query_block, query_seg, query_pos = inputs
        query_heads = query_block.reshape(block, HEADS, HEAD_DIM)
        raw = jnp.einsum('qhe,khe->hqk', query_heads, key_heads, precision=lax.Precision.HIGHEST, preferred_element_type=jnp.float32)
        scores = low_back(raw * 0.125)
        mask = allowed_pairs(query_seg, query_pos, seg, valid, positions)[None]
        masked = jnp.where(mask, scores, masked_score)
        top = lax.optimization_barrier(jnp.max(masked, axis=2, keepdims=True))
        weights = jnp.where(mask, jnp.exp(masked - top), 0.0)
        probs = low(weights / lax.optimization_barrier(jnp.sum(weights, axis=2, keepdims=True)))
        mixed = jnp.einsum('hqk,khe->qhe', probs, value_heads, precision=lax.Precision.HIGHEST, preferred_element_type=jnp.float32)
        return mixed.reshape(block, HEADS * HEAD_DIM)
    blocks = lax.map(jax.checkpoint(one_block), (queries.reshape(count, block, HEADS * HEAD_DIM), seg.reshape(count, block), positions.reshape(count, block)))
    return blocks.reshape(length, HEADS * HEAD_DIM)

def block_forward(x_rows, seg, valid, qkv_weight, qv_bias, out_weight, out_bias, gain1, shift1, in_weight, in_bias, down_weight, down_bias, gain2, shift2):
    queries = low_back(low(product(x_rows, qkv_weight[0]) + qv_bias[0]))
    keys = low_back(low(product(x_rows, qkv_weight[1])))
    values = low_back(low(product(x_rows, qkv_weight[2]) + qv_bias[1]))
    context = low_back(low(attend(queries, keys, values, seg, valid)))
    attn = low_back(product(context, out_weight) + out_bias)
    hidden = layer_norm(x_rows + attn, gain1, shift1)
    pre = low_back(product(low(hidden), in_weight) + in_bias)
    ffn = low_back(product(low(gelu_tanh(pre)), down_weight) + down_bias)
    out_rows = layer_norm(hidden + ffn, gain2, shift2)
    valid_rows = valid.astype(x_rows.dtype)[:, None]
    stats = jnp.stack([jnp.sum(valid_rows * x_rows * x_rows), jnp.sum(valid_rows * attn * attn), jnp.sum(valid_rows * ffn * ffn), jnp.sum(valid_rows)])
    return (out_rows, stats)

def reference(tokens, segment_ids, valid_mask, qkv_weight, qv_bias, out_weight, out_bias, norm1_gain, norm1_shift, in_weight, in_bias, down_weight, down_bias, norm2_gain, norm2_shift, out_cotangent):
    params = tuple((w.astype(jnp.float32) for w in (qkv_weight, qv_bias, out_weight, out_bias, norm1_gain, norm1_shift, in_weight, in_bias, down_weight, down_bias, norm2_gain, norm2_shift)))
    zero_grads = tuple((jnp.zeros(w.shape, jnp.float32) for w in params))

    def one_sequence(carry, inputs):
        grads, stats = carry
        x_seq, seg, valid, cot = inputs

        def forward(x_rows, *weights):
            return block_forward(x_rows, seg, valid, *weights)
        out_rows, back, seq_stats = jax.vjp(forward, x_seq.astype(jnp.float32), *params, has_aux=True)
        cots = back(cot.astype(jnp.float32))
        grads = tuple((g + c for g, c in zip(grads, cots[1:])))
        return ((grads, stats + seq_stats), (out_rows.astype(jnp.bfloat16), cots[0]))
    (grads, stats), (layer_out, tokens_grad) = lax.scan(one_sequence, (zero_grads, jnp.zeros((4,), jnp.float32)), (tokens, segment_ids, valid_mask, out_cotangent))
    stream_rms = jnp.sqrt(stats[:3] / (stats[3] * D))
    return (layer_out, tokens_grad, grads[0], grads[1], grads[2], grads[3], grads[4], grads[5], grads[6], grads[7], grads[8], grads[9], grads[10], grads[11], stream_rms)
```

```python
import functools

import jax
import jax.numpy as jnp
from jax import lax
from jax.experimental import pallas as pl
from jax.experimental.pallas import tpu as pltpu
from jax.sharding import PartitionSpec as P

HEAD_DIM = 64
LANES = 128
TP = 4
EPS = 1e-12
MASKED = -1e30
F32 = jnp.float32
BF16 = jnp.bfloat16
STOP = 99


def nt(left, right):
    return lax.dot_general(left, right, (((1,), (1,)), ((), ())), preferred_element_type=F32)


def nn(left, right):
    return lax.dot_general(left, right, (((1,), (0,)), ((), ())), preferred_element_type=F32)


def gelu_and_slope(pre):
    scale = 0.7978845608028654
    cube = 0.044715
    square = pre * pre
    tanh = jnp.tanh(scale * pre * (1.0 + cube * square))
    half = 0.5 * (1.0 + tanh)
    slope = half + 0.5 * pre * (1.0 - tanh * tanh) * (scale * (1.0 + 3.0 * cube * square))
    return pre * half, slope


def column_sum(rows):
    return jnp.sum(rows, axis=0, keepdims=True)


def norm_forward(rows):
    mean = jnp.mean(rows, axis=-1, keepdims=True)
    centred = rows - mean
    spread = jnp.mean(centred * centred, axis=-1, keepdims=True)
    inverse = lax.rsqrt(spread + EPS)
    return centred * inverse, inverse


def norm_backward(grad, unit, inverse, gain):
    scaled = grad * gain
    first = jnp.mean(scaled, axis=-1, keepdims=True)
    second = jnp.mean(scaled * unit, axis=-1, keepdims=True)
    return inverse * (scaled - first - unit * second)


class Net:
    def __init__(self, send_sems, recv_sems):
        self.send_sems, self.recv_sems, self.copies = send_sems, recv_sems, []

    def send(self, source, target, where):
        place = len(self.copies)
        copy = pltpu.make_async_remote_copy(
            src_ref=source,
            dst_ref=target,
            send_sem=self.send_sems.at[place],
            recv_sem=self.recv_sems.at[place],
            device_id=where,
            device_id_type=pl.DeviceIdType.MESH,
        )
        copy.start()
        self.copies.append(copy)
        return copy

    def finish(self):
        for copy in self.copies:
            copy.wait_send()


def layer_kernel(dims, *refs):
    shards, ctxs, wctx, piece, width, chunk, heads = dims
    quarter = piece // TP
    cols = heads * HEAD_DIM
    (x_ref, cot_ref, code_ref, wa_ref, wi_ref, wd_ref, vec_ref,
     lo_ref, tg_ref, ga_ref, gi_ref, gd_ref, small_ref,
     wa, wi, wd, xt, ht, dft, dat, code_all, bias, kv, kvt, qm, sbuf, pt, ott, mt, vcol, cot,
     hid, act, slope, dffn, dpre, datt, lobuf, tgbuf,
     r1s, r1r, r2s, r2r, gown, gxs, gxr, gzs, gzr, dkvs, dkvr, dkv0, dqt, dproj, dqp, ctxp, dom0, dom1,
     unit1, hidden, resid2, resid1, sa, sb,
     sa1, sa2, sac, sas, sbc, sbs,
     local_sem, send_sems, recv_sems) = refs
    me_s, me_c, me_t = lax.axis_index("shard"), lax.axis_index("ctx"), lax.axis_index("tp")
    t1 = me_t + 1 - 2 * (me_t % 2)
    t2 = (me_t + 2) % TP
    t3 = (t1 + 2) % TP
    wc = me_c if wctx > 1 else 0
    net = Net(send_sems, recv_sems)

    def shard_at(step):
        return (me_s + step) % shards

    def ctx_at(step):
        return (me_c + step) % ctxs

    barrier = pltpu.get_barrier_semaphore()
    peers = [{"tp": t1}, {"tp": t2}]
    peers += [{"ctx": ctx_at(e)} for e in range(1, ctxs)]
    peers += [{"shard": shard_at(d)} for d in range(1, shards)]
    for peer in peers:
        pl.semaphore_signal(barrier, inc=1, device_id=peer, device_id_type=pl.DeviceIdType.MESH)
    pl.semaphore_wait(barrier, len(peers))

    def gather_start(buf, own):
        along = [net.send(own, buf.at[me_s, wc], {"shard": shard_at(d)}) for d in range(1, shards)]
        across = [net.send(own, buf.at[me_s, wc], {"ctx": ctx_at(e)}) for e in range(1, wctx)]
        buf[me_s, wc] = own[...]
        return along, across

    def gather_forward(buf, state):
        along, across = state
        for d in range(1, shards):
            along[d - 1].wait_recv()
            source = buf.at[shard_at(shards - d), wc]
            across += [net.send(source, source, {"ctx": ctx_at(e)}) for e in range(1, wctx)]

    def gather_wait(state):
        for copy in state[1]:
            copy.wait_recv()

    def whole(buf):
        return buf[...].reshape(width, buf.shape[-1])

    def reduce_start(k, partial):
        r1s[k, 0] = partial(t3)
        first = net.send(r1s.at[k, 0], r1r.at[k, 0], {"tp": t1})
        r1s[k, 1] = partial(t1)
        second = net.send(r1s.at[k, 1], r1r.at[k, 1], {"tp": t1})
        part = partial(t2)
        first.wait_recv()
        r2s[k] = (part + r1r[k, 0]).astype(BF16)
        third = net.send(r2s.at[k], r2r.at[k], {"tp": t2})
        return second, third, partial(me_t)

    def reduce_end(k, state):
        second, third, part = state
        second.wait_recv()
        part = part + r1r[k, 1]
        third.wait_recv()
        return part + r2r[k].astype(F32)

    def spread_start(buf, value):
        buf[me_t] = value
        over = net.send(buf.at[me_t], buf.at[me_t], {"tp": t2})
        near = net.send(buf.at[me_t], buf.at[me_t], {"tp": t1})
        return over, near

    def spread_pass(buf, state):
        state[0].wait_recv()
        return net.send(buf.at[t2], buf.at[t2], {"tp": t1})

    def grad_send(k):
        out = []
        for d in list(range(1, shards)) + [0]:
            s = shard_at(d)
            out.append(net.send(gxs.at[k, s], gxr.at[k, s], {"ctx": ctx_at(1)}))
        return out

    def grad_pass(k, state):
        out = []
        for d in range(1, shards):
            s = shard_at(d)
            total = gown[k, s]
            if wctx > 1:
                state[d - 1].wait_recv()
                total = total + gxr[k, s].astype(F32)
            gzs[k, d - 1] = total.astype(BF16)
            out.append(net.send(gzs.at[k, d - 1], gzr.at[k, d - 1], {"shard": s}))
        return out

    def grad_end(k, state, passed, out_ref):
        total = gown[k, me_s]
        if wctx > 1:
            state[shards - 1].wait_recv()
            total = total + gxr[k, me_s].astype(F32)
        for d in range(1, shards):
            passed[d - 1].wait_recv()
            total = total + gzr[k, d - 1].astype(F32)
        out_ref[...] = total

    def grad_product(k, terms):
        for c in range(wctx - 1, -1, -1):
            where = (me_c + c) % wctx if wctx > 1 else 0
            done = {}
            for left, right, start in terms:
                value = nn(left[where].reshape(shards * chunk, piece), right)
                done[start] = done[start] + value if start in done else value
            for start, value in done.items():
                n = value.shape[1]
                value = value.reshape(shards, chunk, n)
                if c > 0:
                    gxs[k, :, :, start:start + n] = value.astype(BF16)
                else:
                    gown[k, :, :, start:start + n] = value

    def store_transposed(target, value):
        turned = jnp.transpose(value)
        for s in range(shards):
            for c in range(wctx):
                begin = (s * wctx + c) * chunk
                target[c, s] = turned[begin:begin + chunk]

    def exchange(buf, source, axis, at, count, me):
        buf[me] = source
        out = [net.send(buf.at[me], buf.at[me], {axis: at(e)}) for e in range(1, count)]
        return out

    def exchange_end(buf, state, count):
        for copy in state:
            copy.wait_recv()
        total = buf[0]
        for i in range(1, count):
            total = total + buf[i]
        return total

    a_state = gather_start(wa, wa_ref)
    code_all[0] = code_ref[...]
    code_sends = [net.send(code_ref, code_all.at[e], {"ctx": ctx_at(e)}) for e in range(1, ctxs)]
    own_rows = pl.ds(pl.multiple_of(me_t * quarter, quarter), quarter)
    fetch = pltpu.make_async_copy(cot_ref.at[own_rows], cot, local_sem)
    fetch.start()
    store_transposed(xt, x_ref[...])
    for copy in code_sends:
        copy.wait_recv()
    query_code = code_ref[1:2, :]
    for e in range(ctxs):
        key_code = jnp.transpose(jnp.broadcast_to(code_all[e][0:1, :], (LANES, piece)))[:, 0:1]
        allowed = key_code == query_code
        if e == 0:
            rows = lax.broadcasted_iota(jnp.int32, (piece, piece), 0)
            lanes = lax.broadcasted_iota(jnp.int32, (piece, piece), 1)
            allowed = allowed | (rows == lanes)
        bias[e] = jnp.where(allowed, 0.0, MASKED)
    valid_rows = jnp.transpose(jnp.broadcast_to(code_ref[2:3, :], (LANES, piece)))
    vcol[...] = valid_rows
    valid = vcol[own_rows, 0:1]
    gather_forward(wa, a_state)
    gather_wait(a_state)
    if STOP <= 1:
        fetch.wait()
        return net.finish()

    b_state = gather_start(wi, wi_ref)
    c_state = gather_start(wd, wd_ref)
    x = x_ref[...]
    w_all = whole(wa)
    kv[0] = (nn(x, w_all[:, 0:2 * cols]) + vec_ref[8:9, 0:2 * cols]).astype(BF16)
    kv_sends = [net.send(kv.at[0], kv.at[e], {"ctx": ctx_at(e)}) for e in range(1, ctxs)]
    q_pad = nn(x, w_all[:, 2 * cols:2 * cols + 256]) + vec_ref[7:8, 0:256]
    q_low = q_pad.astype(BF16).astype(F32) * 0.125
    lane = lax.broadcasted_iota(jnp.int32, (piece, 256), 1)
    for h in range(heads):
        inside = (lane >= h * HEAD_DIM) & (lane < (h + 1) * HEAD_DIM)
        qm[h] = jnp.where(inside, q_low, 0.0).astype(BF16)
    kvt[0] = jnp.transpose(kv[0])
    if STOP <= 2:
        fetch.wait()
        for c in b_state[0] + c_state[0] + b_state[1] + c_state[1] + kv_sends:
            c.wait_recv()
        return net.finish()

    tops = []
    for h in range(heads):
        s = nt(kv[0][:, 0:256], qm[h]) + bias[0]
        sbuf[h, 0] = s
        tops.append(jnp.max(s, axis=0, keepdims=True))
    gather_forward(wi, b_state)
    for e in range(1, ctxs):
        kv_sends[e - 1].wait_recv()
        kvt[e] = jnp.transpose(kv[e])
    ott[0:cols] = jnp.zeros((cols, piece), F32)
    mt[0:cols] = jnp.zeros((cols, piece), F32)
    for h in range(heads):
        top = tops[h]
        for e in range(1, ctxs):
            s = nt(kv[e][:, 0:256], qm[h]) + bias[e]
            sbuf[h, e] = s
            top = jnp.maximum(top, jnp.max(s, axis=0, keepdims=True))
        rows = slice(cols + h * HEAD_DIM, cols + (h + 1) * HEAD_DIM)
        total = jnp.zeros((1, piece), F32)
        mixed = jnp.zeros((HEAD_DIM, piece), F32)
        for e in range(ctxs):
            weights = jnp.exp(sbuf[h, e] - top)
            total = total + column_sum(weights)
            low = weights.astype(BF16)
            pt[h, e] = low
            mixed = mixed + nn(kvt[e, rows], low)
        inverse = 1.0 / total
        ott[rows] = mixed * inverse
        mt[rows] = jnp.broadcast_to(inverse, (HEAD_DIM, piece))
    ctxp[...] = jnp.transpose(ott[...]).astype(BF16)
    gather_forward(wd, c_state)
    if STOP <= 3:
        fetch.wait()
        gather_wait(b_state)
        gather_wait(c_state)
        return net.finish()

    def quarter_rows(q):
        return pl.ds(pl.multiple_of(q * quarter, quarter), quarter)

    state = reduce_start(0, lambda q: nt(ctxp[quarter_rows(q)], whole(wa)[:, 2 * cols:]))
    out_bias, gain1, shift1, in_bias = vec_ref[0:1], vec_ref[1:2], vec_ref[2:3], vec_ref[3:4]
    down_bias, gain2, shift2 = vec_ref[4:5], vec_ref[5:6], vec_ref[6:7]
    x_own = x_ref[own_rows].astype(F32)
    attn = reduce_end(0, state) + out_bias
    unit, inverse1 = norm_forward(x_own + attn)
    unit1[...] = unit
    own_hidden = unit * gain1 + shift1
    hidden[...] = own_hidden
    spread = spread_start(hid, own_hidden.astype(BF16))
    sa[6:7] = column_sum(valid * x_own * x_own)
    sa[7:8] = column_sum(valid * attn * attn)
    sa[9:10] = jnp.broadcast_to(column_sum(valid), (1, width))
    gather_wait(b_state)
    gather_wait(c_state)

    def expand(q):
        pre = nn(hid[q], whole(wi)) + in_bias
        a, s = gelu_and_slope(pre)
        act[q] = a.astype(BF16)
        slope[q] = s

    expand(me_t)
    spread[1].wait_recv()
    expand(t1)
    third = spread_pass(hid, spread)
    expand(t2)
    third.wait_recv()
    expand(t3)
    if STOP <= 4:
        fetch.wait()
        return net.finish()
    state = reduce_start(1, lambda q: nt(act[q], whole(wd)))
    store_transposed(ht, hid[...].reshape(piece, width))
    fetch.wait()
    ffn = reduce_end(1, state) + down_bias
    unit, inverse2 = norm_forward(hidden[...] + ffn)
    low_out = (unit * gain2 + shift2).astype(BF16)
    grad = cot[...]
    d_resid2 = norm_backward(grad, unit, inverse2, gain2)
    resid2[...] = d_resid2
    low = d_resid2.astype(BF16)
    spread = spread_start(dffn, low)
    spread_out = spread_start(lobuf, low_out)
    sa[8:9] = column_sum(valid * ffn * ffn)
    sa[3:4] = column_sum(low.astype(F32))
    sa[4:5] = column_sum(grad * unit)
    sa[5:6] = column_sum(grad)

    def expand_back(q):
        dpre[q] = (nn(dffn[q], whole(wd)) * slope[q]).astype(BF16)

    expand_back(me_t)
    spread[1].wait_recv()
    expand_back(t1)
    third = spread_pass(dffn, spread)
    expand_back(t2)
    third.wait_recv()
    expand_back(t3)
    third_out = spread_pass(lobuf, spread_out)
    state = reduce_start(2, lambda q: nt(dpre[q], whole(wi)))
    sb[0:1] = column_sum(dpre[...].reshape(piece, width).astype(F32))
    store_transposed(dft, dffn[...].reshape(piece, width))
    grad_product(2, [(dft, act[...].reshape(piece, width), 0)])
    d_state = grad_send(2) if wctx > 1 else None
    d_hidden = resid2[...] + reduce_end(2, state)
    d_resid1 = norm_backward(d_hidden, unit1[...], inverse1, gain1)
    resid1[...] = d_resid1
    low = d_resid1.astype(BF16)
    spread = spread_start(datt, low)
    sa[0:1] = column_sum(low.astype(F32))
    sa[1:2] = column_sum(d_hidden * unit1[...])
    sa[2:3] = column_sum(d_hidden)
    sa[10:16] = jnp.zeros((6, width), F32)
    near = net.send(sa, sa1, {"tp": t1})
    grad_product(1, [(ht, dpre[...].reshape(piece, width), 0)])
    i_state = grad_send(1) if wctx > 1 else None
    spread[1].wait_recv()
    third = spread_pass(datt, spread)
    d_pass = grad_pass(2, d_state)
    third.wait_recv()
    near.wait_recv()
    sa2[0] = sa[...] + sa1[...]
    over = net.send(sa2.at[0], sa2.at[1], {"tp": t2})
    if STOP <= 5:
        i_pass = grad_pass(1, i_state)
        grad_end(2, d_state, d_pass, gd_ref)
        grad_end(1, i_state, i_pass, gi_ref)
        over.wait_recv()
        spread_out[1].wait_recv()
        third_out.wait_recv()
        return net.finish()

    d_att_all = datt[...].reshape(piece, width)
    d_ctx = nn(d_att_all, whole(wa)[:, 2 * cols:]).astype(BF16).astype(F32)
    d_mix = d_ctx * jnp.transpose(mt[...])
    lane = lax.broadcasted_iota(jnp.int32, (piece, LANES), 1)
    dom0[...] = d_mix[:, 0:256].astype(BF16)
    last = d_mix[:, 256:384]
    dom1[0] = jnp.where(lane < HEAD_DIM, last, 0.0).astype(BF16)
    dom1[1] = jnp.where(lane >= HEAD_DIM, last, 0.0).astype(BF16)
    product = jnp.transpose(d_mix)[cols:] * ott[cols:]
    deltas = [column_sum(product[h * HEAD_DIM:(h + 1) * HEAD_DIM]) for h in range(heads)]
    i_pass = grad_pass(1, i_state)
    over.wait_recv()
    sa_c = exchange(sac, sa2[0] + sa2[1], "ctx", ctx_at, ctxs, me_c)
    dqt[...] = jnp.zeros((2 * cols, piece), F32)

    def attention_back(e):
        first = jnp.zeros((piece, 256), F32)
        second = jnp.zeros((piece, LANES), F32)
        for h in range(heads):
            if h == 0:
                d_probs = nt(kv[e][:, 0:256], dom0[...])
            else:
                d_probs = nt(kv[e][:, 256:384], dom1[h - 1])
            d_scores = (pt[h, e].astype(F32) * (d_probs - deltas[h])).astype(BF16)
            first = first + nn(d_scores, qm[h])
            if h == 0:
                first = first + nn(pt[h, e], dom0[...])
            else:
                second = second + nn(pt[h, e], dom1[h - 1])
            rows = slice(h * HEAD_DIM, (h + 1) * HEAD_DIM)
            dqt[rows] = dqt[rows] + nn(kvt[e, rows], d_scores)
        return first, second

    dkv_sends = []
    for e in range(ctxs - 1, 0, -1):
        first, second = attention_back(e)
        dkvs[e - 1, :, 0:256] = first.astype(BF16)
        dkvs[e - 1, :, 256:384] = second.astype(BF16)
        dkv_sends.append(net.send(dkvs.at[e - 1], dkvr.at[e - 1], {"ctx": ctx_at(ctxs - e)}))
    sa_s = exchange(sas, exchange_end(sac, sa_c, ctxs), "shard", shard_at, shards, me_s)
    first, second = attention_back(0)
    dkv0[:, 0:256] = first
    dkv0[:, 256:384] = second
    store_transposed(dat, d_att_all)
    total = dkv0[...]
    for i in range(ctxs - 1):
        dkv_sends[i].wait_recv()
        total = total + dkvr[ctxs - 2 - i].astype(F32)
    dproj[...] = total.astype(BF16)
    dqp[...] = jnp.transpose(dqt[...] * 0.125).astype(BF16)
    grad_product(0, [(xt, dproj[...], 0), (xt, dqp[...], 2 * cols), (dat, ctxp[...], 2 * cols)])
    a_gstate = grad_send(0) if wctx > 1 else None
    sb[1:2] = jnp.zeros((1, width), F32)
    sb[2:3] = jnp.zeros((1, width), F32)
    sb[1:2, 0:2 * cols] = column_sum(dproj[...].astype(F32))
    sb[2:3, 0:2 * cols] = column_sum(dqp[...].astype(F32))
    sb[3:8] = jnp.zeros((5, width), F32)
    sb_c = exchange(sbc, sb[...], "ctx", ctx_at, ctxs, me_c)

    def back_tokens(q):
        rows = quarter_rows(q)
        w = whole(wa)
        return nt(dproj[rows], w[:, 0:2 * cols]) + nt(dqp[rows, 0:256], w[:, 2 * cols:2 * cols + 256])

    state = reduce_start(3, back_tokens)
    sb_s = exchange(sbs, exchange_end(sbc, sb_c, ctxs), "shard", shard_at, shards, me_s)
    a_pass = grad_pass(0, a_gstate)
    spread = spread_start(tgbuf, (resid1[...] + reduce_end(3, state)).astype(BF16))
    grad_end(2, d_state, d_pass, gd_ref)
    grad_end(1, i_state, i_pass, gi_ref)
    spread_out[1].wait_recv()
    third_out.wait_recv()
    lo_ref[...] = lobuf[...]
    small_ref[0:16] = exchange_end(sas, sa_s, shards)
    third = spread_pass(tgbuf, spread)
    small_ref[16:24] = exchange_end(sbs, sb_s, shards)
    grad_end(0, a_gstate, a_pass, ga_ref)
    spread[1].wait_recv()
    third.wait_recv()
    tg_ref[...] = tgbuf[...]
    net.finish()


def run_layer(dims, copies, x, cot, code, wa, wi, wd, vec):
    shards, ctxs, wctx, piece, width, chunk, heads = dims
    quarter = piece // TP
    cols = heads * HEAD_DIM
    hidden_cols = wi.shape[1]
    vmem = pl.BlockSpec(memory_space=pltpu.VMEM)
    weights = (shards, wctx, chunk, width)
    turned = (wctx, shards, chunk, piece)
    V = pltpu.VMEM
    scratch = [
        V(weights, BF16), V(weights, BF16), V(weights, BF16),
        V(turned, BF16), V(turned, BF16), V(turned, BF16), V(turned, BF16),
        V((ctxs, 8, piece), F32), V((ctxs, piece, piece), F32),
        V((ctxs, piece, 2 * cols), BF16), V((ctxs, 2 * cols, piece), BF16), V((heads, piece, 256), BF16),
        V((heads, ctxs, piece, piece), F32), V((heads, ctxs, piece, piece), BF16),
        V((2 * cols, piece), F32), V((2 * cols, piece), F32), V((piece, LANES), F32), V((quarter, width), F32),
        V((TP, quarter, width), BF16), V((TP, quarter, hidden_cols), BF16), V((TP, quarter, hidden_cols), F32),
        V((TP, quarter, width), BF16), V((TP, quarter, hidden_cols), BF16), V((TP, quarter, width), BF16),
        V((TP, quarter, width), BF16), V((TP, quarter, width), BF16),
        V((4, 2, quarter, width), F32), V((4, 2, quarter, width), F32),
        V((4, quarter, width), BF16), V((4, quarter, width), BF16),
        V((3, shards, chunk, width), F32), V((3, shards, chunk, width), BF16), V((3, shards, chunk, width), BF16),
        V((3, max(shards - 1, 1), chunk, width), BF16), V((3, max(shards - 1, 1), chunk, width), BF16),
        V((ctxs - 1, piece, 2 * cols), BF16), V((ctxs - 1, piece, 2 * cols), BF16), V((piece, 2 * cols), F32),
        V((2 * cols, piece), F32), V((piece, 2 * cols), BF16), V((piece, 2 * cols), BF16), V((piece, 2 * cols), BF16),
        V((piece, 256), BF16), V((2, piece, LANES), BF16),
        V((quarter, width), F32), V((quarter, width), F32), V((quarter, width), F32), V((quarter, width), F32),
        V((16, width), F32), V((8, width), F32),
        V((16, width), F32), V((2, 16, width), F32), V((ctxs, 16, width), F32), V((shards, 16, width), F32),
        V((ctxs, 8, width), F32), V((shards, 8, width), F32),
        pltpu.SemaphoreType.DMA, pltpu.SemaphoreType.DMA((copies,)), pltpu.SemaphoreType.DMA((copies,)),
    ]
    return pl.pallas_call(
        functools.partial(layer_kernel, dims),
        out_shape=(
            jax.ShapeDtypeStruct((TP, quarter, width), BF16),
            jax.ShapeDtypeStruct((TP, quarter, width), BF16),
            jax.ShapeDtypeStruct((chunk, width), F32),
            jax.ShapeDtypeStruct((chunk, hidden_cols), F32),
            jax.ShapeDtypeStruct((chunk, hidden_cols), F32),
            jax.ShapeDtypeStruct((24, width), F32),
        ),
        in_specs=[vmem, pl.BlockSpec(memory_space=pl.ANY), vmem, vmem, vmem, vmem, vmem],
        out_specs=(vmem,) * 6,
        scratch_shapes=scratch,
        compiler_params=pltpu.CompilerParams(
            collective_id=0, has_side_effects=True, vmem_limit_bytes=67_043_328
        ),
        name="layer",
    )(x, cot, code, wa, wi, wd, vec)


def body(
    sizes,
    tokens, segment_ids, valid_mask, qkv_weight, qv_bias, out_weight, out_bias, norm1_gain, norm1_shift,
    in_weight, in_bias, down_weight, down_bias, norm2_gain, norm2_shift, out_cotangent,
):
    shards, ctxs = sizes
    _, piece, width = tokens.shape
    cols = qkv_weight.shape[2]
    heads = cols // HEAD_DIM
    own = jnp.concatenate([qkv_weight[1], qkv_weight[2], qkv_weight[0], out_weight.T], axis=1)
    parts = [own, in_weight, down_weight.T]
    wctx = ctxs
    if parts[0].shape[0] % 16 or ctxs > 2:
        wctx = 1
        parts = [lax.all_gather(part, "ctx", axis=0, tiled=True) for part in parts]
    chunk = parts[0].shape[0]
    dims = (shards, ctxs, wctx, piece, width, chunk, heads)
    seg = segment_ids.reshape(piece).astype(F32)
    valid = valid_mask.reshape(piece)
    zero = jnp.zeros((piece,), F32)
    code = jnp.stack([jnp.where(valid == 1, seg, -1.0), seg, valid.astype(F32), zero, zero, zero, zero, zero])
    q_bias = jnp.pad(qv_bias[0], (0, width - cols))
    kv_bias = jnp.pad(qv_bias[1], (cols, width - 2 * cols))
    none = jnp.zeros((width,), F32)
    vec = jnp.stack([out_bias, norm1_gain, norm1_shift, in_bias, down_bias, norm2_gain, norm2_shift,
                     q_bias, kv_bias] + [none] * 7)
    lo, tg, ga, gi, gd, small = run_layer(
        dims, 160, tokens.reshape(piece, width), out_cotangent.reshape(piece, width), code, *parts, vec
    )
    if wctx < ctxs:
        ga, gi, gd = (
            lax.psum_scatter(g, "ctx", scatter_dimension=0, tiled=True) for g in (ga, gi, gd)
        )
    g_qkv = jnp.stack([ga[:, 2 * cols:3 * cols], ga[:, 0:cols], ga[:, cols:2 * cols]])
    sums = jnp.sum(small[6:9], axis=1)
    stream_rms = jnp.sqrt(sums / (small[9, 0] * width))
    return (
        lo.reshape(1, piece, width),
        tg.reshape(1, piece, width).astype(F32),
        g_qkv,
        jnp.stack([small[18, 0:cols], small[17, cols:2 * cols]]),
        ga[:, 3 * cols:].T,
        small[0], small[1], small[2],
        gi,
        small[16],
        gd.T,
        small[3], small[4], small[5],
        stream_rms,
    )


def solution(mesh):
    sizes = (mesh.shape["shard"], mesh.shape["ctx"])
    return jax.shard_map(
        functools.partial(body, sizes),
        mesh=mesh,
        in_specs=(
            P("shard", "ctx", None), P("shard", "ctx"), P("shard", "ctx"),
            P(None, ("shard", "ctx"), "tp"), P(None, "tp"), P("tp", ("shard", "ctx")),
            P(), P(), P(),
            P(("shard", "ctx"), "tp"), P("tp"), P("tp", ("shard", "ctx")),
            P(), P(), P(),
            P("shard", "ctx", None),
        ),
        out_specs=(
            P("shard", "ctx", None), P("shard", "ctx", None),
            P(None, ("shard", "ctx"), "tp"), P(None, "tp"), P("tp", ("shard", "ctx")),
            P(), P(), P(),
            P(("shard", "ctx"), "tp"), P("tp"), P("tp", ("shard", "ctx")),
            P(), P(), P(), P(),
        ),
        check_vma=False,
    )
```

```python
import functools

import jax
import jax.numpy as jnp
from jax import lax
from jax.experimental import pallas as pl
from jax.experimental.pallas import tpu as pltpu
from jax.sharding import PartitionSpec as P

HEAD_DIM = 64
LANES = 128
TP = 4
EPS = 1e-12
MASKED = -1e30
F32 = jnp.float32
BF16 = jnp.bfloat16
STOP = 99


def nt(left, right):
    return lax.dot_general(left, right, (((1,), (1,)), ((), ())), preferred_element_type=F32)


def nn(left, right):
    return lax.dot_general(left, right, (((1,), (0,)), ((), ())), preferred_element_type=F32)


def gelu_and_slope(pre):
    scale = 0.7978845608028654
    cube = 0.044715
    square = pre * pre
    tanh = jnp.tanh(scale * pre * (1.0 + cube * square))
    half = 0.5 * (1.0 + tanh)
    slope = half + 0.5 * pre * (1.0 - tanh * tanh) * (scale * (1.0 + 3.0 * cube * square))
    return pre * half, slope


def column_sum(rows):
    return jnp.sum(rows, axis=0, keepdims=True)


def norm_forward(rows):
    mean = jnp.mean(rows, axis=-1, keepdims=True)
    centred = rows - mean
    spread = jnp.mean(centred * centred, axis=-1, keepdims=True)
    inverse = lax.rsqrt(spread + EPS)
    return centred * inverse, inverse


def norm_backward(grad, unit, inverse, gain):
    scaled = grad * gain
    first = jnp.mean(scaled, axis=-1, keepdims=True)
    second = jnp.mean(scaled * unit, axis=-1, keepdims=True)
    return inverse * (scaled - first - unit * second)


class Net:
    def __init__(self, send_sems, recv_sems):
        self.send_sems, self.recv_sems, self.copies = send_sems, recv_sems, []

    def send(self, source, target, where):
        place = len(self.copies)
        copy = pltpu.make_async_remote_copy(
            src_ref=source,
            dst_ref=target,
            send_sem=self.send_sems.at[place],
            recv_sem=self.recv_sems.at[place],
            device_id=where,
            device_id_type=pl.DeviceIdType.MESH,
        )
        copy.start()
        self.copies.append(copy)
        return copy

    def finish(self):
        for copy in self.copies:
            copy.wait_send()


def layer_kernel(dims, *refs):
    shards, ctxs, wctx, piece, width, chunk, heads = dims
    quarter = piece // TP
    cols = heads * HEAD_DIM
    (x_ref, cot_ref, seg_ref, valid_ref, qkv_ref, out_ref, wi_ref, wd_ref, qv_bias_ref, out_bias_ref, gain1_ref,
     shift1_ref, in_bias_ref, down_bias_ref, gain2_ref, shift2_ref,
     lo_ref, tg_ref, ga_ref, gi_ref, gd_ref, small_ref,
     wa, wi, wd, xt, ht, dft, dat, code_all, bias, kv, kvt, qm, sbuf, pt, ott, mt, vcol, cot,
     hid, act, slope, dffn, dpre, datt, lobuf, tgbuf,
     r1s, r1r, r2s, r2r, gown, gxs, gxr, gzs, gzr, dkvs, dkvr, dkv0, dqt, dproj, dqp, ctxp, dom0, dom1,
     unit1, hidden, resid2, resid1, sa, sb,
     sa1, sa2, sac, sas, sbc, sbs,
     wa_ref, code_ref, vec_ref,
     local_sem, send_sems, recv_sems) = refs
    me_s, me_c, me_t = lax.axis_index("shard"), lax.axis_index("ctx"), lax.axis_index("tp")
    t1 = me_t + 1 - 2 * (me_t % 2)
    t2 = (me_t + 2) % TP
    t3 = (t1 + 2) % TP
    wc = me_c if wctx > 1 else 0
    net = Net(send_sems, recv_sems)

    def shard_at(step):
        return (me_s + step) % shards

    def ctx_at(step):
        return (me_c + step) % ctxs

    barrier = pltpu.get_barrier_semaphore()
    peers = [{"tp": t1}, {"tp": t2}]
    peers += [{"ctx": ctx_at(e)} for e in range(1, ctxs)]
    peers += [{"shard": shard_at(d)} for d in range(1, shards)]
    for peer in peers:
        pl.semaphore_signal(barrier, inc=1, device_id=peer, device_id_type=pl.DeviceIdType.MESH)
    pl.semaphore_wait(barrier, len(peers))

    def gather_start(buf, own):
        along = [net.send(own, buf.at[me_s, wc], {"shard": shard_at(d)}) for d in range(1, shards)]
        across = [net.send(own, buf.at[me_s, wc], {"ctx": ctx_at(e)}) for e in range(1, wctx)]
        buf[me_s, wc] = own[...]
        return along, across

    def gather_forward(buf, state):
        along, across = state
        for d in range(1, shards):
            along[d - 1].wait_recv()
            source = buf.at[shard_at(shards - d), wc]
            across += [net.send(source, source, {"ctx": ctx_at(e)}) for e in range(1, wctx)]

    def gather_wait(state):
        for copy in state[1]:
            copy.wait_recv()

    def whole(buf):
        return buf[...].reshape(width, buf.shape[-1])

    def reduce_start(k, partial):
        r1s[k, 0] = partial(t3)
        first = net.send(r1s.at[k, 0], r1r.at[k, 0], {"tp": t1})
        r1s[k, 1] = partial(t1)
        second = net.send(r1s.at[k, 1], r1r.at[k, 1], {"tp": t1})
        part = partial(t2)
        first.wait_recv()
        r2s[k] = (part + r1r[k, 0]).astype(BF16)
        third = net.send(r2s.at[k], r2r.at[k], {"tp": t2})
        return second, third, partial(me_t)

    def reduce_end(k, state):
        second, third, part = state
        second.wait_recv()
        part = part + r1r[k, 1]
        third.wait_recv()
        return part + r2r[k].astype(F32)

    def spread_start(buf, value):
        buf[me_t] = value
        over = net.send(buf.at[me_t], buf.at[me_t], {"tp": t2})
        near = net.send(buf.at[me_t], buf.at[me_t], {"tp": t1})
        return over, near

    def spread_pass(buf, state):
        state[0].wait_recv()
        return net.send(buf.at[t2], buf.at[t2], {"tp": t1})

    def grad_send(k):
        out = []
        for d in list(range(1, shards)) + [0]:
            s = shard_at(d)
            out.append(net.send(gxs.at[k, s], gxr.at[k, s], {"ctx": ctx_at(1)}))
        return out

    def grad_pass(k, state):
        out = []
        for d in range(1, shards):
            s = shard_at(d)
            total = gown[k, s]
            if wctx > 1:
                state[d - 1].wait_recv()
                total = total + gxr[k, s].astype(F32)
            gzs[k, d - 1] = total.astype(BF16)
            out.append(net.send(gzs.at[k, d - 1], gzr.at[k, d - 1], {"shard": s}))
        return out

    def grad_end(k, state, passed, out_ref):
        total = gown[k, me_s]
        if wctx > 1:
            state[shards - 1].wait_recv()
            total = total + gxr[k, me_s].astype(F32)
        for d in range(1, shards):
            passed[d - 1].wait_recv()
            total = total + gzr[k, d - 1].astype(F32)
        out_ref[...] = total

    def grad_product(k, terms):
        for c in range(wctx - 1, -1, -1):
            where = (me_c + c) % wctx if wctx > 1 else 0
            done = {}
            for left, right, start in terms:
                value = nn(left[where].reshape(shards * chunk, piece), right)
                done[start] = done[start] + value if start in done else value
            for start, value in done.items():
                n = value.shape[1]
                value = value.reshape(shards, chunk, n)
                if c > 0:
                    gxs[k, :, :, start:start + n] = value.astype(BF16)
                else:
                    gown[k, :, :, start:start + n] = value

    def store_transposed(target, value):
        turned = jnp.transpose(value)
        for s in range(shards):
            for c in range(wctx):
                begin = (s * wctx + c) * chunk
                target[c, s] = turned[begin:begin + chunk]

    def exchange(buf, source, axis, at, count, me):
        buf[me] = source
        out = [net.send(buf.at[me], buf.at[me], {axis: at(e)}) for e in range(1, count)]
        return out

    def exchange_end(buf, state, count):
        for copy in state:
            copy.wait_recv()
        total = buf[0]
        for i in range(1, count):
            total = total + buf[i]
        return total

    if wctx < ctxs:
        wa_ref[...] = qkv_ref[...]
    else:
        wa_ref[:, 0:cols] = qkv_ref[1]
        wa_ref[:, cols:2 * cols] = qkv_ref[2]
        wa_ref[:, 2 * cols:3 * cols] = qkv_ref[0]
        wa_ref[:, 3 * cols:] = jnp.transpose(out_ref[...].astype(F32)).astype(BF16)
    a_state = gather_start(wa, wa_ref)
    seg = seg_ref[...].astype(F32)
    real = valid_ref[...] == 1
    code_ref[...] = jnp.zeros_like(code_ref)
    code_ref[0:1] = jnp.where(real, seg, -1.0)
    code_ref[1:2] = seg
    code_ref[2:3] = jnp.where(real, 1.0, 0.0)
    code_all[0] = code_ref[...]
    code_sends = [net.send(code_ref, code_all.at[e], {"ctx": ctx_at(e)}) for e in range(1, ctxs)]
    own_rows = pl.ds(pl.multiple_of(me_t * quarter, quarter), quarter)
    fetch = pltpu.make_async_copy(cot_ref.at[own_rows], cot, local_sem)
    fetch.start()
    store_transposed(xt, x_ref[...])
    vec_ref[...] = jnp.zeros_like(vec_ref)
    vec_ref[0:1, 0:cols] = qv_bias_ref[0:1]
    vec_ref[1:2, cols:2 * cols] = qv_bias_ref[1:2]
    for copy in code_sends:
        copy.wait_recv()
    query_code = code_ref[1:2, :]
    for e in range(ctxs):
        key_code = jnp.transpose(jnp.broadcast_to(code_all[e][0:1, :], (LANES, piece)))[:, 0:1]
        allowed = key_code == query_code
        if e == 0:
            rows = lax.broadcasted_iota(jnp.int32, (piece, piece), 0)
            lanes = lax.broadcasted_iota(jnp.int32, (piece, piece), 1)
            allowed = allowed | (rows == lanes)
        bias[e] = jnp.where(allowed, 0.0, MASKED)
    valid_rows = jnp.transpose(jnp.broadcast_to(code_ref[2:3, :], (LANES, piece)))
    vcol[...] = valid_rows
    valid = vcol[own_rows, 0:1]
    gather_forward(wa, a_state)
    gather_wait(a_state)
    if STOP <= 1:
        fetch.wait()
        return net.finish()

    b_state = gather_start(wi, wi_ref)
    c_state = gather_start(wd, wd_ref)
    x = x_ref[...]
    w_all = whole(wa)
    kv[0] = (nn(x, w_all[:, 0:2 * cols]) + vec_ref[1:2, 0:2 * cols]).astype(BF16)
    kv_sends = [net.send(kv.at[0], kv.at[e], {"ctx": ctx_at(e)}) for e in range(1, ctxs)]
    q_pad = nn(x, w_all[:, 2 * cols:2 * cols + 256]) + vec_ref[0:1, 0:256]
    q_low = q_pad.astype(BF16).astype(F32) * 0.125
    lane = lax.broadcasted_iota(jnp.int32, (piece, 256), 1)
    for h in range(heads):
        inside = (lane >= h * HEAD_DIM) & (lane < (h + 1) * HEAD_DIM)
        qm[h] = jnp.where(inside, q_low, 0.0).astype(BF16)
    kvt[0] = jnp.transpose(kv[0])
    if STOP <= 2:
        fetch.wait()
        for c in b_state[0] + c_state[0] + b_state[1] + c_state[1] + kv_sends:
            c.wait_recv()
        return net.finish()

    tops = []
    for h in range(heads):
        s = nt(kv[0][:, 0:256], qm[h]) + bias[0]
        sbuf[h, 0] = s
        tops.append(jnp.max(s, axis=0, keepdims=True))
    gather_forward(wi, b_state)
    for e in range(1, ctxs):
        kv_sends[e - 1].wait_recv()
        kvt[e] = jnp.transpose(kv[e])
    ott[0:cols] = jnp.zeros((cols, piece), F32)
    mt[0:cols] = jnp.zeros((cols, piece), F32)
    for h in range(heads):
        top = tops[h]
        for e in range(1, ctxs):
            s = nt(kv[e][:, 0:256], qm[h]) + bias[e]
            sbuf[h, e] = s
            top = jnp.maximum(top, jnp.max(s, axis=0, keepdims=True))
        rows = slice(cols + h * HEAD_DIM, cols + (h + 1) * HEAD_DIM)
        total = jnp.zeros((1, piece), F32)
        mixed = jnp.zeros((HEAD_DIM, piece), F32)
        for e in range(ctxs):
            weights = jnp.exp(sbuf[h, e] - top)
            total = total + column_sum(weights)
            low = weights.astype(BF16)
            pt[h, e] = low
            mixed = mixed + nn(kvt[e, rows], low)
        inverse = 1.0 / total
        ott[rows] = mixed * inverse
        mt[rows] = jnp.broadcast_to(inverse, (HEAD_DIM, piece))
    ctxp[...] = jnp.transpose(ott[...]).astype(BF16)
    gather_forward(wd, c_state)
    if STOP <= 3:
        fetch.wait()
        gather_wait(b_state)
        gather_wait(c_state)
        return net.finish()

    def quarter_rows(q):
        return pl.ds(pl.multiple_of(q * quarter, quarter), quarter)

    state = reduce_start(0, lambda q: nt(ctxp[quarter_rows(q)], whole(wa)[:, 2 * cols:]))
    out_bias, gain1, shift1, in_bias = (
        ref[...].reshape(1, -1) for ref in (out_bias_ref, gain1_ref, shift1_ref, in_bias_ref)
    )
    down_bias, gain2, shift2 = (ref[...].reshape(1, -1) for ref in (down_bias_ref, gain2_ref, shift2_ref))
    x_own = x_ref[own_rows].astype(F32)
    attn = reduce_end(0, state) + out_bias
    unit, inverse1 = norm_forward(x_own + attn)
    unit1[...] = unit
    own_hidden = unit * gain1 + shift1
    hidden[...] = own_hidden
    spread = spread_start(hid, own_hidden.astype(BF16))
    sa[6:7] = column_sum(valid * x_own * x_own)
    sa[7:8] = column_sum(valid * attn * attn)
    sa[9:10] = jnp.broadcast_to(column_sum(valid), (1, width))
    gather_wait(b_state)
    gather_wait(c_state)

    def expand(q):
        pre = nn(hid[q], whole(wi)) + in_bias
        a, s = gelu_and_slope(pre)
        act[q] = a.astype(BF16)
        slope[q] = s

    expand(me_t)
    spread[1].wait_recv()
    expand(t1)
    third = spread_pass(hid, spread)
    expand(t2)
    third.wait_recv()
    expand(t3)
    if STOP <= 4:
        fetch.wait()
        return net.finish()
    state = reduce_start(1, lambda q: nt(act[q], whole(wd)))
    store_transposed(ht, hid[...].reshape(piece, width))
    fetch.wait()
    ffn = reduce_end(1, state) + down_bias
    unit, inverse2 = norm_forward(hidden[...] + ffn)
    low_out = (unit * gain2 + shift2).astype(BF16)
    grad = cot[...]
    d_resid2 = norm_backward(grad, unit, inverse2, gain2)
    resid2[...] = d_resid2
    low = d_resid2.astype(BF16)
    spread = spread_start(dffn, low)
    spread_out = spread_start(lobuf, low_out)
    sa[8:9] = column_sum(valid * ffn * ffn)
    sa[3:4] = column_sum(low.astype(F32))
    sa[4:5] = column_sum(grad * unit)
    sa[5:6] = column_sum(grad)

    def expand_back(q):
        dpre[q] = (nn(dffn[q], whole(wd)) * slope[q]).astype(BF16)

    expand_back(me_t)
    spread[1].wait_recv()
    expand_back(t1)
    third = spread_pass(dffn, spread)
    expand_back(t2)
    third.wait_recv()
    expand_back(t3)
    third_out = spread_pass(lobuf, spread_out)
    state = reduce_start(2, lambda q: nt(dpre[q], whole(wi)))
    sb[0:1] = column_sum(dpre[...].reshape(piece, width).astype(F32))
    store_transposed(dft, dffn[...].reshape(piece, width))
    grad_product(2, [(dft, act[...].reshape(piece, width), 0)])
    d_state = grad_send(2) if wctx > 1 else None
    d_hidden = resid2[...] + reduce_end(2, state)
    d_resid1 = norm_backward(d_hidden, unit1[...], inverse1, gain1)
    resid1[...] = d_resid1
    low = d_resid1.astype(BF16)
    spread = spread_start(datt, low)
    sa[0:1] = column_sum(low.astype(F32))
    sa[1:2] = column_sum(d_hidden * unit1[...])
    sa[2:3] = column_sum(d_hidden)
    sa[10:16] = jnp.zeros((6, width), F32)
    near = net.send(sa, sa1, {"tp": t1})
    grad_product(1, [(ht, dpre[...].reshape(piece, width), 0)])
    i_state = grad_send(1) if wctx > 1 else None
    spread[1].wait_recv()
    third = spread_pass(datt, spread)
    d_pass = grad_pass(2, d_state)
    third.wait_recv()
    near.wait_recv()
    sa2[0] = sa[...] + sa1[...]
    over = net.send(sa2.at[0], sa2.at[1], {"tp": t2})
    if STOP <= 5:
        i_pass = grad_pass(1, i_state)
        grad_end(2, d_state, d_pass, gd_ref)
        grad_end(1, i_state, i_pass, gi_ref)
        over.wait_recv()
        spread_out[1].wait_recv()
        third_out.wait_recv()
        return net.finish()

    d_att_all = datt[...].reshape(piece, width)
    d_ctx = nn(d_att_all, whole(wa)[:, 2 * cols:]).astype(BF16).astype(F32)
    d_mix = d_ctx * jnp.transpose(mt[...])
    lane = lax.broadcasted_iota(jnp.int32, (piece, LANES), 1)
    dom0[...] = d_mix[:, 0:256].astype(BF16)
    last = d_mix[:, 256:384]
    dom1[0] = jnp.where(lane < HEAD_DIM, last, 0.0).astype(BF16)
    dom1[1] = jnp.where(lane >= HEAD_DIM, last, 0.0).astype(BF16)
    product = jnp.transpose(d_mix)[cols:] * ott[cols:]
    deltas = [column_sum(product[h * HEAD_DIM:(h + 1) * HEAD_DIM]) for h in range(heads)]
    i_pass = grad_pass(1, i_state)
    over.wait_recv()
    sa_c = exchange(sac, sa2[0] + sa2[1], "ctx", ctx_at, ctxs, me_c)
    dqt[...] = jnp.zeros((2 * cols, piece), F32)

    def attention_back(e):
        first = jnp.zeros((piece, 256), F32)
        second = jnp.zeros((piece, LANES), F32)
        for h in range(heads):
            if h == 0:
                d_probs = nt(kv[e][:, 0:256], dom0[...])
            else:
                d_probs = nt(kv[e][:, 256:384], dom1[h - 1])
            d_scores = (pt[h, e].astype(F32) * (d_probs - deltas[h])).astype(BF16)
            first = first + nn(d_scores, qm[h])
            if h == 0:
                first = first + nn(pt[h, e], dom0[...])
            else:
                second = second + nn(pt[h, e], dom1[h - 1])
            rows = slice(h * HEAD_DIM, (h + 1) * HEAD_DIM)
            dqt[rows] = dqt[rows] + nn(kvt[e, rows], d_scores)
        return first, second

    dkv_sends = []
    for e in range(ctxs - 1, 0, -1):
        first, second = attention_back(e)
        dkvs[e - 1, :, 0:256] = first.astype(BF16)
        dkvs[e - 1, :, 256:384] = second.astype(BF16)
        dkv_sends.append(net.send(dkvs.at[e - 1], dkvr.at[e - 1], {"ctx": ctx_at(ctxs - e)}))
    sa_s = exchange(sas, exchange_end(sac, sa_c, ctxs), "shard", shard_at, shards, me_s)
    first, second = attention_back(0)
    dkv0[:, 0:256] = first
    dkv0[:, 256:384] = second
    store_transposed(dat, d_att_all)
    total = dkv0[...]
    for i in range(ctxs - 1):
        dkv_sends[i].wait_recv()
        total = total + dkvr[ctxs - 2 - i].astype(F32)
    dproj[...] = total.astype(BF16)
    dqp[...] = jnp.transpose(dqt[...] * 0.125).astype(BF16)
    grad_product(0, [(xt, dproj[...], 0), (xt, dqp[...], 2 * cols), (dat, ctxp[...], 2 * cols)])
    a_gstate = grad_send(0) if wctx > 1 else None
    sb[1:2] = jnp.zeros((1, width), F32)
    sb[2:3] = jnp.zeros((1, width), F32)
    sb[1:2, 0:2 * cols] = column_sum(dproj[...].astype(F32))
    sb[2:3, 0:2 * cols] = column_sum(dqp[...].astype(F32))
    sb[3:8] = jnp.zeros((5, width), F32)
    sb_c = exchange(sbc, sb[...], "ctx", ctx_at, ctxs, me_c)

    def back_tokens(q):
        rows = quarter_rows(q)
        w = whole(wa)
        return nt(dproj[rows], w[:, 0:2 * cols]) + nt(dqp[rows, 0:256], w[:, 2 * cols:2 * cols + 256])

    state = reduce_start(3, back_tokens)
    sb_s = exchange(sbs, exchange_end(sbc, sb_c, ctxs), "shard", shard_at, shards, me_s)
    a_pass = grad_pass(0, a_gstate)
    spread = spread_start(tgbuf, (resid1[...] + reduce_end(3, state)).astype(BF16))
    grad_end(2, d_state, d_pass, gd_ref)
    grad_end(1, i_state, i_pass, gi_ref)
    spread_out[1].wait_recv()
    third_out.wait_recv()
    lo_ref[...] = lobuf[...]
    small_ref[0:16] = exchange_end(sas, sa_s, shards)
    third = spread_pass(tgbuf, spread)
    small_ref[16:24] = exchange_end(sbs, sb_s, shards)
    grad_end(0, a_gstate, a_pass, ga_ref)
    spread[1].wait_recv()
    third.wait_recv()
    tg_ref[...] = tgbuf[...]
    net.finish()


def run_layer(dims, copies, *operands):
    shards, ctxs, wctx, piece, width, chunk, heads = dims
    quarter = piece // TP
    cols = heads * HEAD_DIM
    hidden_cols = operands[6].shape[1]
    vmem = pl.BlockSpec(memory_space=pltpu.VMEM)
    weights = (shards, wctx, chunk, width)
    turned = (wctx, shards, chunk, piece)
    V = pltpu.VMEM
    scratch = [
        V(weights, BF16), V(weights, BF16), V(weights, BF16),
        V(turned, BF16), V(turned, BF16), V(turned, BF16), V(turned, BF16),
        V((ctxs, 8, piece), F32), V((ctxs, piece, piece), F32),
        V((ctxs, piece, 2 * cols), BF16), V((ctxs, 2 * cols, piece), BF16), V((heads, piece, 256), BF16),
        V((heads, ctxs, piece, piece), F32), V((heads, ctxs, piece, piece), BF16),
        V((2 * cols, piece), F32), V((2 * cols, piece), F32), V((piece, LANES), F32), V((quarter, width), F32),
        V((TP, quarter, width), BF16), V((TP, quarter, hidden_cols), BF16), V((TP, quarter, hidden_cols), F32),
        V((TP, quarter, width), BF16), V((TP, quarter, hidden_cols), BF16), V((TP, quarter, width), BF16),
        V((TP, quarter, width), BF16), V((TP, quarter, width), BF16),
        V((4, 2, quarter, width), F32), V((4, 2, quarter, width), F32),
        V((4, quarter, width), BF16), V((4, quarter, width), BF16),
        V((3, shards, chunk, width), F32), V((3, shards, chunk, width), BF16), V((3, shards, chunk, width), BF16),
        V((3, max(shards - 1, 1), chunk, width), BF16), V((3, max(shards - 1, 1), chunk, width), BF16),
        V((ctxs - 1, piece, 2 * cols), BF16), V((ctxs - 1, piece, 2 * cols), BF16), V((piece, 2 * cols), F32),
        V((2 * cols, piece), F32), V((piece, 2 * cols), BF16), V((piece, 2 * cols), BF16), V((piece, 2 * cols), BF16),
        V((piece, 256), BF16), V((2, piece, LANES), BF16),
        V((quarter, width), F32), V((quarter, width), F32), V((quarter, width), F32), V((quarter, width), F32),
        V((16, width), F32), V((8, width), F32),
        V((16, width), F32), V((2, 16, width), F32), V((ctxs, 16, width), F32), V((shards, 16, width), F32),
        V((ctxs, 8, width), F32), V((shards, 8, width), F32),
        V((chunk, width), BF16), V((8, piece), F32), V((8, 2 * cols), F32),
        pltpu.SemaphoreType.DMA, pltpu.SemaphoreType.DMA((copies,)), pltpu.SemaphoreType.DMA((copies,)),
    ]
    return pl.pallas_call(
        functools.partial(layer_kernel, dims),
        out_shape=(
            jax.ShapeDtypeStruct((TP, quarter, width), BF16),
            jax.ShapeDtypeStruct((TP, quarter, width), BF16),
            jax.ShapeDtypeStruct((chunk, width), F32),
            jax.ShapeDtypeStruct((chunk, hidden_cols), F32),
            jax.ShapeDtypeStruct((chunk, hidden_cols), F32),
            jax.ShapeDtypeStruct((24, width), F32),
        ),
        in_specs=[vmem, pl.BlockSpec(memory_space=pl.ANY)] + [vmem] * (len(operands) - 2),
        out_specs=(vmem,) * 6,
        scratch_shapes=scratch,
        compiler_params=pltpu.CompilerParams(
            collective_id=0, has_side_effects=True, vmem_limit_bytes=67_043_328
        ),
        name="layer",
    )(*operands)


def finish_kernel(cols, *refs):
    (lo, tg, ga, gi, gd, small,
     lo_out, tg_out, qkv_out, qv_out, out_out, in_out, down_out, v0, v1, v2, v3, v4, v5, v6, rms_out) = refs
    lo_out[...] = lo[...]
    tg_out[...] = tg[...].astype(F32)
    qkv_out[0] = ga[:, 2 * cols:3 * cols]
    qkv_out[1] = ga[:, 0:cols]
    qkv_out[2] = ga[:, cols:2 * cols]
    out_out[...] = jnp.transpose(ga[:, 3 * cols:])
    in_out[...] = gi[...]
    down_out[...] = gd[...]
    qv_out[0:1] = small[18:19, 0:cols]
    qv_out[1:2] = small[17:18, cols:2 * cols]
    for row, ref in zip((0, 1, 2, 16, 3, 4, 5), (v0, v1, v2, v3, v4, v5, v6)):
        ref[...] = small[row]
    count = small[9:10, 0:1] * small.shape[1]
    for i in range(3):
        rms_out[0:1, i:i + 1] = jnp.sqrt(jnp.sum(small[6 + i:7 + i], axis=1, keepdims=True) / count)


def run_finish(cols, *operands):
    _, quarter, width = operands[0].shape
    chunk, hidden_cols = operands[3].shape
    shapes = [
        ((TP, quarter, width), BF16), ((TP, quarter, width), F32), ((3, chunk, cols), F32), ((2, cols), F32),
        ((cols, chunk), F32), ((chunk, hidden_cols), F32), ((chunk, hidden_cols), F32),
        ((width,), F32), ((width,), F32), ((width,), F32), ((hidden_cols,), F32),
        ((width,), F32), ((width,), F32), ((width,), F32), ((1, 3), F32),
    ]
    vmem = pl.BlockSpec(memory_space=pltpu.VMEM)
    return pl.pallas_call(
        functools.partial(finish_kernel, cols),
        out_shape=tuple(jax.ShapeDtypeStruct(*shape) for shape in shapes),
        in_specs=[vmem] * len(operands),
        out_specs=(vmem,) * len(shapes),
        name="finish",
    )(*operands)


def body(
    sizes,
    tokens, segment_ids, valid_mask, qkv_weight, qv_bias, out_weight, out_bias, norm1_gain, norm1_shift,
    in_weight, in_bias, down_weight, down_bias, norm2_gain, norm2_shift, out_cotangent,
):
    shards, ctxs = sizes
    _, piece, width = tokens.shape
    cols = qkv_weight.shape[2]
    heads = cols // HEAD_DIM
    raw = qkv_weight.shape[1] % 16 == 0 and ctxs <= 2
    if raw:
        wctx = ctxs
        parts = [qkv_weight, out_weight, in_weight, down_weight.T]
        chunk = in_weight.shape[0]
    else:
        wctx = 1
        own = jnp.concatenate([qkv_weight[1], qkv_weight[2], qkv_weight[0], out_weight.T], axis=1)
        own, into, down = (
            lax.all_gather(part, "ctx", axis=0, tiled=True) for part in (own, in_weight, down_weight.T)
        )
        parts = [own, out_weight, into, down]
        chunk = own.shape[0]
    dims = (shards, ctxs, wctx, piece, width, chunk, heads)
    vectors = [out_bias, norm1_gain, norm1_shift, in_bias, down_bias, norm2_gain, norm2_shift]
    results = run_layer(
        dims, 160, tokens.reshape(piece, width), out_cotangent.reshape(piece, width), segment_ids, valid_mask,
        *parts, qv_bias, *vectors
    )
    if raw:
        lo, tg, g_qkv, g_qv, g_out, g_in, g_down, *sums, rms = run_finish(cols, *results)
        return (
            lo.reshape(1, piece, width), tg.reshape(1, piece, width), g_qkv, g_qv, g_out, sums[0], sums[1], sums[2],
            g_in, sums[3], g_down.T, sums[4], sums[5], sums[6], rms.reshape(-1),
        )
    lo, tg, ga, gi, gd, small = results
    ga, gi, gd = (lax.psum_scatter(g, "ctx", scatter_dimension=0, tiled=True) for g in (ga, gi, gd))
    g_qkv = jnp.stack([ga[:, 2 * cols:3 * cols], ga[:, 0:cols], ga[:, cols:2 * cols]])
    sums = jnp.sum(small[6:9], axis=1)
    return (
        lo.reshape(1, piece, width),
        tg.reshape(1, piece, width).astype(F32),
        g_qkv,
        jnp.stack([small[18, 0:cols], small[17, cols:2 * cols]]),
        ga[:, 3 * cols:].T,
        small[0], small[1], small[2],
        gi,
        small[16],
        gd.T,
        small[3], small[4], small[5],
        jnp.sqrt(sums / (small[9, 0] * width)),
    )


def solution(mesh):
    sizes = (mesh.shape["shard"], mesh.shape["ctx"])
    return jax.shard_map(
        functools.partial(body, sizes),
        mesh=mesh,
        in_specs=(
            P("shard", "ctx", None), P("shard", "ctx"), P("shard", "ctx"),
            P(None, ("shard", "ctx"), "tp"), P(None, "tp"), P("tp", ("shard", "ctx")),
            P(), P(), P(),
            P(("shard", "ctx"), "tp"), P("tp"), P("tp", ("shard", "ctx")),
            P(), P(), P(),
            P("shard", "ctx", None),
        ),
        out_specs=(
            P("shard", "ctx", None), P("shard", "ctx", None),
            P(None, ("shard", "ctx"), "tp"), P(None, "tp"), P("tp", ("shard", "ctx")),
            P(), P(), P(),
            P(("shard", "ctx"), "tp"), P("tp"), P("tp", ("shard", "ctx")),
            P(), P(), P(), P(),
        ),
        check_vma=False,
    )
```

```python
import functools

import jax
import jax.numpy as jnp
from jax import lax
from jax.experimental import pallas as pl
from jax.experimental.pallas import tpu as pltpu
from jax.sharding import PartitionSpec as P

HEAD_DIM = 64
LANES = 128
TP = 4
EPS = 1e-12
MASKED = -1e30
F32 = jnp.float32
BF16 = jnp.bfloat16
BLOCKS = 4
ORDER = (
    "A0A1A2A3B0B1B2B3C0D0C1C2E0D1D2E1F0E2C3G0D3H0F1E3",
    "F2G1G2H1I0F3H2G3I1H3X0I2I3X1",
)


def nt(left, right):
    return lax.dot_general(left, right, (((1,), (1,)), ((), ())), preferred_element_type=F32)


def nn(left, right):
    return lax.dot_general(left, right, (((1,), (0,)), ((), ())), preferred_element_type=F32)


def gelu_and_slope(pre):
    scale = 0.7978845608028654
    cube = 0.044715
    square = pre * pre
    tanh = jnp.tanh(scale * pre * (1.0 + cube * square))
    half = 0.5 * (1.0 + tanh)
    slope = half + 0.5 * pre * (1.0 - tanh * tanh) * (scale * (1.0 + 3.0 * cube * square))
    return pre * half, slope


def column_sum(rows):
    return jnp.sum(rows, axis=0, keepdims=True)


def norm_forward(rows):
    mean = jnp.mean(rows, axis=-1, keepdims=True)
    centred = rows - mean
    spread = jnp.mean(centred * centred, axis=-1, keepdims=True)
    inverse = lax.rsqrt(spread + EPS)
    return centred * inverse, inverse


def norm_backward(grad, unit, inverse, gain):
    scaled = grad * gain
    first = jnp.mean(scaled, axis=-1, keepdims=True)
    second = jnp.mean(scaled * unit, axis=-1, keepdims=True)
    return inverse * (scaled - first - unit * second)


class Net:
    def __init__(self, send_sems, recv_sems):
        self.send_sems, self.recv_sems, self.copies = send_sems, recv_sems, []

    def send(self, source, target, where):
        place = len(self.copies)
        copy = pltpu.make_async_remote_copy(
            src_ref=source,
            dst_ref=target,
            send_sem=self.send_sems.at[place],
            recv_sem=self.recv_sems.at[place],
            device_id=where,
            device_id_type=pl.DeviceIdType.MESH,
        )
        copy.start()
        self.copies.append(copy)
        return copy

    def finish(self):
        for copy in self.copies:
            copy.wait_send()


def layer_kernel(dims, *refs):
    shards, ctxs, wctx, piece, width, chunk, heads = dims
    rows_b = piece // BLOCKS
    half = rows_b // 2
    cols = heads * HEAD_DIM
    (x_ref, cot_ref, seg_ref, valid_ref, qkv_ref, out_ref, wi_ref, wd_ref, qv_bias_ref, out_bias_ref, gain1_ref,
     shift1_ref, in_bias_ref, down_bias_ref, gain2_ref, shift2_ref,
     lo_ref, tg_ref, ga_ref, gi_ref, gd_ref, small_ref,
     wa, wi, wd, xt, ht, dft, dat, code_all, bias, kv, kvt, qm, sbuf, pt, ott, mt, vcol, cot,
     hid, act, slope, dffn, dpre, datt, lobuf, tgbuf,
     part, near_in, far_out, far_in, gown, gxs, gxr, gzs, gzr, dkvs, dkvr, dkv0, dqt, dproj, dqp, ctxp, dom0, dom1,
     unit1, hidden, resid2, resid1, sa, sb,
     sa1, sac, sas, sbc, sbs,
     wa_ref, code_ref, vec_ref,
     local_sems, send_sems, recv_sems) = refs
    me_s, me_c, me_t = lax.axis_index("shard"), lax.axis_index("ctx"), lax.axis_index("tp")
    mine = me_t % 2
    other = 1 - mine
    near = {"tp": me_t + 1 - 2 * mine}
    far = {"tp": (me_t + 2) % TP}
    wc = me_c if wctx > 1 else 0
    net = Net(send_sems, recv_sems)

    def shard_at(step):
        return (me_s + step) % shards

    def ctx_at(step):
        return (me_c + step) % ctxs

    steps = [d for d in range(1, shards) if d % 2] + [d for d in range(1, shards) if d % 2 == 0]

    barrier = pltpu.get_barrier_semaphore()
    peers = [near, far]
    peers += [{"ctx": ctx_at(e)} for e in range(1, ctxs)]
    peers += [{"shard": shard_at(d)} for d in range(1, shards)]
    for peer in peers:
        pl.semaphore_signal(barrier, inc=1, device_id=peer, device_id_type=pl.DeviceIdType.MESH)
    if wctx < ctxs:
        wa_ref[...] = qkv_ref[...]
    else:
        wa_ref[:, 0:cols] = qkv_ref[1]
        wa_ref[:, cols:2 * cols] = qkv_ref[2]
        wa_ref[:, 2 * cols:3 * cols] = qkv_ref[0]
        wa_ref[:, 3 * cols:] = jnp.transpose(out_ref[...].astype(F32)).astype(BF16)
    pl.semaphore_wait(barrier, len(peers))

    def gather_along(buf, own, lo, hi):
        span = slice(lo, hi)
        return {
            d: net.send(own.at[:, span], buf.at[me_s, wc, :, span], {"shard": shard_at(d)}) for d in steps
        }

    def gather_across(buf, own, lo, hi):
        span = slice(lo, hi)
        return [
            net.send(own.at[:, span], buf.at[me_s, wc, :, span], {"ctx": ctx_at(e)}) for e in range(1, wctx)
        ]

    def gather_forward(buf, along, across, lo, hi, which=None):
        span = slice(lo, hi)
        for d in steps if which is None else which:
            along[d].wait_recv()
            source = buf.at[shard_at(shards - d), wc, :, span]
            across += [net.send(source, source, {"ctx": ctx_at(e)}) for e in range(1, wctx)]

    def wait_all(copies):
        for copy in copies:
            copy.wait_recv()

    def whole(buf, lo, hi):
        return buf[:, :, :, lo:hi].reshape(width, hi - lo)

    def sum_start(k, b, value):
        part[k, b] = value.reshape(2, half, width)
        return net.send(part.at[k, b, other], near_in.at[k, b], near)

    def sum_pass(k, b, copy):
        copy.wait_recv()
        far_out[k, b] = (part[k, b, mine] + near_in[k, b]).astype(BF16)
        return net.send(far_out.at[k, b], far_in.at[k, b], far)

    def sum_end(k, b, copy):
        copy.wait_recv()
        return far_out[k, b].astype(F32) + far_in[k, b].astype(F32)

    def share(buf, b, value):
        buf[b, mine] = value
        return net.send(buf.at[b, mine], buf.at[b, mine], near)

    def block(b):
        return slice(b * rows_b, (b + 1) * rows_b)

    def own_rows(b):
        return pl.ds(pl.multiple_of(b * rows_b + mine * half, half), half)

    def grad_across(k, lo, hi):
        span = slice(lo, hi)
        if wctx == 1:
            return None
        return {
            d: net.send(gxs.at[k, shard_at(d), :, span], gxr.at[k, shard_at(d), :, span], {"ctx": ctx_at(1)})
            for d in steps + [0]
        }

    def grad_along(k, lo, hi, across):
        span = slice(lo, hi)
        out = {}
        for d in steps:
            s = shard_at(d)
            total = gown[k, s, :, span]
            if wctx > 1:
                across[d].wait_recv()
                total = total + gxr[k, s, :, span].astype(F32)
            gzs[k, d - 1, :, span] = total.astype(BF16)
            out[d] = net.send(gzs.at[k, d - 1, :, span], gzr.at[k, d - 1, :, span], {"shard": s})
        return out

    def grad_end(k, lo, hi, across, along, out_ref):
        span = slice(lo, hi)
        total = gown[k, me_s, :, span]
        if wctx > 1:
            across[0].wait_recv()
            total = total + gxr[k, me_s, :, span].astype(F32)
        for d in steps:
            along[d].wait_recv()
            total = total + gzr[k, d - 1, :, span].astype(F32)
        out_ref[:, span] = total

    def grad_product(k, lo, terms):
        for c in range(wctx - 1, -1, -1):
            where = (me_c + c) % wctx if wctx > 1 else 0
            value = 0.0
            for left, right in terms:
                value = value + nn(left[where].reshape(shards * chunk, piece), right)
            n = value.shape[1]
            value = value.reshape(shards, chunk, n)
            if c > 0:
                gxs[k, :, :, lo:lo + n] = value.astype(BF16)
            else:
                gown[k, :, :, lo:lo + n] = value

    def store_transposed(target, value):
        turned = jnp.transpose(value)
        for s in range(shards):
            for c in range(wctx):
                begin = (s * wctx + c) * chunk
                target[c, s] = turned[begin:begin + chunk]

    def exchange(buf, source, axis, at, count, me):
        buf[me] = source
        return [net.send(buf.at[me], buf.at[me], {axis: at(e)}) for e in range(1, count)]

    def exchange_end(buf, state, count):
        wait_all(state)
        total = buf[0]
        for i in range(1, count):
            total = total + buf[i]
        return total

    split = 2 * cols
    kv_along = gather_along(wa, wa_ref, 0, split)
    kv_across = gather_across(wa, wa_ref, 0, split)
    seg = seg_ref[...].astype(F32)
    real = valid_ref[...] == 1
    code_ref[...] = jnp.zeros_like(code_ref)
    code_ref[0:1] = jnp.where(real, seg, -1.0)
    code_ref[1:2] = seg
    code_ref[2:3] = jnp.where(real, 1.0, 0.0)
    code_sends = [net.send(code_ref, code_all.at[e], {"ctx": ctx_at(e)}) for e in range(1, ctxs)]
    qo_along = gather_along(wa, wa_ref, split, width)
    qo_across = gather_across(wa, wa_ref, split, width)
    wa[me_s, wc] = wa_ref[...]
    wi[me_s, wc] = wi_ref[...]
    wd[me_s, wc] = wd_ref[...]
    code_all[0] = code_ref[...]
    fetches = [
        pltpu.make_async_copy(cot_ref.at[own_rows(b)], cot.at[b], local_sems.at[b]) for b in range(BLOCKS)
    ]
    for fetch in fetches:
        fetch.start()
    vec_ref[...] = jnp.zeros_like(vec_ref)
    vec_ref[0:1, 0:cols] = qv_bias_ref[0:1]
    vec_ref[1:2, cols:2 * cols] = qv_bias_ref[1:2]
    vcol[...] = jnp.transpose(jnp.broadcast_to(code_ref[2:3, :], (LANES, piece)))
    gather_forward(wa, kv_along, kv_across, 0, split, steps[:1])
    query_code = code_ref[1:2, :]

    def store_bias(e):
        key_code = jnp.transpose(jnp.broadcast_to(code_all[e][0:1, :], (LANES, piece)))[:, 0:1]
        allowed = key_code == query_code
        if e == 0:
            rows = lax.broadcasted_iota(jnp.int32, (piece, piece), 0)
            lanes = lax.broadcasted_iota(jnp.int32, (piece, piece), 1)
            allowed = allowed | (rows == lanes)
        bias[e] = jnp.where(allowed, 0.0, MASKED)

    store_bias(0)
    gather_forward(wa, kv_along, kv_across, 0, split, steps[1:])
    gather_forward(wa, qo_along, qo_across, split, width, steps[:1])
    wait_all(kv_across)

    x = x_ref[...]
    kv[0] = (nn(x, whole(wa, 0, split)) + vec_ref[1:2, 0:split]).astype(BF16)
    gather_forward(wa, qo_along, qo_across, split, width, steps[1:])
    kv_sends = [net.send(kv.at[0], kv.at[e], {"ctx": ctx_at(e)}) for e in range(1, ctxs)]
    in_along = gather_along(wi, wi_ref, 0, width)
    down_along = gather_along(wd, wd_ref, 0, width)
    in_across = gather_across(wi, wi_ref, 0, width)
    down_across = gather_across(wd, wd_ref, 0, width)
    kvt[0] = jnp.transpose(kv[0])
    wait_all(code_sends)
    for e in range(1, ctxs):
        store_bias(e)
    wait_all(qo_across)
    q_low = (nn(x, whole(wa, split, split + 256)) + vec_ref[0:1, 0:256]).astype(BF16).astype(F32) * 0.125
    lane = lax.broadcasted_iota(jnp.int32, (piece, 256), 1)
    for h in range(heads):
        inside = (lane >= h * HEAD_DIM) & (lane < (h + 1) * HEAD_DIM)
        qm[h] = jnp.where(inside, q_low, 0.0).astype(BF16)

    tops = []
    for h in range(heads):
        s = nt(kv[0][:, 0:256], qm[h]) + bias[0]
        sbuf[h, 0] = s
        tops.append(jnp.max(s, axis=0, keepdims=True))
    store_transposed(xt, x_ref[...])
    ott[0:cols] = jnp.zeros((cols, piece), F32)
    mt[0:cols] = jnp.zeros((cols, piece), F32)
    gather_forward(wi, in_along, in_across, 0, width)
    for e in range(1, ctxs):
        kv_sends[e - 1].wait_recv()
        kvt[e] = jnp.transpose(kv[e])
    for h in range(heads):
        top = tops[h]
        for e in range(1, ctxs):
            s = nt(kv[e][:, 0:256], qm[h]) + bias[e]
            sbuf[h, e] = s
            top = jnp.maximum(top, jnp.max(s, axis=0, keepdims=True))
        rows = slice(cols + h * HEAD_DIM, cols + (h + 1) * HEAD_DIM)
        total = jnp.zeros((1, piece), F32)
        mixed = jnp.zeros((HEAD_DIM, piece), F32)
        for e in range(ctxs):
            weights = jnp.exp(sbuf[h, e] - top)
            total = total + column_sum(weights)
            low = weights.astype(BF16)
            pt[h, e] = low
            mixed = mixed + nn(kvt[e, rows], low)
        inverse = 1.0 / total
        ott[rows] = mixed * inverse
        mt[rows] = jnp.broadcast_to(inverse, (HEAD_DIM, piece))
    ctxp[...] = jnp.transpose(ott[...]).astype(BF16)

    out_bias, gain1, shift1, in_bias = (
        ref[...].reshape(1, -1) for ref in (out_bias_ref, gain1_ref, shift1_ref, in_bias_ref)
    )
    down_bias, gain2, shift2 = (ref[...].reshape(1, -1) for ref in (down_bias_ref, gain2_ref, shift2_ref))
    sa[...] = jnp.zeros_like(sa)
    near_copy, far_copy, share_copy, inverse1, out_copy = {}, {}, {}, {}, {}

    def add_sum(row, value):
        sa[row:row + 1] = sa[row:row + 1] + column_sum(value)

    def stage_a(b):
        near_copy[0, b] = sum_start(0, b, nt(ctxp[block(b)], whole(wa, split, width)))

    def stage_b(b):
        far_copy[0, b] = sum_pass(0, b, near_copy[0, b])

    def stage_c(b):
        attn = sum_end(0, b, far_copy[0, b]) + out_bias
        x_own = x_ref[own_rows(b)].astype(F32)
        valid = vcol[own_rows(b), 0:1]
        unit, inverse1[b] = norm_forward(x_own + attn)
        unit1[b] = unit
        own_hidden = unit * gain1 + shift1
        hidden[b] = own_hidden
        share_copy[0, b] = share(hid, b, own_hidden.astype(BF16))
        add_sum(6, valid * x_own * x_own)
        add_sum(7, valid * attn * attn)
        sa[9:10] = sa[9:10] + column_sum(valid)

    def stage_d(b):
        if b == 0:
            wait_all(in_across)
        share_copy[0, b].wait_recv()
        pre = nn(hid[b].reshape(rows_b, width), whole(wi, 0, width)) + in_bias
        value, slope[b] = gelu_and_slope(pre)
        act[b] = value.astype(BF16)
        if b == 0:
            gather_forward(wd, down_along, down_across, 0, width)
            wait_all(down_across)
        near_copy[1, b] = sum_start(1, b, nt(act[b], whole(wd, 0, width)))

    def stage_e(b):
        far_copy[1, b] = sum_pass(1, b, near_copy[1, b])

    def stage_f(b):
        if b == 0:
            for fetch in fetches:
                fetch.wait()
        ffn = sum_end(1, b, far_copy[1, b]) + down_bias
        valid = vcol[own_rows(b), 0:1]
        unit, inverse = norm_forward(hidden[b] + ffn)
        grad = cot[b]
        d_resid2 = norm_backward(grad, unit, inverse, gain2)
        low = d_resid2.astype(BF16)
        share_copy[1, b] = share(dffn, b, low)
        resid2[b] = d_resid2
        out_copy[b] = share(lobuf, b, (unit * gain2 + shift2).astype(BF16))
        add_sum(8, valid * ffn * ffn)
        add_sum(3, low.astype(F32))
        add_sum(4, grad * unit)
        add_sum(5, grad)

    def stage_g(b):
        share_copy[1, b].wait_recv()
        d_act = nn(dffn[b].reshape(rows_b, width), whole(wd, 0, width))
        dpre[b] = (d_act * slope[b]).astype(BF16)
        near_copy[2, b] = sum_start(2, b, nt(dpre[b], whole(wi, 0, width)))

    def stage_h(b):
        far_copy[2, b] = sum_pass(2, b, near_copy[2, b])

    def stage_i(b):
        d_hidden = resid2[b] + sum_end(2, b, far_copy[2, b])
        unit = unit1[b]
        d_resid1 = norm_backward(d_hidden, unit, inverse1[b], gain1)
        low = d_resid1.astype(BF16)
        share_copy[2, b] = share(datt, b, low)
        resid1[b] = d_resid1
        add_sum(0, low.astype(F32))
        add_sum(1, d_hidden * unit)
        add_sum(2, d_hidden)

    stages = dict(A=stage_a, B=stage_b, C=stage_c, D=stage_d, E=stage_e, F=stage_f, G=stage_g, H=stage_h, I=stage_i)
    state = {}

    def down_grads():
        store_transposed(dft, dffn[...].reshape(piece, width))
        grad_product(2, 0, [(dft, act[...].reshape(piece, width))])
        state["down"] = grad_across(2, 0, width)

    def in_grads():
        store_transposed(ht, hid[...].reshape(piece, width))
        grad_product(1, 0, [(ht, dpre[...].reshape(piece, width))])
        state["in"] = grad_across(1, 0, width)

    for name in ORDER:
        for i in range(0, len(name), 2):
            if name[i] == "X":
                (down_grads, in_grads)[int(name[i + 1])]()
            else:
                stages[name[i]](int(name[i + 1]))

    sb[...] = jnp.zeros_like(sb)
    sb[0:1] = column_sum(dpre[...].reshape(piece, width).astype(F32))
    sa_near = net.send(sa, sa1, near)
    down_sums = grad_along(2, 0, width, state["down"])
    for b in range(BLOCKS):
        share_copy[2, b].wait_recv()
    d_att_all = datt[...].reshape(piece, width)
    d_ctx = nn(d_att_all, whole(wa, split, width)).astype(BF16).astype(F32)
    d_mix = d_ctx * jnp.transpose(mt[...])
    lane = lax.broadcasted_iota(jnp.int32, (piece, LANES), 1)
    dom0[...] = d_mix[:, 0:256].astype(BF16)
    last = d_mix[:, 256:384]
    dom1[0] = jnp.where(lane < HEAD_DIM, last, 0.0).astype(BF16)
    dom1[1] = jnp.where(lane >= HEAD_DIM, last, 0.0).astype(BF16)
    product = jnp.transpose(d_mix)[cols:] * ott[cols:]
    deltas = [column_sum(product[h * HEAD_DIM:(h + 1) * HEAD_DIM]) for h in range(heads)]
    dqt[...] = jnp.zeros((2 * cols, piece), F32)

    def attention_back(e):
        first = jnp.zeros((piece, 256), F32)
        second = jnp.zeros((piece, LANES), F32)
        for h in range(heads):
            if h == 0:
                d_probs = nt(kv[e][:, 0:256], dom0[...])
            else:
                d_probs = nt(kv[e][:, 256:384], dom1[h - 1])
            d_scores = (pt[h, e].astype(F32) * (d_probs - deltas[h])).astype(BF16)
            first = first + nn(d_scores, qm[h])
            if h == 0:
                first = first + nn(pt[h, e], dom0[...])
            else:
                second = second + nn(pt[h, e], dom1[h - 1])
            rows = slice(h * HEAD_DIM, (h + 1) * HEAD_DIM)
            dqt[rows] = dqt[rows] + nn(kvt[e, rows], d_scores)
        return first, second

    dkv_sends = []
    for e in range(ctxs - 1, 0, -1):
        first, second = attention_back(e)
        dkvs[e - 1, :, 0:256] = first.astype(BF16)
        dkvs[e - 1, :, 256:384] = second.astype(BF16)
        dkv_sends.append(net.send(dkvs.at[e - 1], dkvr.at[e - 1], {"ctx": ctx_at(ctxs - e)}))
    sa_near.wait_recv()
    sa_c = exchange(sac, sa[...] + sa1[...], "ctx", ctx_at, ctxs, me_c)
    first, second = attention_back(0)
    dkv0[:, 0:256] = first
    dkv0[:, 256:384] = second
    dqp[...] = jnp.transpose(dqt[...] * 0.125).astype(BF16)
    store_transposed(dat, d_att_all)
    grad_product(0, split, [(xt, dqp[...]), (dat, ctxp[...])])
    qo_state = grad_across(0, split, width)
    in_sums = grad_along(1, 0, width, state["in"])
    sa_s = exchange(sas, exchange_end(sac, sa_c, ctxs), "shard", shard_at, shards, me_s)
    total = dkv0[...]
    for i in range(ctxs - 1):
        dkv_sends[i].wait_recv()
        total = total + dkvr[ctxs - 2 - i].astype(F32)
    dproj[...] = total.astype(BF16)

    def back_tokens(b):
        value = nt(dproj[block(b)], whole(wa, 0, split))
        return value + nt(dqp[block(b), 0:256], whole(wa, split, split + 256))

    for b in range(2):
        near_copy[3, b] = sum_start(3, b, back_tokens(b))
    far_copy[3, 0] = sum_pass(3, 0, near_copy[3, 0])
    grad_product(0, 0, [(xt, dproj[...])])
    kv_state = grad_across(0, 0, split)
    far_copy[3, 1] = sum_pass(3, 1, near_copy[3, 1])
    for b in range(2, BLOCKS):
        near_copy[3, b] = sum_start(3, b, back_tokens(b))
    for b in range(2, BLOCKS):
        far_copy[3, b] = sum_pass(3, b, near_copy[3, b])
    sb[1:2, 0:split] = column_sum(dproj[...].astype(F32))
    sb[2:3, 0:split] = column_sum(dqp[...].astype(F32))
    sb_c = exchange(sbc, sb[...], "ctx", ctx_at, ctxs, me_c)
    qo_sums = grad_along(0, split, width, qo_state)
    for b in range(BLOCKS):
        share_copy[3, b] = share(tgbuf, b, (resid1[b] + sum_end(3, b, far_copy[3, b])).astype(BF16))
    sb_s = exchange(sbs, exchange_end(sbc, sb_c, ctxs), "shard", shard_at, shards, me_s)
    kv_sums = grad_along(0, 0, split, kv_state)
    grad_end(2, 0, width, state["down"], down_sums, gd_ref)
    for b in range(BLOCKS):
        out_copy[b].wait_recv()
        lo_ref[b] = lobuf[b].reshape(rows_b, width)
    small_ref[0:16] = exchange_end(sas, sa_s, shards)
    grad_end(1, 0, width, state["in"], in_sums, gi_ref)
    for b in range(BLOCKS):
        share_copy[3, b].wait_recv()
        tg_ref[b] = tgbuf[b].reshape(rows_b, width)
    small_ref[16:24] = exchange_end(sbs, sb_s, shards)
    grad_end(0, split, width, qo_state, qo_sums, ga_ref)
    grad_end(0, 0, split, kv_state, kv_sums, ga_ref)
    net.finish()


def run_layer(dims, copies, *operands):
    shards, ctxs, wctx, piece, width, chunk, heads = dims
    rows_b = piece // BLOCKS
    half = rows_b // 2
    cols = heads * HEAD_DIM
    hidden_cols = operands[6].shape[1]
    vmem = pl.BlockSpec(memory_space=pltpu.VMEM)
    weights = (shards, wctx, chunk, width)
    turned = (wctx, shards, chunk, piece)
    V = pltpu.VMEM
    others = max(shards - 1, 1)
    shared = (BLOCKS, 2, half, width)
    hidden = (BLOCKS, rows_b, hidden_cols)
    scratch = [
        V(weights, BF16), V(weights, BF16), V(weights, BF16),
        V(turned, BF16), V(turned, BF16), V(turned, BF16), V(turned, BF16),
        V((ctxs, 8, piece), F32), V((ctxs, piece, piece), F32),
        V((ctxs, piece, 2 * cols), BF16), V((ctxs, 2 * cols, piece), BF16), V((heads, piece, 256), BF16),
        V((heads, ctxs, piece, piece), F32), V((heads, ctxs, piece, piece), BF16),
        V((2 * cols, piece), F32), V((2 * cols, piece), F32), V((piece, LANES), F32), V((BLOCKS, half, width), F32),
        V(shared, BF16), V(hidden, BF16), V(hidden, F32),
        V(shared, BF16), V(hidden, BF16), V(shared, BF16), V(shared, BF16), V(shared, BF16),
        V((4, BLOCKS, 2, half, width), F32), V((4, BLOCKS, half, width), F32),
        V((4, BLOCKS, half, width), BF16), V((4, BLOCKS, half, width), BF16),
        V((3, shards, chunk, width), F32), V((3, shards, chunk, width), BF16), V((3, shards, chunk, width), BF16),
        V((3, others, chunk, width), BF16), V((3, others, chunk, width), BF16),
        V((ctxs - 1, piece, 2 * cols), BF16), V((ctxs - 1, piece, 2 * cols), BF16), V((piece, 2 * cols), F32),
        V((2 * cols, piece), F32), V((piece, 2 * cols), BF16), V((piece, 2 * cols), BF16), V((piece, 2 * cols), BF16),
        V((piece, 256), BF16), V((2, piece, LANES), BF16),
        V((BLOCKS, half, width), F32), V((BLOCKS, half, width), F32), V((BLOCKS, half, width), F32),
        V((BLOCKS, half, width), F32),
        V((16, width), F32), V((8, width), F32),
        V((16, width), F32), V((ctxs, 16, width), F32), V((shards, 16, width), F32),
        V((ctxs, 8, width), F32), V((shards, 8, width), F32),
        V((chunk, width), BF16), V((8, piece), F32), V((8, 2 * cols), F32),
        pltpu.SemaphoreType.DMA((BLOCKS,)), pltpu.SemaphoreType.DMA((copies,)), pltpu.SemaphoreType.DMA((copies,)),
    ]
    return pl.pallas_call(
        functools.partial(layer_kernel, dims),
        out_shape=(
            jax.ShapeDtypeStruct((BLOCKS, rows_b, width), BF16),
            jax.ShapeDtypeStruct((BLOCKS, rows_b, width), BF16),
            jax.ShapeDtypeStruct((chunk, width), F32),
            jax.ShapeDtypeStruct((chunk, hidden_cols), F32),
            jax.ShapeDtypeStruct((chunk, hidden_cols), F32),
            jax.ShapeDtypeStruct((24, width), F32),
        ),
        in_specs=[vmem, pl.BlockSpec(memory_space=pl.ANY)] + [vmem] * (len(operands) - 2),
        out_specs=(vmem,) * 6,
        scratch_shapes=scratch,
        compiler_params=pltpu.CompilerParams(
            collective_id=0, has_side_effects=True, vmem_limit_bytes=67_043_328
        ),
        name="layer",
    )(*operands)


def finish_kernel(cols, *refs):
    (lo, tg, ga, gi, gd, small,
     lo_out, tg_out, qkv_out, qv_out, out_out, in_out, down_out, v0, v1, v2, v3, v4, v5, v6, rms_out) = refs
    lo_out[...] = lo[...]
    tg_out[...] = tg[...].astype(F32)
    qkv_out[0] = ga[:, 2 * cols:3 * cols]
    qkv_out[1] = ga[:, 0:cols]
    qkv_out[2] = ga[:, cols:2 * cols]
    out_out[...] = jnp.transpose(ga[:, 3 * cols:])
    in_out[...] = gi[...]
    down_out[...] = gd[...]
    qv_out[0:1] = small[18:19, 0:cols]
    qv_out[1:2] = small[17:18, cols:2 * cols]
    for row, ref in zip((0, 1, 2, 16, 3, 4, 5), (v0, v1, v2, v3, v4, v5, v6)):
        ref[...] = small[row]
    count = small[9:10, 0:1] * small.shape[1]
    for i in range(3):
        rms_out[0:1, i:i + 1] = jnp.sqrt(jnp.sum(small[6 + i:7 + i], axis=1, keepdims=True) / count)


def run_finish(cols, *operands):
    _, rows_b, width = operands[0].shape
    chunk, hidden_cols = operands[3].shape
    shapes = [
        ((BLOCKS, rows_b, width), BF16), ((BLOCKS, rows_b, width), F32), ((3, chunk, cols), F32), ((2, cols), F32),
        ((cols, chunk), F32), ((chunk, hidden_cols), F32), ((chunk, hidden_cols), F32),
        ((width,), F32), ((width,), F32), ((width,), F32), ((hidden_cols,), F32),
        ((width,), F32), ((width,), F32), ((width,), F32), ((1, 3), F32),
    ]
    vmem = pl.BlockSpec(memory_space=pltpu.VMEM)
    return pl.pallas_call(
        functools.partial(finish_kernel, cols),
        out_shape=tuple(jax.ShapeDtypeStruct(*shape) for shape in shapes),
        in_specs=[vmem] * len(operands),
        out_specs=(vmem,) * len(shapes),
        name="finish",
    )(*operands)


def body(
    sizes,
    tokens, segment_ids, valid_mask, qkv_weight, qv_bias, out_weight, out_bias, norm1_gain, norm1_shift,
    in_weight, in_bias, down_weight, down_bias, norm2_gain, norm2_shift, out_cotangent,
):
    shards, ctxs = sizes
    _, piece, width = tokens.shape
    cols = qkv_weight.shape[2]
    heads = cols // HEAD_DIM
    raw = qkv_weight.shape[1] % 16 == 0 and ctxs <= 2
    if raw:
        wctx = ctxs
        parts = [qkv_weight, out_weight, in_weight, down_weight.T]
        chunk = in_weight.shape[0]
    else:
        wctx = 1
        own = jnp.concatenate([qkv_weight[1], qkv_weight[2], qkv_weight[0], out_weight.T], axis=1)
        own, into, down = (
            lax.all_gather(part, "ctx", axis=0, tiled=True) for part in (own, in_weight, down_weight.T)
        )
        parts = [own, out_weight, into, down]
        chunk = own.shape[0]
    dims = (shards, ctxs, wctx, piece, width, chunk, heads)
    vectors = [out_bias, norm1_gain, norm1_shift, in_bias, down_bias, norm2_gain, norm2_shift]
    results = run_layer(
        dims, 160, tokens.reshape(piece, width), out_cotangent.reshape(piece, width), segment_ids, valid_mask,
        *parts, qv_bias, *vectors
    )
    if raw:
        lo, tg, g_qkv, g_qv, g_out, g_in, g_down, *sums, rms = run_finish(cols, *results)
        return (
            lo.reshape(1, piece, width), tg.reshape(1, piece, width), g_qkv, g_qv, g_out, sums[0], sums[1], sums[2],
            g_in, sums[3], g_down.T, sums[4], sums[5], sums[6], rms.reshape(-1),
        )
    lo, tg, ga, gi, gd, small = results
    ga, gi, gd = (lax.psum_scatter(g, "ctx", scatter_dimension=0, tiled=True) for g in (ga, gi, gd))
    g_qkv = jnp.stack([ga[:, 2 * cols:3 * cols], ga[:, 0:cols], ga[:, cols:2 * cols]])
    sums = jnp.sum(small[6:9], axis=1)
    return (
        lo.reshape(1, piece, width),
        tg.reshape(1, piece, width).astype(F32),
        g_qkv,
        jnp.stack([small[18, 0:cols], small[17, cols:2 * cols]]),
        ga[:, 3 * cols:].T,
        small[0], small[1], small[2],
        gi,
        small[16],
        gd.T,
        small[3], small[4], small[5],
        jnp.sqrt(sums / (small[9, 0] * width)),
    )


def solution(mesh):
    sizes = (mesh.shape["shard"], mesh.shape["ctx"])
    return jax.shard_map(
        functools.partial(body, sizes),
        mesh=mesh,
        in_specs=(
            P("shard", "ctx", None), P("shard", "ctx"), P("shard", "ctx"),
            P(None, ("shard", "ctx"), "tp"), P(None, "tp"), P("tp", ("shard", "ctx")),
            P(), P(), P(),
            P(("shard", "ctx"), "tp"), P("tp"), P("tp", ("shard", "ctx")),
            P(), P(), P(),
            P("shard", "ctx", None),
        ),
        out_specs=(
            P("shard", "ctx", None), P("shard", "ctx", None),
            P(None, ("shard", "ctx"), "tp"), P(None, "tp"), P("tp", ("shard", "ctx")),
            P(), P(), P(),
            P(("shard", "ctx"), "tp"), P("tp"), P("tp", ("shard", "ctx")),
            P(), P(), P(), P(),
        ),
        check_vma=False,
    )
```

```python
import functools

import jax
import jax.numpy as jnp
from jax import lax
from jax.experimental import pallas as pl
from jax.experimental.pallas import tpu as pltpu
from jax.sharding import PartitionSpec as P

HEAD_DIM = 64
LANES = 128
TP = 4
EPS = 1e-12
MASKED = -1e30
F32 = jnp.float32
BF16 = jnp.bfloat16
BLOCKS = 4
COPIES = 320
IN_RANGES = ((0, 768, False),)
DOWN_RANGES = ((0, 384, True), (384, 768, False))
IN_SUMS = ((0, 768, False),)
DOWN_SUMS = ((0, 384, True), (384, 768, False))
QO_TURN = False
ORDER = (
    "A0A1B0A2B1A3X5B2B3X2X6C0D0C1D1C2D2P0C3P1E0D3P2E1P3",
    "E2F0E3G0F1H0F2G1G2H1I0F3H2G3X0I1H3X3I2I3X4X1",
)


def nt(left, right):
    return lax.dot_general(left, right, (((1,), (1,)), ((), ())), preferred_element_type=F32)


def nn(left, right):
    return lax.dot_general(left, right, (((1,), (0,)), ((), ())), preferred_element_type=F32)


def gelu_and_slope(pre):
    scale = 0.7978845608028654
    cube = 0.044715
    square = pre * pre
    tanh = jnp.tanh(scale * pre * (1.0 + cube * square))
    half = 0.5 * (1.0 + tanh)
    slope = half + 0.5 * pre * (1.0 - tanh * tanh) * (scale * (1.0 + 3.0 * cube * square))
    return pre * half, slope


def column_sum(rows):
    return jnp.sum(rows, axis=0, keepdims=True)


def norm_forward(rows):
    mean = jnp.mean(rows, axis=-1, keepdims=True)
    centred = rows - mean
    spread = jnp.mean(centred * centred, axis=-1, keepdims=True)
    inverse = lax.rsqrt(spread + EPS)
    return centred * inverse, inverse


def norm_backward(grad, unit, inverse, gain):
    scaled = grad * gain
    first = jnp.mean(scaled, axis=-1, keepdims=True)
    second = jnp.mean(scaled * unit, axis=-1, keepdims=True)
    return inverse * (scaled - first - unit * second)


class Net:
    def __init__(self, send_sems, recv_sems):
        self.send_sems, self.recv_sems, self.copies = send_sems, recv_sems, []

    def send(self, source, target, where, when=None, place=None):
        number = len(self.copies)
        copy = pltpu.make_async_remote_copy(
            src_ref=source,
            dst_ref=target,
            send_sem=self.send_sems.at[number],
            recv_sem=self.recv_sems.at[number if place is None else place],
            device_id=where,
            device_id_type=pl.DeviceIdType.MESH,
        )
        self.copies.append((copy, when))
        if when is None:
            copy.start()
        else:
            pl.when(when)(copy.start)
        copy.number = number
        return copy

    def finish(self):
        for copy, when in self.copies:
            if when is None:
                copy.wait_send()
            else:
                pl.when(when)(copy.wait_send)


def layer_kernel(dims, *refs):
    shards, ctxs, wctx, piece, width, chunk, heads = dims
    rows_b = piece // BLOCKS
    half = rows_b // 2
    cols = heads * HEAD_DIM
    (x_ref, cot_ref, qkv_ref, out_ref, wi_ref, wd_ref, seg_ref, valid_ref, qv_bias_ref, out_bias_ref, gain1_ref,
     shift1_ref, in_bias_ref, down_bias_ref, gain2_ref, shift2_ref,
     lo_ref, tg_ref, ga_ref, gi_ref, gd_ref, small_ref,
     wa, wi, wd, xt, yt, xs, code_all, bias, kv, kvt, qm, sbuf, pt, pt_r, ott, mt, vcol, cot,
     hid, act, slope, dffn, dpre, datt, datt_r, lobuf, tgbuf,
     part, near_in, far_out, far_in, gown, gxs, gxr, gzs, gzr, dkv0, dqt, dproj, dqp, ctxp, dom0, dom1,
     unit1, hidden, resid, sa, sb,
     sa1, sac, sas, sbc, sbs,
     qkv_own, out_own, code_ref, vec_ref, stat, stat_in, delta, delta_in,
     local_sems, send_sems, recv_sems) = refs
    me_s, me_c, me_t = lax.axis_index("shard"), lax.axis_index("ctx"), lax.axis_index("tp")
    mine = me_t % 2
    other = 1 - mine
    near = {"tp": me_t + 1 - 2 * mine}
    far = {"tp": (me_t + 2) % TP}
    wc = me_c if wctx > 1 else 0
    net = Net(send_sems, recv_sems)

    def shard_at(step):
        return (me_s + step) % shards

    def ctx_at(step):
        return (me_c + step) % ctxs

    line = shards == 4
    steps = [2, 1, 3] if line else list(range(1, shards))
    side = me_s // 2
    is_hub = (me_s + side) % 2 == 1
    partner, other_hub, other_end = me_s + 1 - 2 * (me_s % 2), 2 - side, 3 - 3 * side

    barrier = pltpu.get_barrier_semaphore()
    local = {}

    def fetch(name, source, target):
        local[name] = pltpu.make_async_copy(source, target, local_sems.at[len(local)])
        local[name].start()

    own_a, own_i, own_d = wa.at[me_s, wc], wi.at[me_s, wc], wd.at[me_s, wc]
    if wctx < ctxs:
        fetch("qkv", qkv_ref, own_a)
    else:
        fetch("qkv", qkv_ref, qkv_own)
        fetch("out", out_ref, out_own)
    fetch("x", x_ref, xs.at[0])
    fetch("wi", wi_ref, own_i)
    fetch("wd", wd_ref, own_d)
    peers = [near, far]
    peers += [{"ctx": ctx_at(e)} for e in range(1, ctxs)]
    peers += [{"shard": shard_at(d)} for d in range(1, shards)]
    for peer in peers:
        pl.semaphore_signal(barrier, inc=1, device_id=peer, device_id_type=pl.DeviceIdType.MESH)
    local["qkv"].wait()
    if wctx == ctxs:
        local["out"].wait()
        wa[me_s, wc, :, 0:cols] = qkv_own[1]
        wa[me_s, wc, :, cols:2 * cols] = qkv_own[2]
        wa[me_s, wc, :, 2 * cols:3 * cols] = qkv_own[0]
        wa[me_s, wc, :, 3 * cols:] = jnp.transpose(out_own[...].astype(F32)).astype(BF16)
    local["x"].wait()
    pl.semaphore_wait(barrier, len(peers))

    class Gather:
        def __init__(self, buf, lo, hi, turn=False):
            self.buf, self.span, self.turn = buf, slice(lo, hi), turn and wctx > 1
            self.along, self.across = {}, []

        def piece(self, s, c):
            return self.buf.at[s, c, :, self.span]

        def send_along(self, c):
            reach = {1: me_s != 3, 3: me_s != 0} if line else {}
            own = self.piece(me_s, {"own": wc, "peer": 1 - wc}.get(c, 0))
            for d in steps:
                self.along[c, d] = net.send(own, own, {"shard": shard_at(d)}, reach.get(d))

        def send_across(self, s):
            if wctx > 1:
                piece = self.piece(s, wc)
                self.across.append(net.send(piece, piece, {"ctx": ctx_at(1)}))

        def start(self):
            self.send_along(0 if wctx == 1 else "own")

        def start_across(self):
            self.send_across(me_s)

        def second(self):
            if self.turn:
                self.across[0].wait_recv()
                self.send_along("peer")

        def arrive(self, name, d):
            c = {"own": wc, "peer": 1 - wc}.get(name, 0)
            self.along[name, d].wait_recv()
            s = shard_at(shards - d)
            if line and d == 2:
                piece = self.piece(s, c)
                net.send(piece, piece, {"shard": 3}, me_s == 2, self.along[name, 3].number)
                net.send(piece, piece, {"shard": 0}, me_s == 1, self.along[name, 1].number)
            if name == "own" and not self.turn:
                self.send_across(s)

        def middle(self):
            if line:
                for name, d in list(self.along):
                    if d == 2:
                        self.arrive(name, d)

        def rest(self):
            for name, d in list(self.along):
                if d != 2 or not line:
                    self.arrive(name, d)

        def wait(self):
            for copy in self.across[1 if self.turn else 0:]:
                copy.wait_recv()

    def wait_all(copies):
        for copy in copies:
            copy.wait_recv()

    def whole(buf, lo, hi):
        return buf[:, :, :, lo:hi].reshape(width, hi - lo)

    def sum_start(k, b, value):
        part[k, b] = value.reshape(2, half, width)
        return net.send(part.at[k, b, other], near_in.at[k, b], near)

    def sum_pass(k, b, copy):
        copy.wait_recv()
        far_out[k, b] = (part[k, b, mine] + near_in[k, b]).astype(BF16)
        return net.send(far_out.at[k, b], far_in.at[k, b], far)

    def sum_end(k, b, copy):
        copy.wait_recv()
        return far_out[k, b].astype(F32) + far_in[k, b].astype(F32)

    def share(buf, b, value):
        buf[b, mine] = value
        return net.send(buf.at[b, mine], buf.at[b, mine], near)

    def block(b):
        return slice(b * rows_b, (b + 1) * rows_b)

    def own_rows(b):
        return pl.ds(pl.multiple_of(b * rows_b + mine * half, half), half)

    roles = [other_end, other_hub, partner, me_s] if line else [shard_at(d) for d in range(1, shards)] + [me_s]

    class Sums:
        def __init__(self, k, lo, hi, turn=False):
            self.k, self.span, self.turn = k, slice(lo, hi), turn and wctx > 1
            self.across, self.copies = {}, {}

        def term(self, s, c):
            if c:
                return gxs[self.k, s, :, self.span].astype(F32)
            total = gown[self.k, s, :, self.span]
            if wctx > 1 and not self.turn:
                total = total + gxr[self.k, s, :, self.span].astype(F32)
            return total

        def out_slot(self, c, r):
            return gzs.at[c, self.k, r, :, self.span]

        def in_slot(self, c, r):
            return gzr.at[c, self.k, r, :, self.span]

        def passes(self):
            return (1, 0) if self.turn else (0,)

        def start(self, which=None):
            if wctx == 1 or self.turn:
                return
            for r in range(shards) if which is None else which:
                s = roles[r]
                self.across[r] = net.send(
                    gxs.at[self.k, s, :, self.span], gxr.at[self.k, s, :, self.span], {"ctx": ctx_at(1)}
                )

        def along(self):
            outer = jnp.logical_not(is_hub)
            for r in range(shards - 1):
                if r in self.across:
                    self.across[r].wait_recv()
                for c in self.passes():
                    if line and r < 2:

                        @pl.when(outer)
                        def _():
                            gzs[c, self.k, r, :, self.span] = self.term(roles[r], c).astype(BF16)

                        self.copies[c, r] = net.send(
                            self.out_slot(c, r), self.in_slot(c, r), {"shard": partner}, outer
                        )
                    else:
                        gzs[c, self.k, r, :, self.span] = self.term(roles[r], c).astype(BF16)
                        self.copies[c, r] = net.send(
                            self.out_slot(c, r), self.in_slot(c, r), {"shard": roles[r]}
                        )

        def merge(self):
            if not line:
                return
            for r in range(2):
                for c in self.passes():

                    @pl.when(is_hub)
                    def _():
                        self.copies[c, r].wait_recv()
                        total = self.term(roles[r], c) + gzr[c, self.k, r, :, self.span].astype(F32)
                        gzs[c, self.k, r, :, self.span] = total.astype(BF16)

                    place = self.copies[c, 3].number if r else None
                    copy = net.send(self.out_slot(c, r), self.in_slot(c, 3), {"shard": roles[r]}, is_hub, place)
                    if r == 0:
                        self.copies[c, 3] = copy

        def total(self, c):
            value = self.term(me_s, c)
            for r in (2, 3) if line else range(shards - 1):
                self.copies[c, r].wait_recv()
                value = value + gzr[c, self.k, r, :, self.span].astype(F32)
            return value

        def turned(self):
            if not self.turn:
                return
            gzs[1, self.k, 3, :, self.span] = self.total(1).astype(BF16)
            self.final = net.send(self.out_slot(1, 3), gxr.at[self.k, me_s, :, self.span], {"ctx": ctx_at(1)})

        def end(self, out_ref):
            if shards - 1 in self.across:
                self.across[shards - 1].wait_recv()
            value = self.total(0)
            if self.turn:
                self.final.wait_recv()
                value = value + gxr[self.k, me_s, :, self.span].astype(F32)
            out_ref[:, self.span] = value

    g_down = [Sums(2, *r) for r in DOWN_SUMS]
    g_in = [Sums(1, *r) for r in IN_SUMS]
    g_kv, g_qo = Sums(0, 0, 2 * cols), Sums(0, 2 * cols, width, QO_TURN)

    def each(items, name, *args):
        for item in items:
            getattr(item, name)(*args)

    def grad_product(k, lo, terms):
        for c in range(wctx - 1, -1, -1):
            where = (me_c + c) % wctx if wctx > 1 else 0
            value = 0.0
            for left, right in terms:
                value = value + nn(left[where].reshape(shards * chunk, piece), right)
            n = value.shape[1]
            value = value.reshape(shards, chunk, n)
            if c > 0:
                gxs[k, :, :, lo:lo + n] = value.astype(BF16)
            else:
                gown[k, :, :, lo:lo + n] = value

    def store_transposed(target, value):
        turned = jnp.transpose(value)
        for s in range(shards):
            for c in range(wctx):
                begin = (s * wctx + c) * chunk
                target[c, s] = turned[begin:begin + chunk]

    def exchange(buf, source, axis, at, count, me):
        buf[me] = source
        return [net.send(buf.at[me], buf.at[me], {axis: at(e)}) for e in range(1, count)]

    def exchange_end(buf, state, count):
        wait_all(state)
        total = buf[0]
        for i in range(1, count):
            total = total + buf[i]
        return total

    quarter = piece // TP

    def token_rows(t):
        return pl.ds(pl.multiple_of(t * quarter, quarter), quarter)

    me_rows, far_rows = token_rows(me_t), token_rows((me_t + 2) % TP)
    split = 2 * cols
    w_kv, w_qo = Gather(wa, 0, split), Gather(wa, split, width, True)
    w_in = [Gather(wi, *r) for r in IN_RANGES]
    w_down = [Gather(wd, *r) for r in DOWN_RANGES]
    w_kv.start()
    w_qo.start_across()
    token_in = [
        net.send(xs.at[0, me_rows], xs.at[e, me_rows], {"ctx": ctx_at(e)}) for e in range(1, ctxs)
    ]
    w_kv.start_across()
    w_qo.start()
    seg = seg_ref[...].astype(F32)
    real = valid_ref[...] == 1
    code_ref[...] = jnp.zeros_like(code_ref)
    code_ref[0:1] = jnp.where(real, seg, -1.0)
    code_ref[1:2] = seg
    code_ref[2:3] = jnp.where(real, 1.0, 0.0)
    code_sends = [net.send(code_ref, code_all.at[e], {"ctx": ctx_at(e)}) for e in range(1, ctxs)]
    code_all[0] = code_ref[...]
    for b in range(BLOCKS):
        fetch("cot%d" % b, cot_ref.at[own_rows(b)], cot.at[b])
    vec_ref[...] = jnp.zeros_like(vec_ref)
    vec_ref[0:1, 0:cols] = qv_bias_ref[0:1]
    vec_ref[1:2, cols:2 * cols] = qv_bias_ref[1:2]
    vcol[...] = jnp.transpose(jnp.broadcast_to(code_ref[2:3, :], (LANES, piece)))
    w_qo.second()
    w_kv.middle()
    token_far, token_near = [], []
    for e in range(1, ctxs):
        token_in[e - 1].wait_recv()
        token_far.append(net.send(xs.at[e, me_rows], xs.at[e, me_rows], far))
        token_near.append(net.send(xs.at[e, me_rows], xs.at[e, me_rows], near))

    def column_code(e):
        return jnp.transpose(jnp.broadcast_to(code_all[e][0:1, :], (LANES, piece)))[:, 0:1]

    def store_bias(e):
        allowed = column_code(e) == code_ref[1:2, :]
        if e == 0:
            rows = lax.broadcasted_iota(jnp.int32, (piece, piece), 0)
            lanes = lax.broadcasted_iota(jnp.int32, (piece, piece), 1)
            allowed = allowed | (rows == lanes)
        bias[e] = jnp.where(allowed, 0.0, MASKED)

    store_bias(0)
    w_kv.rest()
    w_qo.middle()
    local["wi"].wait()
    local["wd"].wait()
    for gather in w_in:
        gather.start()
    for e in range(1, ctxs):
        token_far[e - 1].wait_recv()
        token_near.append(net.send(xs.at[e, far_rows], xs.at[e, far_rows], near))
    for gather in w_in + w_down:
        gather.start_across()
    wait_all(code_sends)
    for e in range(1, ctxs):
        store_bias(e)
    w_kv.wait()

    x = xs[0]

    def project_kv(e):
        kv[e] = (nn(xs[e], whole(wa, 0, split)) + vec_ref[1:2, 0:split]).astype(BF16)
        kvt[e] = jnp.transpose(kv[e])

    lane = lax.broadcasted_iota(jnp.int32, (piece, 256), 1)

    def project_q(e):
        low = (nn(xs[e], whole(wa, split, split + 256)) + vec_ref[0:1, 0:256]).astype(BF16).astype(F32) * 0.125
        for h in range(heads):
            inside = (lane >= h * HEAD_DIM) & (lane < (h + 1) * HEAD_DIM)
            qm[e, h] = jnp.where(inside, low, 0.0).astype(BF16)

    project_kv(0)
    w_qo.rest()
    for gather in w_down:
        gather.start()
    w_qo.wait()
    project_q(0)
    wait_all(token_near)
    for e in range(1, ctxs):
        project_kv(e)
    for gather in w_in:
        gather.middle()

    ott[0:cols] = jnp.zeros((cols, piece), F32)
    mt[0:cols] = jnp.zeros((cols, piece), F32)
    stat[...] = jnp.zeros_like(stat)
    delta[...] = jnp.zeros_like(delta)
    for h in range(heads):
        top = None
        for e in range(ctxs):
            s = nt(kv[e][:, 0:256], qm[0, h]) + bias[e]
            sbuf[e] = s
            high = jnp.max(s, axis=0, keepdims=True)
            top = high if top is None else jnp.maximum(top, high)
        rows = slice(cols + h * HEAD_DIM, cols + (h + 1) * HEAD_DIM)
        total = jnp.zeros((1, piece), F32)
        mixed = jnp.zeros((HEAD_DIM, piece), F32)
        for e in range(ctxs):
            weights = jnp.exp(sbuf[e] - top)
            total = total + column_sum(weights)
            low = weights.astype(BF16)
            pt[h, e] = low
            mixed = mixed + nn(kvt[e, rows], low)
        inverse = 1.0 / total
        ott[rows] = mixed * inverse
        mt[rows] = jnp.broadcast_to(inverse, (HEAD_DIM, piece))
        stat[h:h + 1] = top
        stat[4 + h:5 + h] = inverse
        if h == 0:
            for gather in w_in:
                gather.second()
        if h == 1:
            for gather in w_down:
                gather.second()
    stat_sends = [net.send(stat, stat_in.at[e - 1], {"ctx": ctx_at(e)}) for e in range(1, ctxs)]
    ctxp[...] = jnp.transpose(ott[...]).astype(BF16)
    for gather in w_in:
        gather.rest()

    out_bias, gain1, shift1, in_bias = (
        ref[...].reshape(1, -1) for ref in (out_bias_ref, gain1_ref, shift1_ref, in_bias_ref)
    )
    down_bias, gain2, shift2 = (ref[...].reshape(1, -1) for ref in (down_bias_ref, gain2_ref, shift2_ref))
    sa[...] = jnp.zeros_like(sa)
    near_copy, far_copy, share_copy, inverse1, out_copy = {}, {}, {}, {}, {}

    def add_sum(row, value):
        sa[row:row + 1] = sa[row:row + 1] + column_sum(value)

    def stage_a(b):
        near_copy[0, b] = sum_start(0, b, nt(ctxp[block(b)], whole(wa, split, width)))

    def stage_b(b):
        far_copy[0, b] = sum_pass(0, b, near_copy[0, b])

    def stage_c(b):
        attn = sum_end(0, b, far_copy[0, b]) + out_bias
        x_own = xs[0, own_rows(b)].astype(F32)
        valid = vcol[own_rows(b), 0:1]
        unit, inverse1[b] = norm_forward(x_own + attn)
        unit1[b] = unit
        own_hidden = unit * gain1 + shift1
        hidden[b] = own_hidden
        share_copy[0, b] = share(hid, b, own_hidden.astype(BF16))
        add_sum(6, valid * x_own * x_own)
        add_sum(7, valid * attn * attn)
        sa[9:10] = sa[9:10] + column_sum(valid)

    def stage_d(b):
        if b == 0:
            for gather in w_in:
                gather.wait()
        share_copy[0, b].wait_recv()
        pre = nn(hid[b].reshape(rows_b, width), whole(wi, 0, width)) + in_bias
        value, slope[b] = gelu_and_slope(pre)
        act[b] = value.astype(BF16)

    def stage_p(b):
        if b == 0:
            for gather in w_down:
                gather.wait()
        near_copy[1, b] = sum_start(1, b, nt(act[b], whole(wd, 0, width)))

    def stage_e(b):
        far_copy[1, b] = sum_pass(1, b, near_copy[1, b])

    def stage_f(b):
        local["cot%d" % b].wait()
        ffn = sum_end(1, b, far_copy[1, b]) + down_bias
        valid = vcol[own_rows(b), 0:1]
        unit, inverse = norm_forward(hidden[b] + ffn)
        grad = cot[b]
        d_resid2 = norm_backward(grad, unit, inverse, gain2)
        low = d_resid2.astype(BF16)
        share_copy[1, b] = share(dffn, b, low)
        resid[b] = d_resid2
        out_copy[b] = share(lobuf, b, (unit * gain2 + shift2).astype(BF16))
        add_sum(8, valid * ffn * ffn)
        add_sum(3, low.astype(F32))
        add_sum(4, grad * unit)
        add_sum(5, grad)

    def stage_g(b):
        share_copy[1, b].wait_recv()
        d_act = nn(dffn[b].reshape(rows_b, width), whole(wd, 0, width))
        dpre[b] = (d_act * slope[b]).astype(BF16)
        near_copy[2, b] = sum_start(2, b, nt(dpre[b], whole(wi, 0, width)))

    def stage_h(b):
        far_copy[2, b] = sum_pass(2, b, near_copy[2, b])

    def stage_i(b):
        d_hidden = resid[b] + sum_end(2, b, far_copy[2, b])
        unit = unit1[b]
        d_resid1 = norm_backward(d_hidden, unit, inverse1[b], gain1)
        low = d_resid1.astype(BF16)
        share_copy[2, b] = share(datt, b, low)
        resid[b] = d_resid1
        add_sum(0, low.astype(F32))
        add_sum(1, d_hidden * unit)
        add_sum(2, d_hidden)

    stages = dict(A=stage_a, B=stage_b, C=stage_c, D=stage_d, E=stage_e, P=stage_p, F=stage_f, G=stage_g, H=stage_h, I=stage_i)

    def down_grads():
        store_transposed(yt, dffn[...].reshape(piece, width))
        grad_product(2, 0, [(yt, act[...].reshape(piece, width))])
        each(g_down, "start", (0, 1))
        for item in g_down:
            if item.turn:
                item.along()

    def in_grads():
        each(g_down, "start", range(2, shards))
        store_transposed(yt, hid[...].reshape(piece, width))
        grad_product(1, 0, [(yt, dpre[...].reshape(piece, width))])
        each(g_in, "start")
        for item in g_in:
            if item.turn:
                item.along()

    def remote_probs():
        store_transposed(xt, x)
        for e in range(1, ctxs):
            project_q(e)
            bias[e] = jnp.where(column_code(0) == code_all[e][1:2, :], 0.0, MASKED)
            stat_sends[e - 1].wait_recv()
            for h in range(heads):
                s = nt(kv[0][:, 0:256], qm[e, h]) + bias[e]
                pt_r[h, e - 1] = jnp.exp(s - stat_in[e - 1, h:h + 1]).astype(BF16)

    cross = {}

    def cross_send(j):
        b = 2 * j + me_t // 2
        for e in range(1, ctxs):
            cross[j, e] = net.send(datt.at[b, mine], datt_r.at[e - 1, b, mine], {"ctx": ctx_at(e)})

    def cross_pass(j):
        b = 2 * j + me_t // 2
        for e in range(1, ctxs):
            cross[j, e].wait_recv()
            source = datt_r.at[e - 1, b, mine]
            cross[j, e, "far"] = net.send(source, source, far)
            cross[j, e, "near"] = net.send(source, source, near)

    def cross_last(j):
        b = 2 * j + (me_t // 2 + 1) % 2
        for e in range(1, ctxs):
            cross[j, e, "far"].wait_recv()
            source = datt_r.at[e - 1, b, mine]
            cross[j, e, "last"] = net.send(source, source, near)

    def down_middle():
        for gather in w_down:
            gather.middle()

    def down_rest():
        for gather in w_down:
            gather.rest()

    extras = (down_grads, in_grads, remote_probs, lambda: cross_send(0), lambda: cross_send(1), down_middle, down_rest)
    for name in ORDER:
        for i in range(0, len(name), 2):
            if name[i] == "X":
                extras[int(name[i + 1])]()
            else:
                stages[name[i]](int(name[i + 1]))

    sb[...] = jnp.zeros_like(sb)
    sb[0:1] = column_sum(dpre[...].reshape(piece, width).astype(F32))
    sa_near = net.send(sa, sa1, near)
    for b in range(BLOCKS):
        share_copy[2, b].wait_recv()
    lane = lax.broadcasted_iota(jnp.int32, (piece, LANES), 1)

    def mixed_gradient(e, d_att, scale):
        d_mix = nn(d_att, whole(wa, split, width)).astype(BF16).astype(F32) * jnp.transpose(scale)
        dom0[e] = d_mix[:, 0:256].astype(BF16)
        last = d_mix[:, 256:384]
        dom1[e, 0] = jnp.where(lane < HEAD_DIM, last, 0.0).astype(BF16)
        dom1[e, 1] = jnp.where(lane >= HEAD_DIM, last, 0.0).astype(BF16)
        return d_mix

    d_att_all = datt[...].reshape(piece, width)
    d_mix = mixed_gradient(0, d_att_all, mt[...])
    product = jnp.transpose(d_mix)[cols:] * ott[cols:]
    for h in range(heads):
        delta[h:h + 1] = column_sum(product[h * HEAD_DIM:(h + 1) * HEAD_DIM])
    for item in g_down:
        if item.turn:
            item.merge()
        else:
            item.along()
    delta_sends = [net.send(delta, delta_in.at[e - 1], {"ctx": ctx_at(e)}) for e in range(1, ctxs)]
    cross_pass(0)

    def score_gradient(h, keys, queries, probs, deltas):
        if h == 0:
            d_probs = nt(kv[keys][:, 0:256], dom0[queries])
        else:
            d_probs = nt(kv[keys][:, 256:384], dom1[queries, h - 1])
        return (probs.astype(F32) * (d_probs - deltas)).astype(BF16)

    def key_gradient(h, queries, probs, d_scores):
        first = nn(d_scores, qm[queries, h])
        if h == 0:
            dkv0[:, 0:256] = dkv0[:, 0:256] + first + nn(probs, dom0[queries])
        else:
            dkv0[:, 0:256] = dkv0[:, 0:256] + first
            dkv0[:, 256:384] = dkv0[:, 256:384] + nn(probs, dom1[queries, h - 1])

    dkv0[...] = jnp.zeros_like(dkv0)
    dqt[...] = jnp.zeros((2 * cols, piece), F32)
    for e in range(ctxs):
        for h in range(heads):
            d_scores = score_gradient(h, e, 0, pt[h, e], delta[h:h + 1])
            rows = slice(h * HEAD_DIM, (h + 1) * HEAD_DIM)
            dqt[rows] = dqt[rows] + nn(kvt[e, rows], d_scores)
            if e == 0:
                key_gradient(h, 0, pt[h, 0], d_scores)
        if e == 0:
            cross_pass(1)
            cross_last(0)
            for item in g_down:
                if item.turn:
                    item.turned()
                else:
                    item.merge()
    sa_near.wait_recv()
    sa_c = exchange(sac, sa[...] + sa1[...], "ctx", ctx_at, ctxs, me_c)
    cross_last(1)
    dqp[...] = jnp.transpose(dqt[...] * 0.125).astype(BF16)
    store_transposed(yt, d_att_all)
    grad_product(0, split, [(xt, dqp[...]), (yt, ctxp[...])])
    g_qo.start()
    if g_qo.turn:
        g_qo.along()
    sa_s = exchange(sas, exchange_end(sac, sa_c, ctxs), "shard", shard_at, shards, me_s)
    for e in range(1, ctxs):
        for j in range(BLOCKS // 2):
            cross[j, e, "near"].wait_recv()
            cross[j, e, "last"].wait_recv()
        delta_sends[e - 1].wait_recv()
        for h in range(heads):
            rows = slice(cols + h * HEAD_DIM, cols + (h + 1) * HEAD_DIM)
            mt[rows] = jnp.broadcast_to(stat_in[e - 1, 4 + h:5 + h], (HEAD_DIM, piece))
        mixed_gradient(e, datt_r[e - 1].reshape(piece, width), mt[...])
        for h in range(heads):
            probs = pt_r[h, e - 1]
            d_scores = score_gradient(h, 0, e, probs, delta_in[e - 1, h:h + 1])
            key_gradient(h, e, probs, d_scores)
    for item in g_in:
        if item.turn:
            item.merge()
        else:
            item.along()
    dproj[...] = dkv0[...].astype(BF16)

    def back_tokens(b):
        value = nt(dproj[block(b)], whole(wa, 0, split))
        return value + nt(dqp[block(b), 0:256], whole(wa, split, split + 256))

    for b in range(2):
        near_copy[3, b] = sum_start(3, b, back_tokens(b))
    far_copy[3, 0] = sum_pass(3, 0, near_copy[3, 0])
    grad_product(0, 0, [(xt, dproj[...])])
    g_kv.start()
    far_copy[3, 1] = sum_pass(3, 1, near_copy[3, 1])
    for b in range(2, BLOCKS):
        near_copy[3, b] = sum_start(3, b, back_tokens(b))
    for b in range(2, BLOCKS):
        far_copy[3, b] = sum_pass(3, b, near_copy[3, b])
    sb[1:2, 0:split] = column_sum(dproj[...].astype(F32))
    sb[2:3, 0:split] = column_sum(dqp[...].astype(F32))
    sb_c = exchange(sbc, sb[...], "ctx", ctx_at, ctxs, me_c)
    for item in g_in:
        if item.turn:
            item.turned()
        else:
            item.merge()
    if g_qo.turn:
        g_qo.merge()
    else:
        g_qo.along()
    for b in range(BLOCKS):
        share_copy[3, b] = share(tgbuf, b, (resid[b] + sum_end(3, b, far_copy[3, b])).astype(BF16))
    sb_s = exchange(sbs, exchange_end(sbc, sb_c, ctxs), "shard", shard_at, shards, me_s)
    g_kv.along()
    if g_qo.turn:
        g_qo.turned()
    else:
        g_qo.merge()
    each(g_down, "end", gd_ref)
    for b in range(BLOCKS):
        out_copy[b].wait_recv()
        lo_ref[b] = lobuf[b].reshape(rows_b, width)
    small_ref[0:16] = exchange_end(sas, sa_s, shards)
    g_kv.merge()
    each(g_in, "end", gi_ref)
    for b in range(BLOCKS):
        share_copy[3, b].wait_recv()
        tg_ref[b] = tgbuf[b].reshape(rows_b, width)
    small_ref[16:24] = exchange_end(sbs, sb_s, shards)
    g_qo.end(ga_ref)
    g_kv.end(ga_ref)
    net.finish()


def run_layer(dims, copies, *operands):
    shards, ctxs, wctx, piece, width, chunk, heads = dims
    rows_b = piece // BLOCKS
    half = rows_b // 2
    cols = heads * HEAD_DIM
    hidden_cols = operands[4].shape[1]
    vmem = pl.BlockSpec(memory_space=pltpu.VMEM)
    weights = (shards, wctx, chunk, width)
    turned = (wctx, shards, chunk, piece)
    V = pltpu.VMEM
    shared = (BLOCKS, 2, half, width)
    hidden = (BLOCKS, rows_b, hidden_cols)
    scratch = [
        V(weights, BF16), V(weights, BF16), V(weights, BF16),
        V(turned, BF16), V(turned, BF16),
        V((ctxs, piece, width), BF16),
        V((ctxs, 8, piece), F32), V((ctxs, piece, piece), F32),
        V((ctxs, piece, 2 * cols), BF16), V((ctxs, 2 * cols, piece), BF16), V((ctxs, heads, piece, 256), BF16),
        V((ctxs, piece, piece), F32), V((heads, ctxs, piece, piece), BF16), V((heads, ctxs - 1, piece, piece), BF16),
        V((2 * cols, piece), F32), V((2 * cols, piece), F32), V((piece, LANES), F32), V((BLOCKS, half, width), F32),
        V(shared, BF16), V(hidden, BF16), V(hidden, F32),
        V(shared, BF16), V(hidden, BF16), V(shared, BF16), V((ctxs - 1,) + shared, BF16), V(shared, BF16),
        V(shared, BF16),
        V((4, BLOCKS, 2, half, width), F32), V((4, BLOCKS, half, width), F32),
        V((4, BLOCKS, half, width), BF16), V((4, BLOCKS, half, width), BF16),
        V((3, shards, chunk, width), F32), V((3, shards, chunk, width), BF16), V((3, shards, chunk, width), BF16),
        V((wctx, 3, shards, chunk, width), BF16), V((wctx, 3, shards, chunk, width), BF16),
        V((piece, 2 * cols), F32),
        V((2 * cols, piece), F32), V((piece, 2 * cols), BF16), V((piece, 2 * cols), BF16), V((piece, 2 * cols), BF16),
        V((ctxs, piece, 256), BF16), V((ctxs, 2, piece, LANES), BF16),
        V((BLOCKS, half, width), F32), V((BLOCKS, half, width), F32), V((BLOCKS, half, width), F32),
        V((16, width), F32), V((8, width), F32),
        V((16, width), F32), V((ctxs, 16, width), F32), V((shards, 16, width), F32),
        V((ctxs, 8, width), F32), V((shards, 8, width), F32),
        V((3, chunk, cols), BF16), V((cols, chunk), BF16), V((8, piece), F32), V((8, 2 * cols), F32),
        V((8, piece), F32), V((ctxs - 1, 8, piece), F32), V((8, piece), F32), V((ctxs - 1, 8, piece), F32),
        pltpu.SemaphoreType.DMA((BLOCKS + 5,)), pltpu.SemaphoreType.DMA((copies,)),
        pltpu.SemaphoreType.DMA((copies,)),
    ]
    return pl.pallas_call(
        functools.partial(layer_kernel, dims),
        out_shape=(
            jax.ShapeDtypeStruct((BLOCKS, rows_b, width), BF16),
            jax.ShapeDtypeStruct((BLOCKS, rows_b, width), BF16),
            jax.ShapeDtypeStruct((chunk, width), F32),
            jax.ShapeDtypeStruct((chunk, hidden_cols), F32),
            jax.ShapeDtypeStruct((chunk, hidden_cols), F32),
            jax.ShapeDtypeStruct((24, width), F32),
        ),
        in_specs=[pl.BlockSpec(memory_space=pl.ANY)] * 6 + [vmem] * (len(operands) - 6),
        out_specs=(vmem,) * 6,
        scratch_shapes=scratch,
        compiler_params=pltpu.CompilerParams(
            collective_id=0, has_side_effects=True, vmem_limit_bytes=67_043_328
        ),
        name="layer",
    )(*operands)


def finish_kernel(cols, *refs):
    (lo, tg, ga, gi, gd, small,
     lo_out, tg_out, qkv_out, qv_out, out_out, in_out, down_out, v0, v1, v2, v3, v4, v5, v6, rms_out) = refs
    lo_out[...] = lo[...]
    tg_out[...] = tg[...].astype(F32)
    qkv_out[0] = ga[:, 2 * cols:3 * cols]
    qkv_out[1] = ga[:, 0:cols]
    qkv_out[2] = ga[:, cols:2 * cols]
    out_out[...] = jnp.transpose(ga[:, 3 * cols:])
    in_out[...] = gi[...]
    down_out[...] = gd[...]
    qv_out[0:1] = small[18:19, 0:cols]
    qv_out[1:2] = small[17:18, cols:2 * cols]
    for row, ref in zip((0, 1, 2, 16, 3, 4, 5), (v0, v1, v2, v3, v4, v5, v6)):
        ref[...] = small[row]
    count = small[9:10, 0:1] * small.shape[1]
    for i in range(3):
        rms_out[0:1, i:i + 1] = jnp.sqrt(jnp.sum(small[6 + i:7 + i], axis=1, keepdims=True) / count)


def run_finish(cols, *operands):
    _, rows_b, width = operands[0].shape
    chunk, hidden_cols = operands[3].shape
    shapes = [
        ((BLOCKS, rows_b, width), BF16), ((BLOCKS, rows_b, width), F32), ((3, chunk, cols), F32), ((2, cols), F32),
        ((cols, chunk), F32), ((chunk, hidden_cols), F32), ((chunk, hidden_cols), F32),
        ((width,), F32), ((width,), F32), ((width,), F32), ((hidden_cols,), F32),
        ((width,), F32), ((width,), F32), ((width,), F32), ((1, 3), F32),
    ]
    vmem = pl.BlockSpec(memory_space=pltpu.VMEM)
    return pl.pallas_call(
        functools.partial(finish_kernel, cols),
        out_shape=tuple(jax.ShapeDtypeStruct(*shape) for shape in shapes),
        in_specs=[vmem] * len(operands),
        out_specs=(vmem,) * len(shapes),
        name="finish",
    )(*operands)


def body(
    sizes,
    tokens, segment_ids, valid_mask, qkv_weight, qv_bias, out_weight, out_bias, norm1_gain, norm1_shift,
    in_weight, in_bias, down_weight, down_bias, norm2_gain, norm2_shift, out_cotangent,
):
    shards, ctxs = sizes
    _, piece, width = tokens.shape
    cols = qkv_weight.shape[2]
    heads = cols // HEAD_DIM
    raw = qkv_weight.shape[1] % 16 == 0 and ctxs <= 2
    if raw:
        wctx = ctxs
        parts = [qkv_weight, out_weight, in_weight, down_weight.T]
        chunk = in_weight.shape[0]
    else:
        wctx = 1
        own = jnp.concatenate([qkv_weight[1], qkv_weight[2], qkv_weight[0], out_weight.T], axis=1)
        own, into, down = (
            lax.all_gather(part, "ctx", axis=0, tiled=True) for part in (own, in_weight, down_weight.T)
        )
        parts = [own, out_weight, into, down]
        chunk = own.shape[0]
    dims = (shards, ctxs, wctx, piece, width, chunk, heads)
    vectors = [out_bias, norm1_gain, norm1_shift, in_bias, down_bias, norm2_gain, norm2_shift]
    results = run_layer(
        dims, COPIES, tokens.reshape(piece, width), out_cotangent.reshape(piece, width), *parts,
        segment_ids, valid_mask, qv_bias, *vectors
    )
    if raw:
        lo, tg, g_qkv, g_qv, g_out, g_in, g_down, *sums, rms = run_finish(cols, *results)
        return (
            lo.reshape(1, piece, width), tg.reshape(1, piece, width), g_qkv, g_qv, g_out, sums[0], sums[1], sums[2],
            g_in, sums[3], g_down.T, sums[4], sums[5], sums[6], rms.reshape(-1),
        )
    lo, tg, ga, gi, gd, small = results
    ga, gi, gd = (lax.psum_scatter(g, "ctx", scatter_dimension=0, tiled=True) for g in (ga, gi, gd))
    g_qkv = jnp.stack([ga[:, 2 * cols:3 * cols], ga[:, 0:cols], ga[:, cols:2 * cols]])
    sums = jnp.sum(small[6:9], axis=1)
    return (
        lo.reshape(1, piece, width),
        tg.reshape(1, piece, width).astype(F32),
        g_qkv,
        jnp.stack([small[18, 0:cols], small[17, cols:2 * cols]]),
        ga[:, 3 * cols:].T,
        small[0], small[1], small[2],
        gi,
        small[16],
        gd.T,
        small[3], small[4], small[5],
        jnp.sqrt(sums / (small[9, 0] * width)),
    )


def solution(mesh):
    sizes = (mesh.shape["shard"], mesh.shape["ctx"])
    return jax.shard_map(
        functools.partial(body, sizes),
        mesh=mesh,
        in_specs=(
            P("shard", "ctx", None), P("shard", "ctx"), P("shard", "ctx"),
            P(None, ("shard", "ctx"), "tp"), P(None, "tp"), P("tp", ("shard", "ctx")),
            P(), P(), P(),
            P(("shard", "ctx"), "tp"), P("tp"), P("tp", ("shard", "ctx")),
            P(), P(), P(),
            P("shard", "ctx", None),
        ),
        out_specs=(
            P("shard", "ctx", None), P("shard", "ctx", None),
            P(None, ("shard", "ctx"), "tp"), P(None, "tp"), P("tp", ("shard", "ctx")),
            P(), P(), P(),
            P(("shard", "ctx"), "tp"), P("tp"), P("tp", ("shard", "ctx")),
            P(), P(), P(), P(),
        ),
        check_vma=False,
    )
```

```python
import functools

import jax
import jax.numpy as jnp
from jax import lax
from jax.experimental import pallas as pl
from jax.experimental.pallas import tpu as pltpu
from jax.sharding import PartitionSpec as P

HEAD_DIM = 64
LANES = 128
TP = 4
EPS = 1e-12
MASKED = -1e30
F32 = jnp.float32
BF16 = jnp.bfloat16
BLOCKS = 4
COPIES = 320
IN_RANGES = ((0, 768, False),)
DOWN_RANGES = ((0, 384, True), (384, 768, False))
IN_SUMS = ((0, 384, True), (384, 768, False))
DOWN_SUMS = ((0, 384, True), (384, 768, False))
QO_TURN = False
QO_FIRST = False
ORDER = (
    "A0A1B0A2B1A3X5B2B3X2X6C0D0C1D1C2D2P0C3P1E0D3P2E1P3",
    "E2F0E3G0F1H0F2G1G2H1I0F3H2G3X0I1H3X3I2I3X4X1",
)


def nt(left, right):
    return lax.dot_general(left, right, (((1,), (1,)), ((), ())), preferred_element_type=F32)


def nn(left, right):
    return lax.dot_general(left, right, (((1,), (0,)), ((), ())), preferred_element_type=F32)


def gelu_and_slope(pre):
    scale = 0.7978845608028654
    cube = 0.044715
    square = pre * pre
    tanh = jnp.tanh(scale * pre * (1.0 + cube * square))
    half = 0.5 * (1.0 + tanh)
    slope = half + 0.5 * pre * (1.0 - tanh * tanh) * (scale * (1.0 + 3.0 * cube * square))
    return pre * half, slope


def column_sum(rows):
    return jnp.sum(rows, axis=0, keepdims=True)


def norm_forward(rows):
    mean = jnp.mean(rows, axis=-1, keepdims=True)
    centred = rows - mean
    spread = jnp.mean(centred * centred, axis=-1, keepdims=True)
    inverse = lax.rsqrt(spread + EPS)
    return centred * inverse, inverse


def norm_backward(grad, unit, inverse, gain):
    scaled = grad * gain
    first = jnp.mean(scaled, axis=-1, keepdims=True)
    second = jnp.mean(scaled * unit, axis=-1, keepdims=True)
    return inverse * (scaled - first - unit * second)


class Net:
    def __init__(self, send_sems, recv_sems):
        self.send_sems, self.recv_sems, self.copies = send_sems, recv_sems, []

    def send(self, source, target, where, when=None, place=None):
        number = len(self.copies)
        copy = pltpu.make_async_remote_copy(
            src_ref=source,
            dst_ref=target,
            send_sem=self.send_sems.at[number],
            recv_sem=self.recv_sems.at[number if place is None else place],
            device_id=where,
            device_id_type=pl.DeviceIdType.MESH,
        )
        self.copies.append((copy, when))
        if when is None:
            copy.start()
        else:
            pl.when(when)(copy.start)
        copy.number = number
        return copy

    def finish(self):
        for copy, when in self.copies:
            if when is None:
                copy.wait_send()
            else:
                pl.when(when)(copy.wait_send)


def layer_kernel(dims, *refs):
    shards, ctxs, wctx, piece, width, chunk, heads = dims
    rows_b = piece // BLOCKS
    half = rows_b // 2
    cols = heads * HEAD_DIM
    (x_ref, cot_ref, qkv_ref, out_ref, wi_ref, wd_ref, seg_ref, valid_ref, qv_bias_ref, out_bias_ref, gain1_ref,
     shift1_ref, in_bias_ref, down_bias_ref, gain2_ref, shift2_ref,
     lo_ref, tg_ref, ga_ref, gi_ref, gd_ref, small_ref,
     wa, wi, wd, xt, yt, xs, code_all, bias, kv, kvt, qm, sbuf, pt, pt_r, ott, mt, vcol, cot,
     hid, act, slope, dffn, dpre, datt, datt_r, lobuf, tgbuf,
     part, near_in, far_out, far_in, gown, gxs, gxr, gzs, gzr, dkv0, dqt, dproj, dqp, ctxp, dom0, dom1,
     unit1, hidden, resid, sa, sb,
     sa1, sac, sas, sbc, sbs,
     qkv_own, out_own, code_ref, vec_ref, stat, stat_in, delta, delta_in,
     local_sems, send_sems, recv_sems) = refs
    me_s, me_c, me_t = lax.axis_index("shard"), lax.axis_index("ctx"), lax.axis_index("tp")
    mine = me_t % 2
    other = 1 - mine
    near = {"tp": me_t + 1 - 2 * mine}
    far = {"tp": (me_t + 2) % TP}
    wc = me_c if wctx > 1 else 0
    net = Net(send_sems, recv_sems)

    def shard_at(step):
        return (me_s + step) % shards

    def ctx_at(step):
        return (me_c + step) % ctxs

    line = shards == 4
    steps = [2, 1, 3] if line else list(range(1, shards))
    side = me_s // 2
    is_hub = (me_s + side) % 2 == 1
    partner, other_hub, other_end = me_s + 1 - 2 * (me_s % 2), 2 - side, 3 - 3 * side

    barrier = pltpu.get_barrier_semaphore()
    local = {}

    def fetch(name, source, target):
        local[name] = pltpu.make_async_copy(source, target, local_sems.at[len(local)])
        local[name].start()

    own_a, own_i, own_d = wa.at[me_s, wc], wi.at[me_s, wc], wd.at[me_s, wc]
    if wctx < ctxs:
        fetch("qkv", qkv_ref, own_a)
    else:
        fetch("qkv", qkv_ref, qkv_own)
        fetch("out", out_ref, out_own)
    fetch("x", x_ref, xs.at[0])
    fetch("wi", wi_ref, own_i)
    fetch("wd", wd_ref, own_d)
    peers = [near, far]
    peers += [{"ctx": ctx_at(e)} for e in range(1, ctxs)]
    peers += [{"shard": shard_at(d)} for d in range(1, shards)]
    for peer in peers:
        pl.semaphore_signal(barrier, inc=1, device_id=peer, device_id_type=pl.DeviceIdType.MESH)
    local["qkv"].wait()
    if wctx == ctxs:
        local["out"].wait()
        wa[me_s, wc, :, 0:cols] = qkv_own[1]
        wa[me_s, wc, :, cols:2 * cols] = qkv_own[2]
        wa[me_s, wc, :, 2 * cols:3 * cols] = qkv_own[0]
        wa[me_s, wc, :, 3 * cols:] = jnp.transpose(out_own[...].astype(F32)).astype(BF16)
    local["x"].wait()
    pl.semaphore_wait(barrier, len(peers))

    class Gather:
        def __init__(self, buf, lo, hi, turn=False):
            self.buf, self.span, self.turn = buf, slice(lo, hi), turn and wctx > 1
            self.along, self.across = {}, []

        def piece(self, s, c):
            return self.buf.at[s, c, :, self.span]

        def send_along(self, c):
            reach = {1: me_s != 3, 3: me_s != 0} if line else {}
            own = self.piece(me_s, {"own": wc, "peer": 1 - wc}.get(c, 0))
            for d in steps:
                self.along[c, d] = net.send(own, own, {"shard": shard_at(d)}, reach.get(d))

        def send_across(self, s):
            if wctx > 1:
                piece = self.piece(s, wc)
                self.across.append(net.send(piece, piece, {"ctx": ctx_at(1)}))

        def start(self):
            self.send_along(0 if wctx == 1 else "own")

        def start_across(self):
            self.send_across(me_s)

        def second(self):
            if self.turn:
                self.across[0].wait_recv()
                self.send_along("peer")

        def arrive(self, name, d):
            c = {"own": wc, "peer": 1 - wc}.get(name, 0)
            self.along[name, d].wait_recv()
            s = shard_at(shards - d)
            if line and d == 2:
                piece = self.piece(s, c)
                net.send(piece, piece, {"shard": 3}, me_s == 2, self.along[name, 3].number)
                net.send(piece, piece, {"shard": 0}, me_s == 1, self.along[name, 1].number)
            if name == "own" and not self.turn:
                self.send_across(s)

        def middle(self):
            if line:
                for name, d in list(self.along):
                    if d == 2:
                        self.arrive(name, d)

        def rest(self):
            for name, d in list(self.along):
                if d != 2 or not line:
                    self.arrive(name, d)

        def wait(self):
            for copy in self.across[1 if self.turn else 0:]:
                copy.wait_recv()

    def wait_all(copies):
        for copy in copies:
            copy.wait_recv()

    def whole(buf, lo, hi):
        return buf[:, :, :, lo:hi].reshape(width, hi - lo)

    def sum_start(k, b, value):
        part[k, b] = value.reshape(2, half, width)
        return net.send(part.at[k, b, other], near_in.at[k, b], near)

    def sum_pass(k, b, copy):
        copy.wait_recv()
        far_out[k, b] = (part[k, b, mine] + near_in[k, b]).astype(BF16)
        return net.send(far_out.at[k, b], far_in.at[k, b], far)

    def sum_end(k, b, copy):
        copy.wait_recv()
        return far_out[k, b].astype(F32) + far_in[k, b].astype(F32)

    def share(buf, b, value):
        buf[b, mine] = value
        return net.send(buf.at[b, mine], buf.at[b, mine], near)

    def block(b):
        return slice(b * rows_b, (b + 1) * rows_b)

    def own_rows(b):
        return pl.ds(pl.multiple_of(b * rows_b + mine * half, half), half)

    roles = [other_end, other_hub, partner, me_s] if line else [shard_at(d) for d in range(1, shards)] + [me_s]

    class Sums:
        def __init__(self, k, lo, hi, turn=False):
            self.k, self.span, self.turn = k, slice(lo, hi), turn and wctx > 1
            self.across, self.copies = {}, {}

        def term(self, s, c):
            if c:
                return gxs[self.k, s, :, self.span].astype(F32)
            total = gown[self.k, s, :, self.span]
            if wctx > 1 and not self.turn:
                total = total + gxr[self.k, s, :, self.span].astype(F32)
            return total

        def out_slot(self, c, r):
            return gzs.at[c, self.k, r, :, self.span]

        def in_slot(self, c, r):
            return gzr.at[c, self.k, r, :, self.span]

        def passes(self):
            return (1, 0) if self.turn else (0,)

        def start(self, which=None):
            if wctx == 1 or self.turn:
                return
            for r in range(shards) if which is None else which:
                s = roles[r]
                self.across[r] = net.send(
                    gxs.at[self.k, s, :, self.span], gxr.at[self.k, s, :, self.span], {"ctx": ctx_at(1)}
                )

        def along(self):
            outer = jnp.logical_not(is_hub)
            for r in range(shards - 1):
                if r in self.across:
                    self.across[r].wait_recv()
                for c in self.passes():
                    if line and r < 2:

                        @pl.when(outer)
                        def _():
                            gzs[c, self.k, r, :, self.span] = self.term(roles[r], c).astype(BF16)

                        self.copies[c, r] = net.send(
                            self.out_slot(c, r), self.in_slot(c, r), {"shard": partner}, outer
                        )
                    else:
                        gzs[c, self.k, r, :, self.span] = self.term(roles[r], c).astype(BF16)
                        self.copies[c, r] = net.send(
                            self.out_slot(c, r), self.in_slot(c, r), {"shard": roles[r]}
                        )

        def merge(self):
            if not line:
                return
            for r in range(2):
                for c in self.passes():

                    @pl.when(is_hub)
                    def _():
                        self.copies[c, r].wait_recv()
                        total = self.term(roles[r], c) + gzr[c, self.k, r, :, self.span].astype(F32)
                        gzs[c, self.k, r, :, self.span] = total.astype(BF16)

                    place = self.copies[c, 3].number if r else None
                    copy = net.send(self.out_slot(c, r), self.in_slot(c, 3), {"shard": roles[r]}, is_hub, place)
                    if r == 0:
                        self.copies[c, 3] = copy

        def total(self, c):
            value = self.term(me_s, c)
            for r in (2, 3) if line else range(shards - 1):
                self.copies[c, r].wait_recv()
                value = value + gzr[c, self.k, r, :, self.span].astype(F32)
            return value

        def turned(self):
            if not self.turn:
                return
            gzs[1, self.k, 3, :, self.span] = self.total(1).astype(BF16)
            self.final = net.send(self.out_slot(1, 3), gxr.at[self.k, me_s, :, self.span], {"ctx": ctx_at(1)})

        def end(self, out_ref):
            if shards - 1 in self.across:
                self.across[shards - 1].wait_recv()
            value = self.total(0)
            if self.turn:
                self.final.wait_recv()
                value = value + gxr[self.k, me_s, :, self.span].astype(F32)
            out_ref[:, self.span] = value

    g_down = [Sums(2, *r) for r in DOWN_SUMS]
    g_in = [Sums(1, *r) for r in IN_SUMS]
    g_kv, g_qo = Sums(0, 0, 2 * cols), Sums(0, 2 * cols, width, QO_TURN)

    def each(items, name, *args):
        for item in items:
            getattr(item, name)(*args)

    def grad_product(k, lo, terms):
        for c in range(wctx - 1, -1, -1):
            where = (me_c + c) % wctx if wctx > 1 else 0
            value = 0.0
            for left, right in terms:
                value = value + nn(left[where].reshape(shards * chunk, piece), right)
            n = value.shape[1]
            value = value.reshape(shards, chunk, n)
            if c > 0:
                gxs[k, :, :, lo:lo + n] = value.astype(BF16)
            else:
                gown[k, :, :, lo:lo + n] = value

    def store_transposed(target, value):
        turned = jnp.transpose(value)
        for s in range(shards):
            for c in range(wctx):
                begin = (s * wctx + c) * chunk
                target[c, s] = turned[begin:begin + chunk]

    def exchange(buf, source, axis, at, count, me):
        buf[me] = source
        return [net.send(buf.at[me], buf.at[me], {axis: at(e)}) for e in range(1, count)]

    def exchange_end(buf, state, count):
        wait_all(state)
        total = buf[0]
        for i in range(1, count):
            total = total + buf[i]
        return total

    quarter = piece // TP

    def token_rows(t):
        return pl.ds(pl.multiple_of(t * quarter, quarter), quarter)

    me_rows, far_rows = token_rows(me_t), token_rows((me_t + 2) % TP)
    split = 2 * cols
    w_kv, w_qo = Gather(wa, 0, split), Gather(wa, split, width, QO_FIRST)
    w_in = [Gather(wi, *r) for r in IN_RANGES]
    w_down = [Gather(wd, *r) for r in DOWN_RANGES]
    w_kv.start()
    w_qo.start_across()
    token_in = [
        net.send(xs.at[0, me_rows], xs.at[e, me_rows], {"ctx": ctx_at(e)}) for e in range(1, ctxs)
    ]
    w_kv.start_across()
    w_qo.start()
    seg = seg_ref[...].astype(F32)
    real = valid_ref[...] == 1
    code_ref[...] = jnp.zeros_like(code_ref)
    code_ref[0:1] = jnp.where(real, seg, -1.0)
    code_ref[1:2] = seg
    code_ref[2:3] = jnp.where(real, 1.0, 0.0)
    code_sends = [net.send(code_ref, code_all.at[e], {"ctx": ctx_at(e)}) for e in range(1, ctxs)]
    code_all[0] = code_ref[...]
    for b in range(BLOCKS):
        fetch("cot%d" % b, cot_ref.at[own_rows(b)], cot.at[b])
    vec_ref[...] = jnp.zeros_like(vec_ref)
    vec_ref[0:1, 0:cols] = qv_bias_ref[0:1]
    vec_ref[1:2, cols:2 * cols] = qv_bias_ref[1:2]
    vcol[...] = jnp.transpose(jnp.broadcast_to(code_ref[2:3, :], (LANES, piece)))
    w_qo.second()
    w_kv.middle()
    token_far, token_near = [], []
    for e in range(1, ctxs):
        token_in[e - 1].wait_recv()
        token_far.append(net.send(xs.at[e, me_rows], xs.at[e, me_rows], far))
        token_near.append(net.send(xs.at[e, me_rows], xs.at[e, me_rows], near))

    def column_code(e):
        return jnp.transpose(jnp.broadcast_to(code_all[e][0:1, :], (LANES, piece)))[:, 0:1]

    def store_bias(e):
        allowed = column_code(e) == code_ref[1:2, :]
        if e == 0:
            rows = lax.broadcasted_iota(jnp.int32, (piece, piece), 0)
            lanes = lax.broadcasted_iota(jnp.int32, (piece, piece), 1)
            allowed = allowed | (rows == lanes)
        bias[e] = jnp.where(allowed, 0.0, MASKED)

    store_bias(0)
    w_kv.rest()
    w_qo.middle()
    local["wi"].wait()
    local["wd"].wait()
    for gather in w_in + w_down:
        gather.start()
    for e in range(1, ctxs):
        token_far[e - 1].wait_recv()
        token_near.append(net.send(xs.at[e, far_rows], xs.at[e, far_rows], near))
    for gather in w_in + w_down:
        gather.start_across()
    wait_all(code_sends)
    for e in range(1, ctxs):
        store_bias(e)
    w_kv.wait()

    x = xs[0]

    def project_kv(e):
        kv[e] = (nn(xs[e], whole(wa, 0, split)) + vec_ref[1:2, 0:split]).astype(BF16)
        kvt[e] = jnp.transpose(kv[e])

    lane = lax.broadcasted_iota(jnp.int32, (piece, 256), 1)

    def project_q(e):
        low = (nn(xs[e], whole(wa, split, split + 256)) + vec_ref[0:1, 0:256]).astype(BF16).astype(F32) * 0.125
        for h in range(heads):
            inside = (lane >= h * HEAD_DIM) & (lane < (h + 1) * HEAD_DIM)
            qm[e, h] = jnp.where(inside, low, 0.0).astype(BF16)

    project_kv(0)
    w_qo.rest()
    for gather in w_in + w_down:
        gather.second()
    for gather in w_in:
        gather.middle()
    w_qo.wait()
    project_q(0)
    wait_all(token_near)
    for e in range(1, ctxs):
        project_kv(e)
    for gather in w_in:
        gather.rest()

    ott[0:cols] = jnp.zeros((cols, piece), F32)
    mt[0:cols] = jnp.zeros((cols, piece), F32)
    stat[...] = jnp.zeros_like(stat)
    delta[...] = jnp.zeros_like(delta)
    for h in range(heads):
        top = None
        for e in range(ctxs):
            s = nt(kv[e][:, 0:256], qm[0, h]) + bias[e]
            sbuf[e] = s
            high = jnp.max(s, axis=0, keepdims=True)
            top = high if top is None else jnp.maximum(top, high)
        rows = slice(cols + h * HEAD_DIM, cols + (h + 1) * HEAD_DIM)
        total = jnp.zeros((1, piece), F32)
        mixed = jnp.zeros((HEAD_DIM, piece), F32)
        for e in range(ctxs):
            weights = jnp.exp(sbuf[e] - top)
            total = total + column_sum(weights)
            low = weights.astype(BF16)
            pt[h, e] = low
            mixed = mixed + nn(kvt[e, rows], low)
        inverse = 1.0 / total
        ott[rows] = mixed * inverse
        mt[rows] = jnp.broadcast_to(inverse, (HEAD_DIM, piece))
        stat[h:h + 1] = top
        stat[4 + h:5 + h] = inverse
    stat_sends = [net.send(stat, stat_in.at[e - 1], {"ctx": ctx_at(e)}) for e in range(1, ctxs)]
    ctxp[...] = jnp.transpose(ott[...]).astype(BF16)

    out_bias, gain1, shift1, in_bias = (
        ref[...].reshape(1, -1) for ref in (out_bias_ref, gain1_ref, shift1_ref, in_bias_ref)
    )
    down_bias, gain2, shift2 = (ref[...].reshape(1, -1) for ref in (down_bias_ref, gain2_ref, shift2_ref))
    sa[...] = jnp.zeros_like(sa)
    near_copy, far_copy, share_copy, inverse1, out_copy = {}, {}, {}, {}, {}

    def add_sum(row, value):
        sa[row:row + 1] = sa[row:row + 1] + column_sum(value)

    def stage_a(b):
        near_copy[0, b] = sum_start(0, b, nt(ctxp[block(b)], whole(wa, split, width)))

    def stage_b(b):
        far_copy[0, b] = sum_pass(0, b, near_copy[0, b])

    def stage_c(b):
        attn = sum_end(0, b, far_copy[0, b]) + out_bias
        x_own = xs[0, own_rows(b)].astype(F32)
        valid = vcol[own_rows(b), 0:1]
        unit, inverse1[b] = norm_forward(x_own + attn)
        unit1[b] = unit
        own_hidden = unit * gain1 + shift1
        hidden[b] = own_hidden
        share_copy[0, b] = share(hid, b, own_hidden.astype(BF16))
        add_sum(6, valid * x_own * x_own)
        add_sum(7, valid * attn * attn)
        sa[9:10] = sa[9:10] + column_sum(valid)

    def stage_d(b):
        if b == 0:
            for gather in w_in:
                gather.wait()
        share_copy[0, b].wait_recv()
        pre = nn(hid[b].reshape(rows_b, width), whole(wi, 0, width)) + in_bias
        value, slope[b] = gelu_and_slope(pre)
        act[b] = value.astype(BF16)

    def stage_p(b):
        if b == 0:
            for gather in w_down:
                gather.wait()
        near_copy[1, b] = sum_start(1, b, nt(act[b], whole(wd, 0, width)))

    def stage_e(b):
        far_copy[1, b] = sum_pass(1, b, near_copy[1, b])

    def stage_f(b):
        local["cot%d" % b].wait()
        ffn = sum_end(1, b, far_copy[1, b]) + down_bias
        valid = vcol[own_rows(b), 0:1]
        unit, inverse = norm_forward(hidden[b] + ffn)
        grad = cot[b]
        d_resid2 = norm_backward(grad, unit, inverse, gain2)
        low = d_resid2.astype(BF16)
        share_copy[1, b] = share(dffn, b, low)
        resid[b] = d_resid2
        out_copy[b] = share(lobuf, b, (unit * gain2 + shift2).astype(BF16))
        add_sum(8, valid * ffn * ffn)
        add_sum(3, low.astype(F32))
        add_sum(4, grad * unit)
        add_sum(5, grad)

    def stage_g(b):
        share_copy[1, b].wait_recv()
        d_act = nn(dffn[b].reshape(rows_b, width), whole(wd, 0, width))
        dpre[b] = (d_act * slope[b]).astype(BF16)
        near_copy[2, b] = sum_start(2, b, nt(dpre[b], whole(wi, 0, width)))

    def stage_h(b):
        far_copy[2, b] = sum_pass(2, b, near_copy[2, b])

    def stage_i(b):
        d_hidden = resid[b] + sum_end(2, b, far_copy[2, b])
        unit = unit1[b]
        d_resid1 = norm_backward(d_hidden, unit, inverse1[b], gain1)
        low = d_resid1.astype(BF16)
        share_copy[2, b] = share(datt, b, low)
        resid[b] = d_resid1
        add_sum(0, low.astype(F32))
        add_sum(1, d_hidden * unit)
        add_sum(2, d_hidden)

    stages = dict(A=stage_a, B=stage_b, C=stage_c, D=stage_d, E=stage_e, P=stage_p, F=stage_f, G=stage_g, H=stage_h, I=stage_i)

    def down_grads():
        store_transposed(yt, dffn[...].reshape(piece, width))
        grad_product(2, 0, [(yt, act[...].reshape(piece, width))])
        each(g_down, "start", (0, 1))
        for item in g_down:
            if item.turn:
                item.along()

    def in_grads():
        each(g_down, "start", range(2, shards))
        store_transposed(yt, hid[...].reshape(piece, width))
        grad_product(1, 0, [(yt, dpre[...].reshape(piece, width))])
        each(g_in, "start")
        for item in g_in:
            if item.turn:
                item.along()

    def remote_probs():
        store_transposed(xt, x)
        for e in range(1, ctxs):
            project_q(e)
            bias[e] = jnp.where(column_code(0) == code_all[e][1:2, :], 0.0, MASKED)
            stat_sends[e - 1].wait_recv()
            for h in range(heads):
                s = nt(kv[0][:, 0:256], qm[e, h]) + bias[e]
                pt_r[h, e - 1] = jnp.exp(s - stat_in[e - 1, h:h + 1]).astype(BF16)

    cross = {}

    def cross_send(j):
        b = 2 * j + me_t // 2
        for e in range(1, ctxs):
            cross[j, e] = net.send(datt.at[b, mine], datt_r.at[e - 1, b, mine], {"ctx": ctx_at(e)})

    def cross_pass(j):
        b = 2 * j + me_t // 2
        for e in range(1, ctxs):
            cross[j, e].wait_recv()
            source = datt_r.at[e - 1, b, mine]
            cross[j, e, "far"] = net.send(source, source, far)
            cross[j, e, "near"] = net.send(source, source, near)

    def cross_last(j):
        b = 2 * j + (me_t // 2 + 1) % 2
        for e in range(1, ctxs):
            cross[j, e, "far"].wait_recv()
            source = datt_r.at[e - 1, b, mine]
            cross[j, e, "last"] = net.send(source, source, near)

    def down_middle():
        for gather in w_down:
            gather.middle()

    def down_rest():
        for gather in w_down:
            gather.rest()

    extras = (down_grads, in_grads, remote_probs, lambda: cross_send(0), lambda: cross_send(1), down_middle, down_rest)
    for name in ORDER:
        for i in range(0, len(name), 2):
            if name[i] == "X":
                extras[int(name[i + 1])]()
            else:
                stages[name[i]](int(name[i + 1]))

    sb[...] = jnp.zeros_like(sb)
    sb[0:1] = column_sum(dpre[...].reshape(piece, width).astype(F32))
    sa_near = net.send(sa, sa1, near)
    for b in range(BLOCKS):
        share_copy[2, b].wait_recv()
    lane = lax.broadcasted_iota(jnp.int32, (piece, LANES), 1)

    def mixed_gradient(e, d_att, scale):
        d_mix = nn(d_att, whole(wa, split, width)).astype(BF16).astype(F32) * jnp.transpose(scale)
        dom0[e] = d_mix[:, 0:256].astype(BF16)
        last = d_mix[:, 256:384]
        dom1[e, 0] = jnp.where(lane < HEAD_DIM, last, 0.0).astype(BF16)
        dom1[e, 1] = jnp.where(lane >= HEAD_DIM, last, 0.0).astype(BF16)
        return d_mix

    d_att_all = datt[...].reshape(piece, width)
    d_mix = mixed_gradient(0, d_att_all, mt[...])
    product = jnp.transpose(d_mix)[cols:] * ott[cols:]
    for h in range(heads):
        delta[h:h + 1] = column_sum(product[h * HEAD_DIM:(h + 1) * HEAD_DIM])
    delta_sends = [net.send(delta, delta_in.at[e - 1], {"ctx": ctx_at(e)}) for e in range(1, ctxs)]
    cross_pass(0)
    for item in g_down:
        if item.turn:
            item.merge()

    def score_gradient(h, keys, queries, probs, deltas):
        if h == 0:
            d_probs = nt(kv[keys][:, 0:256], dom0[queries])
        else:
            d_probs = nt(kv[keys][:, 256:384], dom1[queries, h - 1])
        return (probs.astype(F32) * (d_probs - deltas)).astype(BF16)

    def key_gradient(h, queries, probs, d_scores):
        first = nn(d_scores, qm[queries, h])
        if h == 0:
            dkv0[:, 0:256] = dkv0[:, 0:256] + first + nn(probs, dom0[queries])
        else:
            dkv0[:, 0:256] = dkv0[:, 0:256] + first
            dkv0[:, 256:384] = dkv0[:, 256:384] + nn(probs, dom1[queries, h - 1])

    dkv0[...] = jnp.zeros_like(dkv0)
    dqt[...] = jnp.zeros((2 * cols, piece), F32)
    for e in range(ctxs):
        for h in range(heads):
            d_scores = score_gradient(h, e, 0, pt[h, e], delta[h:h + 1])
            rows = slice(h * HEAD_DIM, (h + 1) * HEAD_DIM)
            dqt[rows] = dqt[rows] + nn(kvt[e, rows], d_scores)
            if e == 0:
                key_gradient(h, 0, pt[h, 0], d_scores)
        if e == 0:
            cross_pass(1)
            cross_last(0)
            for item in g_down:
                if not item.turn:
                    item.along()
    sa_near.wait_recv()
    sa_c = exchange(sac, sa[...] + sa1[...], "ctx", ctx_at, ctxs, me_c)
    cross_last(1)
    each(g_down, "turned")
    for item in g_in:
        if item.turn:
            item.merge()
    dqp[...] = jnp.transpose(dqt[...] * 0.125).astype(BF16)
    store_transposed(yt, d_att_all)
    grad_product(0, split, [(xt, dqp[...]), (yt, ctxp[...])])
    g_qo.start()
    if g_qo.turn:
        g_qo.along()
    for item in g_down:
        if not item.turn:
            item.merge()
    sa_s = exchange(sas, exchange_end(sac, sa_c, ctxs), "shard", shard_at, shards, me_s)
    for e in range(1, ctxs):
        for j in range(BLOCKS // 2):
            cross[j, e, "near"].wait_recv()
            cross[j, e, "last"].wait_recv()
        delta_sends[e - 1].wait_recv()
        for h in range(heads):
            rows = slice(cols + h * HEAD_DIM, cols + (h + 1) * HEAD_DIM)
            mt[rows] = jnp.broadcast_to(stat_in[e - 1, 4 + h:5 + h], (HEAD_DIM, piece))
        mixed_gradient(e, datt_r[e - 1].reshape(piece, width), mt[...])
        for h in range(heads):
            probs = pt_r[h, e - 1]
            d_scores = score_gradient(h, 0, e, probs, delta_in[e - 1, h:h + 1])
            key_gradient(h, e, probs, d_scores)
    for item in g_in:
        if item.turn:
            item.turned()
        else:
            item.along()
    dproj[...] = dkv0[...].astype(BF16)

    def back_tokens(b):
        value = nt(dproj[block(b)], whole(wa, 0, split))
        return value + nt(dqp[block(b), 0:256], whole(wa, split, split + 256))

    for b in range(2):
        near_copy[3, b] = sum_start(3, b, back_tokens(b))
    far_copy[3, 0] = sum_pass(3, 0, near_copy[3, 0])
    grad_product(0, 0, [(xt, dproj[...])])
    g_kv.start()
    far_copy[3, 1] = sum_pass(3, 1, near_copy[3, 1])
    for b in range(2, BLOCKS):
        near_copy[3, b] = sum_start(3, b, back_tokens(b))
    for b in range(2, BLOCKS):
        far_copy[3, b] = sum_pass(3, b, near_copy[3, b])
    sb[1:2, 0:split] = column_sum(dproj[...].astype(F32))
    sb[2:3, 0:split] = column_sum(dqp[...].astype(F32))
    sb_c = exchange(sbc, sb[...], "ctx", ctx_at, ctxs, me_c)
    for item in g_in:
        if not item.turn:
            item.merge()
    if g_qo.turn:
        g_qo.merge()
    else:
        g_qo.along()
    for b in range(BLOCKS):
        share_copy[3, b] = share(tgbuf, b, (resid[b] + sum_end(3, b, far_copy[3, b])).astype(BF16))
    sb_s = exchange(sbs, exchange_end(sbc, sb_c, ctxs), "shard", shard_at, shards, me_s)
    g_kv.along()
    if g_qo.turn:
        g_qo.turned()
    else:
        g_qo.merge()
    each(g_down, "end", gd_ref)
    for b in range(BLOCKS):
        out_copy[b].wait_recv()
        lo_ref[b] = lobuf[b].reshape(rows_b, width)
    small_ref[0:16] = exchange_end(sas, sa_s, shards)
    g_kv.merge()
    each(g_in, "end", gi_ref)
    for b in range(BLOCKS):
        share_copy[3, b].wait_recv()
        tg_ref[b] = tgbuf[b].reshape(rows_b, width)
    small_ref[16:24] = exchange_end(sbs, sb_s, shards)
    g_qo.end(ga_ref)
    g_kv.end(ga_ref)
    net.finish()


def run_layer(dims, copies, *operands):
    shards, ctxs, wctx, piece, width, chunk, heads = dims
    rows_b = piece // BLOCKS
    half = rows_b // 2
    cols = heads * HEAD_DIM
    hidden_cols = operands[4].shape[1]
    vmem = pl.BlockSpec(memory_space=pltpu.VMEM)
    weights = (shards, wctx, chunk, width)
    turned = (wctx, shards, chunk, piece)
    V = pltpu.VMEM
    shared = (BLOCKS, 2, half, width)
    hidden = (BLOCKS, rows_b, hidden_cols)
    scratch = [
        V(weights, BF16), V(weights, BF16), V(weights, BF16),
        V(turned, BF16), V(turned, BF16),
        V((ctxs, piece, width), BF16),
        V((ctxs, 8, piece), F32), V((ctxs, piece, piece), F32),
        V((ctxs, piece, 2 * cols), BF16), V((ctxs, 2 * cols, piece), BF16), V((ctxs, heads, piece, 256), BF16),
        V((ctxs, piece, piece), F32), V((heads, ctxs, piece, piece), BF16), V((heads, ctxs - 1, piece, piece), BF16),
        V((2 * cols, piece), F32), V((2 * cols, piece), F32), V((piece, LANES), F32), V((BLOCKS, half, width), F32),
        V(shared, BF16), V(hidden, BF16), V(hidden, F32),
        V(shared, BF16), V(hidden, BF16), V(shared, BF16), V((ctxs - 1,) + shared, BF16), V(shared, BF16),
        V(shared, BF16),
        V((4, BLOCKS, 2, half, width), F32), V((4, BLOCKS, half, width), F32),
        V((4, BLOCKS, half, width), BF16), V((4, BLOCKS, half, width), BF16),
        V((3, shards, chunk, width), F32), V((3, shards, chunk, width), BF16), V((3, shards, chunk, width), BF16),
        V((wctx, 3, shards, chunk, width), BF16), V((wctx, 3, shards, chunk, width), BF16),
        V((piece, 2 * cols), F32),
        V((2 * cols, piece), F32), V((piece, 2 * cols), BF16), V((piece, 2 * cols), BF16), V((piece, 2 * cols), BF16),
        V((ctxs, piece, 256), BF16), V((ctxs, 2, piece, LANES), BF16),
        V((BLOCKS, half, width), F32), V((BLOCKS, half, width), F32), V((BLOCKS, half, width), F32),
        V((16, width), F32), V((8, width), F32),
        V((16, width), F32), V((ctxs, 16, width), F32), V((shards, 16, width), F32),
        V((ctxs, 8, width), F32), V((shards, 8, width), F32),
        V((3, chunk, cols), BF16), V((cols, chunk), BF16), V((8, piece), F32), V((8, 2 * cols), F32),
        V((8, piece), F32), V((ctxs - 1, 8, piece), F32), V((8, piece), F32), V((ctxs - 1, 8, piece), F32),
        pltpu.SemaphoreType.DMA((BLOCKS + 5,)), pltpu.SemaphoreType.DMA((copies,)),
        pltpu.SemaphoreType.DMA((copies,)),
    ]
    return pl.pallas_call(
        functools.partial(layer_kernel, dims),
        out_shape=(
            jax.ShapeDtypeStruct((BLOCKS, rows_b, width), BF16),
            jax.ShapeDtypeStruct((BLOCKS, rows_b, width), BF16),
            jax.ShapeDtypeStruct((chunk, width), F32),
            jax.ShapeDtypeStruct((chunk, hidden_cols), F32),
            jax.ShapeDtypeStruct((chunk, hidden_cols), F32),
            jax.ShapeDtypeStruct((24, width), F32),
        ),
        in_specs=[pl.BlockSpec(memory_space=pl.ANY)] * 6 + [vmem] * (len(operands) - 6),
        out_specs=(vmem,) * 6,
        scratch_shapes=scratch,
        compiler_params=pltpu.CompilerParams(
            collective_id=0, has_side_effects=True, vmem_limit_bytes=67_043_328
        ),
        name="layer",
    )(*operands)


def finish_kernel(cols, *refs):
    (lo, tg, ga, gi, gd, small,
     lo_out, tg_out, qkv_out, qv_out, out_out, in_out, down_out, v0, v1, v2, v3, v4, v5, v6, rms_out) = refs
    lo_out[...] = lo[...]
    tg_out[...] = tg[...].astype(F32)
    qkv_out[0] = ga[:, 2 * cols:3 * cols]
    qkv_out[1] = ga[:, 0:cols]
    qkv_out[2] = ga[:, cols:2 * cols]
    out_out[...] = jnp.transpose(ga[:, 3 * cols:])
    in_out[...] = gi[...]
    down_out[...] = gd[...]
    qv_out[0:1] = small[18:19, 0:cols]
    qv_out[1:2] = small[17:18, cols:2 * cols]
    for row, ref in zip((0, 1, 2, 16, 3, 4, 5), (v0, v1, v2, v3, v4, v5, v6)):
        ref[...] = small[row]
    count = small[9:10, 0:1] * small.shape[1]
    for i in range(3):
        rms_out[0:1, i:i + 1] = jnp.sqrt(jnp.sum(small[6 + i:7 + i], axis=1, keepdims=True) / count)


def run_finish(cols, *operands):
    _, rows_b, width = operands[0].shape
    chunk, hidden_cols = operands[3].shape
    shapes = [
        ((BLOCKS, rows_b, width), BF16), ((BLOCKS, rows_b, width), F32), ((3, chunk, cols), F32), ((2, cols), F32),
        ((cols, chunk), F32), ((chunk, hidden_cols), F32), ((chunk, hidden_cols), F32),
        ((width,), F32), ((width,), F32), ((width,), F32), ((hidden_cols,), F32),
        ((width,), F32), ((width,), F32), ((width,), F32), ((1, 3), F32),
    ]
    vmem = pl.BlockSpec(memory_space=pltpu.VMEM)
    return pl.pallas_call(
        functools.partial(finish_kernel, cols),
        out_shape=tuple(jax.ShapeDtypeStruct(*shape) for shape in shapes),
        in_specs=[vmem] * len(operands),
        out_specs=(vmem,) * len(shapes),
        name="finish",
    )(*operands)


def body(
    sizes,
    tokens, segment_ids, valid_mask, qkv_weight, qv_bias, out_weight, out_bias, norm1_gain, norm1_shift,
    in_weight, in_bias, down_weight, down_bias, norm2_gain, norm2_shift, out_cotangent,
):
    shards, ctxs = sizes
    _, piece, width = tokens.shape
    cols = qkv_weight.shape[2]
    heads = cols // HEAD_DIM
    raw = qkv_weight.shape[1] % 16 == 0 and ctxs <= 2
    if raw:
        wctx = ctxs
        parts = [qkv_weight, out_weight, in_weight, down_weight.T]
        chunk = in_weight.shape[0]
    else:
        wctx = 1
        own = jnp.concatenate([qkv_weight[1], qkv_weight[2], qkv_weight[0], out_weight.T], axis=1)
        own, into, down = (
            lax.all_gather(part, "ctx", axis=0, tiled=True) for part in (own, in_weight, down_weight.T)
        )
        parts = [own, out_weight, into, down]
        chunk = own.shape[0]
    dims = (shards, ctxs, wctx, piece, width, chunk, heads)
    vectors = [out_bias, norm1_gain, norm1_shift, in_bias, down_bias, norm2_gain, norm2_shift]
    results = run_layer(
        dims, COPIES, tokens.reshape(piece, width), out_cotangent.reshape(piece, width), *parts,
        segment_ids, valid_mask, qv_bias, *vectors
    )
    if raw:
        lo, tg, g_qkv, g_qv, g_out, g_in, g_down, *sums, rms = run_finish(cols, *results)
        return (
            lo.reshape(1, piece, width), tg.reshape(1, piece, width), g_qkv, g_qv, g_out, sums[0], sums[1], sums[2],
            g_in, sums[3], g_down.T, sums[4], sums[5], sums[6], rms.reshape(-1),
        )
    lo, tg, ga, gi, gd, small = results
    ga, gi, gd = (lax.psum_scatter(g, "ctx", scatter_dimension=0, tiled=True) for g in (ga, gi, gd))
    g_qkv = jnp.stack([ga[:, 2 * cols:3 * cols], ga[:, 0:cols], ga[:, cols:2 * cols]])
    sums = jnp.sum(small[6:9], axis=1)
    return (
        lo.reshape(1, piece, width),
        tg.reshape(1, piece, width).astype(F32),
        g_qkv,
        jnp.stack([small[18, 0:cols], small[17, cols:2 * cols]]),
        ga[:, 3 * cols:].T,
        small[0], small[1], small[2],
        gi,
        small[16],
        gd.T,
        small[3], small[4], small[5],
        jnp.sqrt(sums / (small[9, 0] * width)),
    )


def solution(mesh):
    sizes = (mesh.shape["shard"], mesh.shape["ctx"])
    return jax.shard_map(
        functools.partial(body, sizes),
        mesh=mesh,
        in_specs=(
            P("shard", "ctx", None), P("shard", "ctx"), P("shard", "ctx"),
            P(None, ("shard", "ctx"), "tp"), P(None, "tp"), P("tp", ("shard", "ctx")),
            P(), P(), P(),
            P(("shard", "ctx"), "tp"), P("tp"), P("tp", ("shard", "ctx")),
            P(), P(), P(),
            P("shard", "ctx", None),
        ),
        out_specs=(
            P("shard", "ctx", None), P("shard", "ctx", None),
            P(None, ("shard", "ctx"), "tp"), P(None, "tp"), P("tp", ("shard", "ctx")),
            P(), P(), P(),
            P(("shard", "ctx"), "tp"), P("tp"), P("tp", ("shard", "ctx")),
            P(), P(), P(), P(),
        ),
        check_vma=False,
    )
```

```python
import functools

import jax
import jax.numpy as jnp
from jax import lax
from jax.experimental import pallas as pl
from jax.experimental.pallas import tpu as pltpu
from jax.sharding import PartitionSpec as P

HEAD_DIM = 64
LANES = 128
TP = 4
EPS = 1e-12
MASKED = -1e30
F32 = jnp.float32
BF16 = jnp.bfloat16
BLOCKS = 4
COPIES = {(4, 2): 181}
IN_RANGES = ((0, 768, False),)
DOWN_RANGES = ((0, 384, True), (384, 768, False))
IN_SUMS = ((0, 384, True), (384, 768, False))
DOWN_SUMS = ((0, 384, True), (384, 768, False))
QO_TURN = False
QO_FIRST = False
OA = "A0A1B0A2B1A3X5B2B3X2X6C0D0C1D1C2D2P0C3P1E0D3P2E1P3"
OB = "E2F0E3G0F1H0F2G1G2H1I0F3H2X0G3I1H3X3I2I3X4X1"
ORDER = (OA, OB,
)


def nt(left, right):
    return lax.dot_general(left, right, (((1,), (1,)), ((), ())), preferred_element_type=F32)


def nn(left, right):
    return lax.dot_general(left, right, (((1,), (0,)), ((), ())), preferred_element_type=F32)


def gelu_and_slope(pre):
    scale = 0.7978845608028654
    cube = 0.044715
    square = pre * pre
    tanh = jnp.tanh(scale * pre * (1.0 + cube * square))
    half = 0.5 * (1.0 + tanh)
    slope = half + 0.5 * pre * (1.0 - tanh * tanh) * (scale * (1.0 + 3.0 * cube * square))
    return pre * half, slope


def column_sum(rows):
    return jnp.sum(rows, axis=0, keepdims=True)


def norm_forward(rows):
    mean = jnp.mean(rows, axis=-1, keepdims=True)
    centred = rows - mean
    spread = jnp.mean(centred * centred, axis=-1, keepdims=True)
    inverse = lax.rsqrt(spread + EPS)
    return centred * inverse, inverse


def norm_backward(grad, unit, inverse, gain):
    scaled = grad * gain
    first = jnp.mean(scaled, axis=-1, keepdims=True)
    second = jnp.mean(scaled * unit, axis=-1, keepdims=True)
    return inverse * (scaled - first - unit * second)


class Net:
    def __init__(self, send_sems, recv_sems):
        self.send_sems, self.recv_sems, self.copies = send_sems, recv_sems, []

    def send(self, source, target, where, when=None, place=None):
        number = len(self.copies)
        copy = pltpu.make_async_remote_copy(
            src_ref=source,
            dst_ref=target,
            send_sem=self.send_sems.at[number],
            recv_sem=self.recv_sems.at[number if place is None else place],
            device_id=where,
            device_id_type=pl.DeviceIdType.MESH,
        )
        self.copies.append((copy, when))
        if when is None:
            copy.start()
        else:
            pl.when(when)(copy.start)
        copy.number = number
        return copy

    def finish(self):
        for copy, when in self.copies:
            if when is None:
                copy.wait_send()
            else:
                pl.when(when)(copy.wait_send)


def layer_kernel(dims, *refs):
    shards, ctxs, wctx, piece, width, chunk, heads = dims
    rows_b = piece // BLOCKS
    half = rows_b // 2
    cols = heads * HEAD_DIM
    (x_ref, cot_ref, qkv_ref, out_ref, wi_ref, wd_ref, seg_ref, valid_ref, qv_bias_ref, out_bias_ref, gain1_ref,
     shift1_ref, in_bias_ref, down_bias_ref, gain2_ref, shift2_ref,
     lo_ref, tg_ref, ga_ref, gi_ref, gd_ref, small_ref,
     wa, wi, wd, xt, yt, xs, code_all, bias, kv, kvt, qm, sbuf, pt, pt_r, ott, mt, vcol, cot,
     hid, act, slope, dffn, dpre, datt, datt_r, lobuf, tgbuf,
     part, near_in, far_out, far_in, gown, gxs, gxr, gzs, gzr, dkv0, dqt, dproj, dqp, ctxp, dom0, dom1,
     unit1, hidden, resid, sa, sb,
     sa1, sac, sas, sbc, sbs,
     qkv_own, out_own, code_ref, vec_ref, stat, stat_in, delta, delta_in,
     local_sems, send_sems, recv_sems) = refs
    me_s, me_c, me_t = lax.axis_index("shard"), lax.axis_index("ctx"), lax.axis_index("tp")
    mine = me_t % 2
    other = 1 - mine
    near = {"tp": me_t + 1 - 2 * mine}
    far = {"tp": (me_t + 2) % TP}
    wc = me_c if wctx > 1 else 0
    net = Net(send_sems, recv_sems)

    def shard_at(step):
        return (me_s + step) % shards

    def ctx_at(step):
        return (me_c + step) % ctxs

    line = shards == 4
    steps = [2, 1, 3] if line else list(range(1, shards))
    side = me_s // 2
    is_hub = (me_s + side) % 2 == 1
    partner, other_hub, other_end = me_s + 1 - 2 * (me_s % 2), 2 - side, 3 - 3 * side

    barrier = pltpu.get_barrier_semaphore()
    local = {}

    def fetch(name, source, target):
        local[name] = pltpu.make_async_copy(source, target, local_sems.at[len(local)])
        local[name].start()

    own_a, own_i, own_d = wa.at[me_s, wc], wi.at[me_s, wc], wd.at[me_s, wc]
    if wctx < ctxs:
        fetch("qkv", qkv_ref, own_a)
    else:
        fetch("qkv", qkv_ref, qkv_own)
        fetch("out", out_ref, out_own)
    fetch("x", x_ref, xs.at[0])
    fetch("wi", wi_ref, own_i)
    fetch("wd", wd_ref, own_d)
    peers = [near, far]
    peers += [{"ctx": ctx_at(e)} for e in range(1, ctxs)]
    peers += [{"shard": shard_at(d)} for d in range(1, shards)]
    for peer in peers:
        pl.semaphore_signal(barrier, inc=1, device_id=peer, device_id_type=pl.DeviceIdType.MESH)
    local["qkv"].wait()
    if wctx == ctxs:
        local["out"].wait()
        wa[me_s, wc, :, 0:cols] = qkv_own[1]
        wa[me_s, wc, :, cols:2 * cols] = qkv_own[2]
        wa[me_s, wc, :, 2 * cols:3 * cols] = qkv_own[0]
        wa[me_s, wc, :, 3 * cols:] = jnp.transpose(out_own[...].astype(F32)).astype(BF16)
    local["x"].wait()
    pl.semaphore_wait(barrier, len(peers))

    class Gather:
        def __init__(self, buf, lo, hi, turn=False):
            self.buf, self.span, self.turn = buf, slice(lo, hi), turn and wctx > 1
            self.along, self.across = {}, []

        def piece(self, s, c):
            return self.buf.at[s, c, :, self.span]

        def send_along(self, c):
            reach = {1: me_s != 3, 3: me_s != 0} if line else {}
            own = self.piece(me_s, {"own": wc, "peer": 1 - wc}.get(c, 0))
            for d in steps:
                self.along[c, d] = net.send(own, own, {"shard": shard_at(d)}, reach.get(d))

        def send_across(self, s):
            if wctx > 1:
                piece = self.piece(s, wc)
                self.across.append(net.send(piece, piece, {"ctx": ctx_at(1)}))

        def start(self):
            self.send_along(0 if wctx == 1 else "own")

        def start_across(self):
            self.send_across(me_s)

        def second(self):
            if self.turn:
                self.across[0].wait_recv()
                self.send_along("peer")

        def arrive(self, name, d):
            c = {"own": wc, "peer": 1 - wc}.get(name, 0)
            self.along[name, d].wait_recv()
            s = shard_at(shards - d)
            if line and d == 2:
                piece = self.piece(s, c)
                net.send(piece, piece, {"shard": 3}, me_s == 2, self.along[name, 3].number)
                net.send(piece, piece, {"shard": 0}, me_s == 1, self.along[name, 1].number)
            if name == "own" and not self.turn:
                self.send_across(s)

        def middle(self):
            if line:
                for name, d in list(self.along):
                    if d == 2:
                        self.arrive(name, d)

        def rest(self):
            for name, d in list(self.along):
                if d != 2 or not line:
                    self.arrive(name, d)

        def wait(self):
            for copy in self.across[1 if self.turn else 0:]:
                copy.wait_recv()

    def wait_all(copies):
        for copy in copies:
            copy.wait_recv()

    def whole(buf, lo, hi):
        return buf[:, :, :, lo:hi].reshape(width, hi - lo)

    def sum_start(k, b, value):
        part[k, b] = value.reshape(2, half, width)
        return net.send(part.at[k, b, other], near_in.at[k, b], near)

    def sum_pass(k, b, copy):
        copy.wait_recv()
        far_out[k, b] = (part[k, b, mine] + near_in[k, b]).astype(BF16)
        return net.send(far_out.at[k, b], far_in.at[k, b], far)

    def sum_end(k, b, copy):
        copy.wait_recv()
        return far_out[k, b].astype(F32) + far_in[k, b].astype(F32)

    def share(buf, b, value):
        buf[b, mine] = value
        return net.send(buf.at[b, mine], buf.at[b, mine], near)

    def block(b):
        return slice(b * rows_b, (b + 1) * rows_b)

    def own_rows(b):
        return pl.ds(pl.multiple_of(b * rows_b + mine * half, half), half)

    roles = [other_end, other_hub, partner, me_s] if line else [shard_at(d) for d in range(1, shards)] + [me_s]

    class Sums:
        def __init__(self, k, lo, hi, turn=False):
            self.k, self.span, self.turn = k, slice(lo, hi), turn and wctx > 1
            self.across, self.copies = {}, {}

        def term(self, s, c):
            if c:
                return gxs[self.k, s, :, self.span].astype(F32)
            total = gown[self.k, s, :, self.span]
            if wctx > 1 and not self.turn:
                total = total + gxr[self.k, s, :, self.span].astype(F32)
            return total

        def out_slot(self, c, r):
            return gzs.at[c, self.k, r, :, self.span]

        def in_slot(self, c, r):
            return gzr.at[c, self.k, r, :, self.span]

        def passes(self):
            return (1, 0) if self.turn else (0,)

        def start(self, which=None):
            if wctx == 1 or self.turn:
                return
            for r in range(shards) if which is None else which:
                s = roles[r]
                self.across[r] = net.send(
                    gxs.at[self.k, s, :, self.span], gxr.at[self.k, s, :, self.span], {"ctx": ctx_at(1)}
                )

        def along(self):
            outer = jnp.logical_not(is_hub)
            for r in range(shards - 1):
                if r in self.across:
                    self.across[r].wait_recv()
                for c in self.passes():
                    if line and r < 2:

                        @pl.when(outer)
                        def _():
                            gzs[c, self.k, r, :, self.span] = self.term(roles[r], c).astype(BF16)

                        self.copies[c, r] = net.send(
                            self.out_slot(c, r), self.in_slot(c, r), {"shard": partner}, outer
                        )
                    else:
                        gzs[c, self.k, r, :, self.span] = self.term(roles[r], c).astype(BF16)
                        self.copies[c, r] = net.send(
                            self.out_slot(c, r), self.in_slot(c, r), {"shard": roles[r]}
                        )

        def merge(self):
            if not line:
                return
            for r in range(2):
                for c in self.passes():

                    @pl.when(is_hub)
                    def _():
                        self.copies[c, r].wait_recv()
                        total = self.term(roles[r], c) + gzr[c, self.k, r, :, self.span].astype(F32)
                        gzs[c, self.k, r, :, self.span] = total.astype(BF16)

                    place = self.copies[c, 3].number if r else None
                    copy = net.send(self.out_slot(c, r), self.in_slot(c, 3), {"shard": roles[r]}, is_hub, place)
                    if r == 0:
                        self.copies[c, 3] = copy

        def total(self, c):
            value = self.term(me_s, c)
            for r in (2, 3) if line else range(shards - 1):
                self.copies[c, r].wait_recv()
                value = value + gzr[c, self.k, r, :, self.span].astype(F32)
            return value

        def turned(self):
            if not self.turn:
                return
            gzs[1, self.k, 3, :, self.span] = self.total(1).astype(BF16)
            self.final = net.send(self.out_slot(1, 3), gxr.at[self.k, me_s, :, self.span], {"ctx": ctx_at(1)})

        def end(self, out_ref):
            if shards - 1 in self.across:
                self.across[shards - 1].wait_recv()
            value = self.total(0)
            if self.turn:
                self.final.wait_recv()
                value = value + gxr[self.k, me_s, :, self.span].astype(F32)
            out_ref[:, self.span] = value

    g_down = [Sums(2, *r) for r in DOWN_SUMS]
    g_in = [Sums(1, *r) for r in IN_SUMS]
    g_kv, g_qo = Sums(0, 0, 2 * cols), Sums(0, 2 * cols, width, QO_TURN)

    def each(items, name, *args):
        for item in items:
            getattr(item, name)(*args)

    def grad_product(k, lo, terms):
        for c in range(wctx - 1, -1, -1):
            where = (me_c + c) % wctx if wctx > 1 else 0
            value = 0.0
            for left, right in terms:
                value = value + nn(left[where].reshape(shards * chunk, piece), right)
            n = value.shape[1]
            value = value.reshape(shards, chunk, n)
            if c > 0:
                gxs[k, :, :, lo:lo + n] = value.astype(BF16)
            else:
                gown[k, :, :, lo:lo + n] = value

    def store_transposed(target, value):
        turned = jnp.transpose(value)
        for s in range(shards):
            for c in range(wctx):
                begin = (s * wctx + c) * chunk
                target[c, s] = turned[begin:begin + chunk]

    def exchange(buf, source, axis, at, count, me):
        buf[me] = source
        return [net.send(buf.at[me], buf.at[me], {axis: at(e)}) for e in range(1, count)]

    def exchange_end(buf, state, count):
        wait_all(state)
        total = buf[0]
        for i in range(1, count):
            total = total + buf[i]
        return total

    quarter = piece // TP

    def token_rows(t):
        return pl.ds(pl.multiple_of(t * quarter, quarter), quarter)

    me_rows, far_rows = token_rows(me_t), token_rows((me_t + 2) % TP)
    split = 2 * cols
    w_kv, w_qo = Gather(wa, 0, split), Gather(wa, split, width, QO_FIRST)
    w_in = [Gather(wi, *r) for r in IN_RANGES]
    w_down = [Gather(wd, *r) for r in DOWN_RANGES]
    w_kv.start()
    w_qo.start_across()
    token_in = [
        net.send(xs.at[0, me_rows], xs.at[e, me_rows], {"ctx": ctx_at(e)}) for e in range(1, ctxs)
    ]
    w_kv.start_across()
    w_qo.start()
    seg = seg_ref[...].astype(F32)
    real = valid_ref[...] == 1
    code_ref[...] = jnp.zeros_like(code_ref)
    code_ref[0:1] = jnp.where(real, seg, -1.0)
    code_ref[1:2] = seg
    code_ref[2:3] = jnp.where(real, 1.0, 0.0)
    code_sends = [net.send(code_ref, code_all.at[e], {"ctx": ctx_at(e)}) for e in range(1, ctxs)]
    code_all[0] = code_ref[...]
    for b in range(BLOCKS):
        fetch("cot%d" % b, cot_ref.at[own_rows(b)], cot.at[b])
    vec_ref[...] = jnp.zeros_like(vec_ref)
    vec_ref[0:1, 0:cols] = qv_bias_ref[0:1]
    vec_ref[1:2, cols:2 * cols] = qv_bias_ref[1:2]
    vcol[...] = jnp.transpose(jnp.broadcast_to(code_ref[2:3, :], (LANES, piece)))
    w_qo.second()
    w_kv.middle()
    token_far, token_near = [], []
    for e in range(1, ctxs):
        token_in[e - 1].wait_recv()
        token_far.append(net.send(xs.at[e, me_rows], xs.at[e, me_rows], far))
        token_near.append(net.send(xs.at[e, me_rows], xs.at[e, me_rows], near))

    def column_code(e):
        return jnp.transpose(jnp.broadcast_to(code_all[e][0:1, :], (LANES, piece)))[:, 0:1]

    def store_bias(e):
        allowed = column_code(e) == code_ref[1:2, :]
        if e == 0:
            rows = lax.broadcasted_iota(jnp.int32, (piece, piece), 0)
            lanes = lax.broadcasted_iota(jnp.int32, (piece, piece), 1)
            allowed = allowed | (rows == lanes)
        bias[e] = jnp.where(allowed, 0.0, MASKED)

    store_bias(0)
    w_kv.rest()
    w_qo.middle()
    local["wi"].wait()
    local["wd"].wait()
    for gather in w_in + w_down:
        gather.start()
    for e in range(1, ctxs):
        token_far[e - 1].wait_recv()
        token_near.append(net.send(xs.at[e, far_rows], xs.at[e, far_rows], near))
    for gather in w_in + w_down:
        gather.start_across()
    wait_all(code_sends)
    for e in range(1, ctxs):
        store_bias(e)
    w_kv.wait()

    x = xs[0]

    def project_kv(e):
        kv[e] = (nn(xs[e], whole(wa, 0, split)) + vec_ref[1:2, 0:split]).astype(BF16)
        kvt[e] = jnp.transpose(kv[e])

    lane = lax.broadcasted_iota(jnp.int32, (piece, 256), 1)

    def project_q(e):
        low = (nn(xs[e], whole(wa, split, split + 256)) + vec_ref[0:1, 0:256]).astype(BF16).astype(F32) * 0.125
        for h in range(heads):
            inside = (lane >= h * HEAD_DIM) & (lane < (h + 1) * HEAD_DIM)
            qm[e, h] = jnp.where(inside, low, 0.0).astype(BF16)

    project_kv(0)
    w_qo.rest()
    for gather in w_in + w_down:
        gather.second()
    for gather in w_in:
        gather.middle()
    w_qo.wait()
    project_q(0)
    wait_all(token_near)
    for e in range(1, ctxs):
        project_kv(e)
    each(w_in, "rest")

    ott[0:cols] = jnp.zeros((cols, piece), F32)
    mt[0:cols] = jnp.zeros((cols, piece), F32)
    stat[...] = jnp.zeros_like(stat)
    delta[...] = jnp.zeros_like(delta)
    for h in range(heads):
        top = None
        for e in range(ctxs):
            s = nt(kv[e][:, 0:256], qm[0, h]) + bias[e]
            sbuf[e] = s
            high = jnp.max(s, axis=0, keepdims=True)
            top = high if top is None else jnp.maximum(top, high)
        rows = slice(cols + h * HEAD_DIM, cols + (h + 1) * HEAD_DIM)
        total = jnp.zeros((1, piece), F32)
        mixed = jnp.zeros((HEAD_DIM, piece), F32)
        for e in range(ctxs):
            weights = jnp.exp(sbuf[e] - top)
            total = total + column_sum(weights)
            low = weights.astype(BF16)
            pt[h, e] = low
            mixed = mixed + nn(kvt[e, rows], low)
        inverse = 1.0 / total
        ott[rows] = mixed * inverse
        mt[rows] = jnp.broadcast_to(inverse, (HEAD_DIM, piece))
        stat[h:h + 1] = top
        stat[4 + h:5 + h] = inverse
    stat_sends = [net.send(stat, stat_in.at[e - 1], {"ctx": ctx_at(e)}) for e in range(1, ctxs)]
    ctxp[...] = jnp.transpose(ott[...]).astype(BF16)

    out_bias, gain1, shift1, in_bias = (
        ref[...].reshape(1, -1) for ref in (out_bias_ref, gain1_ref, shift1_ref, in_bias_ref)
    )
    down_bias, gain2, shift2 = (ref[...].reshape(1, -1) for ref in (down_bias_ref, gain2_ref, shift2_ref))
    sa[...] = jnp.zeros_like(sa)
    near_copy, far_copy, share_copy, inverse1, out_copy = {}, {}, {}, {}, {}

    def add_sum(row, value):
        sa[row:row + 1] = sa[row:row + 1] + column_sum(value)

    def stage_a(b):
        near_copy[0, b] = sum_start(0, b, nt(ctxp[block(b)], whole(wa, split, width)))

    def stage_b(b):
        far_copy[0, b] = sum_pass(0, b, near_copy[0, b])

    def stage_c(b):
        attn = sum_end(0, b, far_copy[0, b]) + out_bias
        x_own = xs[0, own_rows(b)].astype(F32)
        valid = vcol[own_rows(b), 0:1]
        unit, inverse1[b] = norm_forward(x_own + attn)
        unit1[b] = unit
        own_hidden = unit * gain1 + shift1
        hidden[b] = own_hidden
        share_copy[0, b] = share(hid, b, own_hidden.astype(BF16))
        add_sum(6, valid * x_own * x_own)
        add_sum(7, valid * attn * attn)
        sa[9:10] = sa[9:10] + column_sum(valid)

    def stage_d(b):
        if b == 0:
            for gather in w_in:
                gather.wait()
        share_copy[0, b].wait_recv()
        pre = nn(hid[b].reshape(rows_b, width), whole(wi, 0, width)) + in_bias
        value, slope[b] = gelu_and_slope(pre)
        act[b] = value.astype(BF16)

    def stage_p(b):
        if b == 0:
            for gather in w_down:
                gather.wait()
        near_copy[1, b] = sum_start(1, b, nt(act[b], whole(wd, 0, width)))

    def stage_e(b):
        far_copy[1, b] = sum_pass(1, b, near_copy[1, b])

    def stage_f(b):
        local["cot%d" % b].wait()
        ffn = sum_end(1, b, far_copy[1, b]) + down_bias
        valid = vcol[own_rows(b), 0:1]
        unit, inverse = norm_forward(hidden[b] + ffn)
        grad = cot[b]
        d_resid2 = norm_backward(grad, unit, inverse, gain2)
        low = d_resid2.astype(BF16)
        share_copy[1, b] = share(dffn, b, low)
        resid[b] = d_resid2
        out_copy[b] = share(lobuf, b, (unit * gain2 + shift2).astype(BF16))
        add_sum(8, valid * ffn * ffn)
        add_sum(3, low.astype(F32))
        add_sum(4, grad * unit)
        add_sum(5, grad)

    ready = set()

    def cotangent_ready(b):
        if b not in ready:
            ready.add(b)
            share_copy[1, b].wait_recv()

    def stage_g(b):
        cotangent_ready(b)
        d_act = nn(dffn[b].reshape(rows_b, width), whole(wd, 0, width))
        dpre[b] = (d_act * slope[b]).astype(BF16)
        near_copy[2, b] = sum_start(2, b, nt(dpre[b], whole(wi, 0, width)))

    def stage_h(b):
        far_copy[2, b] = sum_pass(2, b, near_copy[2, b])

    def stage_i(b):
        d_hidden = resid[b] + sum_end(2, b, far_copy[2, b])
        unit = unit1[b]
        d_resid1 = norm_backward(d_hidden, unit, inverse1[b], gain1)
        low = d_resid1.astype(BF16)
        share_copy[2, b] = share(datt, b, low)
        resid[b] = d_resid1
        add_sum(0, low.astype(F32))
        add_sum(1, d_hidden * unit)
        add_sum(2, d_hidden)

    stages = dict(A=stage_a, B=stage_b, C=stage_c, D=stage_d, E=stage_e, P=stage_p, F=stage_f, G=stage_g, H=stage_h, I=stage_i)

    def down_grads():
        for b in range(BLOCKS):
            cotangent_ready(b)
        store_transposed(yt, dffn[...].reshape(piece, width))
        grad_product(2, 0, [(yt, act[...].reshape(piece, width))])
        each(g_down, "start", (0, 1))
        for item in g_down:
            if item.turn:
                item.along()

    def in_grads():
        each(g_down, "start", range(2, shards))
        store_transposed(yt, hid[...].reshape(piece, width))
        grad_product(1, 0, [(yt, dpre[...].reshape(piece, width))])
        each(g_in, "start")
        for item in g_in:
            if item.turn:
                item.along()

    def remote_probs():
        store_transposed(xt, x)
        for e in range(1, ctxs):
            project_q(e)
            bias[e] = jnp.where(column_code(0) == code_all[e][1:2, :], 0.0, MASKED)
            stat_sends[e - 1].wait_recv()
            for h in range(heads):
                s = nt(kv[0][:, 0:256], qm[e, h]) + bias[e]
                pt_r[h, e - 1] = jnp.exp(s - stat_in[e - 1, h:h + 1]).astype(BF16)

    cross = {}

    def cross_send(j):
        b = 2 * j + me_t // 2
        for e in range(1, ctxs):
            cross[j, e] = net.send(datt.at[b, mine], datt_r.at[e - 1, b, mine], {"ctx": ctx_at(e)})

    def cross_pass(j):
        b = 2 * j + me_t // 2
        for e in range(1, ctxs):
            cross[j, e].wait_recv()
            source = datt_r.at[e - 1, b, mine]
            cross[j, e, "far"] = net.send(source, source, far)
            cross[j, e, "near"] = net.send(source, source, near)

    def cross_last(j):
        b = 2 * j + (me_t // 2 + 1) % 2
        for e in range(1, ctxs):
            cross[j, e, "far"].wait_recv()
            source = datt_r.at[e - 1, b, mine]
            cross[j, e, "last"] = net.send(source, source, near)

    def down_middle():
        for gather in w_down:
            gather.middle()

    def down_rest():
        for gather in w_down:
            gather.rest()

    extras = (down_grads, in_grads, remote_probs, lambda: cross_send(0), lambda: cross_send(1), down_middle, down_rest)
    for name in ORDER:
        for i in range(0, len(name), 2):
            if name[i] == "X":
                extras[int(name[i + 1])]()
            else:
                stages[name[i]](int(name[i + 1]))

    sb[...] = jnp.zeros_like(sb)
    sb[0:1] = column_sum(dpre[...].reshape(piece, width).astype(F32))
    sa_near = net.send(sa, sa1, near)
    for b in range(BLOCKS):
        share_copy[2, b].wait_recv()
    lane = lax.broadcasted_iota(jnp.int32, (piece, LANES), 1)

    def mixed_gradient(e, d_att, scale):
        d_mix = nn(d_att, whole(wa, split, width)).astype(BF16).astype(F32) * jnp.transpose(scale)
        dom0[e] = d_mix[:, 0:256].astype(BF16)
        last = d_mix[:, 256:384]
        dom1[e, 0] = jnp.where(lane < HEAD_DIM, last, 0.0).astype(BF16)
        dom1[e, 1] = jnp.where(lane >= HEAD_DIM, last, 0.0).astype(BF16)
        return d_mix

    d_att_all = datt[...].reshape(piece, width)
    d_mix = mixed_gradient(0, d_att_all, mt[...])
    product = jnp.transpose(d_mix)[cols:] * ott[cols:]
    for h in range(heads):
        delta[h:h + 1] = column_sum(product[h * HEAD_DIM:(h + 1) * HEAD_DIM])
    delta_sends = [net.send(delta, delta_in.at[e - 1], {"ctx": ctx_at(e)}) for e in range(1, ctxs)]
    cross_pass(0)
    for item in g_down:
        if item.turn:
            item.merge()

    def score_gradient(h, keys, queries, probs, deltas):
        if h == 0:
            d_probs = nt(kv[keys][:, 0:256], dom0[queries])
        else:
            d_probs = nt(kv[keys][:, 256:384], dom1[queries, h - 1])
        return (probs.astype(F32) * (d_probs - deltas)).astype(BF16)

    def key_gradient(h, queries, probs, d_scores):
        first = nn(d_scores, qm[queries, h])
        if h == 0:
            dkv0[:, 0:256] = dkv0[:, 0:256] + first + nn(probs, dom0[queries])
        else:
            dkv0[:, 0:256] = dkv0[:, 0:256] + first
            dkv0[:, 256:384] = dkv0[:, 256:384] + nn(probs, dom1[queries, h - 1])

    dkv0[...] = jnp.zeros_like(dkv0)
    dqt[...] = jnp.zeros((2 * cols, piece), F32)
    for e in range(ctxs):
        for h in range(heads):
            d_scores = score_gradient(h, e, 0, pt[h, e], delta[h:h + 1])
            rows = slice(h * HEAD_DIM, (h + 1) * HEAD_DIM)
            dqt[rows] = dqt[rows] + nn(kvt[e, rows], d_scores)
            if e == 0:
                key_gradient(h, 0, pt[h, 0], d_scores)
        if e == 0:
            cross_pass(1)
            cross_last(0)
            for item in g_down:
                if not item.turn:
                    item.along()
    sa_near.wait_recv()
    sa_c = exchange(sac, sa[...] + sa1[...], "ctx", ctx_at, ctxs, me_c)
    cross_last(1)
    each(g_down, "turned")
    for item in g_in:
        if item.turn:
            item.merge()
    dqp[...] = jnp.transpose(dqt[...] * 0.125).astype(BF16)
    store_transposed(yt, d_att_all)
    grad_product(0, split, [(xt, dqp[...]), (yt, ctxp[...])])
    g_qo.start()
    if g_qo.turn:
        g_qo.along()
    for item in g_down:
        if not item.turn:
            item.merge()
    sa_s = exchange(sas, exchange_end(sac, sa_c, ctxs), "shard", shard_at, shards, me_s)
    for e in range(1, ctxs):
        for j in range(BLOCKS // 2):
            cross[j, e, "near"].wait_recv()
            cross[j, e, "last"].wait_recv()
        delta_sends[e - 1].wait_recv()
        for h in range(heads):
            rows = slice(cols + h * HEAD_DIM, cols + (h + 1) * HEAD_DIM)
            mt[rows] = jnp.broadcast_to(stat_in[e - 1, 4 + h:5 + h], (HEAD_DIM, piece))
        mixed_gradient(e, datt_r[e - 1].reshape(piece, width), mt[...])
        for h in range(heads):
            probs = pt_r[h, e - 1]
            d_scores = score_gradient(h, 0, e, probs, delta_in[e - 1, h:h + 1])
            key_gradient(h, e, probs, d_scores)
    for item in g_in:
        if item.turn:
            item.turned()
        else:
            item.along()
    dproj[...] = dkv0[...].astype(BF16)

    def back_tokens(b):
        value = nt(dproj[block(b)], whole(wa, 0, split))
        return value + nt(dqp[block(b), 0:256], whole(wa, split, split + 256))

    for b in range(2):
        near_copy[3, b] = sum_start(3, b, back_tokens(b))
    far_copy[3, 0] = sum_pass(3, 0, near_copy[3, 0])
    grad_product(0, 0, [(xt, dproj[...])])
    g_kv.start()
    far_copy[3, 1] = sum_pass(3, 1, near_copy[3, 1])
    for b in range(2, BLOCKS):
        near_copy[3, b] = sum_start(3, b, back_tokens(b))
    for b in range(2, BLOCKS):
        far_copy[3, b] = sum_pass(3, b, near_copy[3, b])
    sb[1:2, 0:split] = column_sum(dproj[...].astype(F32))
    sb[2:3, 0:split] = column_sum(dqp[...].astype(F32))
    sb_c = exchange(sbc, sb[...], "ctx", ctx_at, ctxs, me_c)
    for item in g_in:
        if not item.turn:
            item.merge()
    if g_qo.turn:
        g_qo.merge()
    else:
        g_qo.along()
    for b in range(BLOCKS):
        share_copy[3, b] = share(tgbuf, b, (resid[b] + sum_end(3, b, far_copy[3, b])).astype(BF16))
    sb_s = exchange(sbs, exchange_end(sbc, sb_c, ctxs), "shard", shard_at, shards, me_s)
    g_kv.along()
    if g_qo.turn:
        g_qo.turned()
    else:
        g_qo.merge()
    each(g_down, "end", gd_ref)
    for b in range(BLOCKS):
        out_copy[b].wait_recv()
        lo_ref[b] = lobuf[b].reshape(rows_b, width)
    small_ref[0:16] = exchange_end(sas, sa_s, shards)
    g_kv.merge()
    each(g_in, "end", gi_ref)
    for b in range(BLOCKS):
        share_copy[3, b].wait_recv()
        tg_ref[b] = tgbuf[b].reshape(rows_b, width)
    small_ref[16:24] = exchange_end(sbs, sb_s, shards)
    g_qo.end(ga_ref)
    g_kv.end(ga_ref)
    net.finish()


def run_layer(dims, copies, *operands):
    shards, ctxs, wctx, piece, width, chunk, heads = dims
    rows_b = piece // BLOCKS
    half = rows_b // 2
    cols = heads * HEAD_DIM
    hidden_cols = operands[4].shape[1]
    vmem = pl.BlockSpec(memory_space=pltpu.VMEM)
    weights = (shards, wctx, chunk, width)
    turned = (wctx, shards, chunk, piece)
    V = pltpu.VMEM
    shared = (BLOCKS, 2, half, width)
    hidden = (BLOCKS, rows_b, hidden_cols)
    scratch = [
        V(weights, BF16), V(weights, BF16), V(weights, BF16),
        V(turned, BF16), V(turned, BF16),
        V((ctxs, piece, width), BF16),
        V((ctxs, 8, piece), F32), V((ctxs, piece, piece), F32),
        V((ctxs, piece, 2 * cols), BF16), V((ctxs, 2 * cols, piece), BF16), V((ctxs, heads, piece, 256), BF16),
        V((ctxs, piece, piece), F32), V((heads, ctxs, piece, piece), BF16), V((heads, ctxs - 1, piece, piece), BF16),
        V((2 * cols, piece), F32), V((2 * cols, piece), F32), V((piece, LANES), F32), V((BLOCKS, half, width), F32),
        V(shared, BF16), V(hidden, BF16), V(hidden, F32),
        V(shared, BF16), V(hidden, BF16), V(shared, BF16), V((ctxs - 1,) + shared, BF16), V(shared, BF16),
        V(shared, BF16),
        V((4, BLOCKS, 2, half, width), F32), V((4, BLOCKS, half, width), F32),
        V((4, BLOCKS, half, width), BF16), V((4, BLOCKS, half, width), BF16),
        V((3, shards, chunk, width), F32), V((3, shards, chunk, width), BF16), V((3, shards, chunk, width), BF16),
        V((wctx, 3, shards, chunk, width), BF16), V((wctx, 3, shards, chunk, width), BF16),
        V((piece, 2 * cols), F32),
        V((2 * cols, piece), F32), V((piece, 2 * cols), BF16), V((piece, 2 * cols), BF16), V((piece, 2 * cols), BF16),
        V((ctxs, piece, 256), BF16), V((ctxs, 2, piece, LANES), BF16),
        V((BLOCKS, half, width), F32), V((BLOCKS, half, width), F32), V((BLOCKS, half, width), F32),
        V((16, width), F32), V((8, width), F32),
        V((16, width), F32), V((ctxs, 16, width), F32), V((shards, 16, width), F32),
        V((ctxs, 8, width), F32), V((shards, 8, width), F32),
        V((3, chunk, cols), BF16), V((cols, chunk), BF16), V((8, piece), F32), V((8, 2 * cols), F32),
        V((8, piece), F32), V((ctxs - 1, 8, piece), F32), V((8, piece), F32), V((ctxs - 1, 8, piece), F32),
        pltpu.SemaphoreType.DMA((BLOCKS + 5,)), pltpu.SemaphoreType.DMA((copies,)),
        pltpu.SemaphoreType.DMA((copies,)),
    ]
    return pl.pallas_call(
        functools.partial(layer_kernel, dims),
        out_shape=(
            jax.ShapeDtypeStruct((BLOCKS, rows_b, width), BF16),
            jax.ShapeDtypeStruct((BLOCKS, rows_b, width), BF16),
            jax.ShapeDtypeStruct((chunk, width), F32),
            jax.ShapeDtypeStruct((chunk, hidden_cols), F32),
            jax.ShapeDtypeStruct((chunk, hidden_cols), F32),
            jax.ShapeDtypeStruct((24, width), F32),
        ),
        in_specs=[pl.BlockSpec(memory_space=pl.ANY)] * 6 + [vmem] * (len(operands) - 6),
        out_specs=(vmem,) * 6,
        scratch_shapes=scratch,
        compiler_params=pltpu.CompilerParams(
            collective_id=0, has_side_effects=True, vmem_limit_bytes=67_043_328
        ),
        name="layer",
    )(*operands)


def finish_kernel(cols, *refs):
    (lo, tg, ga, gi, gd, small,
     lo_out, tg_out, qkv_out, qv_out, out_out, in_out, down_out, v0, v1, v2, v3, v4, v5, v6, rms_out) = refs
    lo_out[...] = lo[...]
    tg_out[...] = tg[...].astype(F32)

    @pl.when(pl.program_id(0) == 0)
    def _():
        qkv_out[0] = ga[:, 2 * cols:3 * cols]
        qkv_out[1] = ga[:, 0:cols]
        qkv_out[2] = ga[:, cols:2 * cols]
        out_out[...] = jnp.transpose(ga[:, 3 * cols:])
        in_out[...] = gi[...]
        down_out[...] = gd[...]
        qv_out[0:1] = small[18:19, 0:cols]
        qv_out[1:2] = small[17:18, cols:2 * cols]
        for row, ref in zip((0, 1, 2, 16, 3, 4, 5), (v0, v1, v2, v3, v4, v5, v6)):
            ref[...] = small[row]
        count = small[9:10, 0:1] * small.shape[1]
        for i in range(3):
            rms_out[0:1, i:i + 1] = jnp.sqrt(jnp.sum(small[6 + i:7 + i], axis=1, keepdims=True) / count)


def run_finish(cols, *operands):
    blocks, rows_b, width = operands[0].shape
    chunk, hidden_cols = operands[3].shape
    shapes = [
        ((blocks, rows_b, width), BF16), ((blocks, rows_b, width), F32), ((3, chunk, cols), F32), ((2, cols), F32),
        ((cols, chunk), F32), ((chunk, hidden_cols), F32), ((chunk, hidden_cols), F32),
        ((width,), F32), ((width,), F32), ((width,), F32), ((hidden_cols,), F32),
        ((width,), F32), ((width,), F32), ((width,), F32), ((1, 3), F32),
    ]
    rows = pl.BlockSpec((1, rows_b, width), lambda i: (i, 0, 0))

    def fixed(shape):
        return pl.BlockSpec(shape, lambda i: (0,) * len(shape))

    return pl.pallas_call(
        functools.partial(finish_kernel, cols),
        grid=(blocks,),
        out_shape=tuple(jax.ShapeDtypeStruct(*shape) for shape in shapes),
        in_specs=[rows, rows] + [fixed(operand.shape) for operand in operands[2:]],
        out_specs=(rows, rows) + tuple(fixed(shape[0]) for shape in shapes[2:]),
        name="finish",
    )(*operands)


def body(
    sizes,
    tokens, segment_ids, valid_mask, qkv_weight, qv_bias, out_weight, out_bias, norm1_gain, norm1_shift,
    in_weight, in_bias, down_weight, down_bias, norm2_gain, norm2_shift, out_cotangent,
):
    shards, ctxs = sizes
    _, piece, width = tokens.shape
    cols = qkv_weight.shape[2]
    heads = cols // HEAD_DIM
    raw = qkv_weight.shape[1] % 16 == 0 and ctxs <= 2
    if raw:
        wctx = ctxs
        parts = [qkv_weight, out_weight, in_weight, down_weight.T]
        chunk = in_weight.shape[0]
    else:
        wctx = 1
        own = jnp.concatenate([qkv_weight[1], qkv_weight[2], qkv_weight[0], out_weight.T], axis=1)
        own, into, down = (
            lax.all_gather(part, "ctx", axis=0, tiled=True) for part in (own, in_weight, down_weight.T)
        )
        parts = [own, out_weight, into, down]
        chunk = own.shape[0]
    dims = (shards, ctxs, wctx, piece, width, chunk, heads)
    vectors = [out_bias, norm1_gain, norm1_shift, in_bias, down_bias, norm2_gain, norm2_shift]
    results = run_layer(
        dims, COPIES.get((shards, ctxs), 320), tokens.reshape(piece, width), out_cotangent.reshape(piece, width), *parts,
        segment_ids, valid_mask, qv_bias, *vectors
    )
    if raw:
        lo, tg, g_qkv, g_qv, g_out, g_in, g_down, *sums, rms = run_finish(cols, *results)
        return (
            lo.reshape(1, piece, width), tg.reshape(1, piece, width), g_qkv, g_qv, g_out, sums[0], sums[1], sums[2],
            g_in, sums[3], g_down.T, sums[4], sums[5], sums[6], rms.reshape(-1),
        )
    lo, tg, ga, gi, gd, small = results
    ga, gi, gd = (lax.psum_scatter(g, "ctx", scatter_dimension=0, tiled=True) for g in (ga, gi, gd))
    g_qkv = jnp.stack([ga[:, 2 * cols:3 * cols], ga[:, 0:cols], ga[:, cols:2 * cols]])
    sums = jnp.sum(small[6:9], axis=1)
    return (
        lo.reshape(1, piece, width),
        tg.reshape(1, piece, width).astype(F32),
        g_qkv,
        jnp.stack([small[18, 0:cols], small[17, cols:2 * cols]]),
        ga[:, 3 * cols:].T,
        small[0], small[1], small[2],
        gi,
        small[16],
        gd.T,
        small[3], small[4], small[5],
        jnp.sqrt(sums / (small[9, 0] * width)),
    )


def solution(mesh):
    sizes = (mesh.shape["shard"], mesh.shape["ctx"])
    return jax.shard_map(
        functools.partial(body, sizes),
        mesh=mesh,
        in_specs=(
            P("shard", "ctx", None), P("shard", "ctx"), P("shard", "ctx"),
            P(None, ("shard", "ctx"), "tp"), P(None, "tp"), P("tp", ("shard", "ctx")),
            P(), P(), P(),
            P(("shard", "ctx"), "tp"), P("tp"), P("tp", ("shard", "ctx")),
            P(), P(), P(),
            P("shard", "ctx", None),
        ),
        out_specs=(
            P("shard", "ctx", None), P("shard", "ctx", None),
            P(None, ("shard", "ctx"), "tp"), P(None, "tp"), P("tp", ("shard", "ctx")),
            P(), P(), P(),
            P(("shard", "ctx"), "tp"), P("tp"), P("tp", ("shard", "ctx")),
            P(), P(), P(), P(),
        ),
        check_vma=False,
    )
```

```python
import functools

import jax
import jax.numpy as jnp
from jax import lax
from jax.experimental import pallas as pl
from jax.experimental.pallas import tpu as pltpu
from jax.sharding import PartitionSpec as P

HEAD_DIM = 64
LANES = 128
TP = 4
EPS = 1e-12
MASKED = -1e30
F32 = jnp.float32
BF16 = jnp.bfloat16
BLOCKS = 4
POOL = 96
COPIES = {(4, 2): 181}
IN_RANGES = ((0, 768, False),)
DOWN_RANGES = ((0, 384, True), (384, 768, False))
IN_SUMS = ((0, 384, True), (384, 768, False))
DOWN_SUMS = ((0, 384, True), (384, 768, False))
QO_TURN = False
QO_FIRST = False
OA = "A0A1B0A2B1A3X5B2B3X2X6C0D0C1D1C2D2P0C3P1E0D3P2E1P3"
OB = "E2F0E3G0F1H0F2G1G2H1I0F3H2X0G3I1H3X3I2I3X4X1"
ORDER = (OA, OB,
)


def nt(left, right):
    return lax.dot_general(left, right, (((1,), (1,)), ((), ())), preferred_element_type=F32)


def nn(left, right):
    return lax.dot_general(left, right, (((1,), (0,)), ((), ())), preferred_element_type=F32)


def gelu_and_slope(pre):
    scale = 0.7978845608028654
    cube = 0.044715
    square = pre * pre
    tanh = jnp.tanh(scale * pre * (1.0 + cube * square))
    half = 0.5 * (1.0 + tanh)
    slope = half + 0.5 * pre * (1.0 - tanh * tanh) * (scale * (1.0 + 3.0 * cube * square))
    return pre * half, slope


def column_sum(rows):
    return jnp.sum(rows, axis=0, keepdims=True)


def norm_forward(rows):
    mean = jnp.mean(rows, axis=-1, keepdims=True)
    centred = rows - mean
    spread = jnp.mean(centred * centred, axis=-1, keepdims=True)
    inverse = lax.rsqrt(spread + EPS)
    return centred * inverse, inverse


def norm_backward(grad, unit, inverse, gain):
    scaled = grad * gain
    first = jnp.mean(scaled, axis=-1, keepdims=True)
    second = jnp.mean(scaled * unit, axis=-1, keepdims=True)
    return inverse * (scaled - first - unit * second)


class Net:
    def __init__(self, send_sems, recv_sems):
        self.send_sems, self.recv_sems, self.copies = send_sems, recv_sems, []

    def send(self, source, target, where, when=None, place=None):
        number = len(self.copies)
        if number >= POOL:
            self.sent(number - POOL)
        copy = pltpu.make_async_remote_copy(
            src_ref=source,
            dst_ref=target,
            send_sem=self.send_sems.at[number % POOL],
            recv_sem=self.recv_sems.at[number if place is None else place],
            device_id=where,
            device_id_type=pl.DeviceIdType.MESH,
        )
        self.copies.append((copy, when))
        if when is None:
            copy.start()
        else:
            pl.when(when)(copy.start)
        copy.number = number
        return copy

    def finish(self):
        for number in range(max(0, len(self.copies) - POOL), len(self.copies)):
            self.sent(number)

    def sent(self, number):
        copy, when = self.copies[number]
        if when is None:
            copy.wait_send()
        else:
            pl.when(when)(copy.wait_send)


def layer_kernel(dims, *refs):
    shards, ctxs, wctx, piece, width, chunk, heads = dims
    rows_b = piece // BLOCKS
    half = rows_b // 2
    cols = heads * HEAD_DIM
    (x_ref, cot_ref, qkv_ref, out_ref, wi_ref, wd_ref, seg_ref, valid_ref, qv_bias_ref, out_bias_ref, gain1_ref,
     shift1_ref, in_bias_ref, down_bias_ref, gain2_ref, shift2_ref,
     lo_ref, tg_ref, ga_ref, gi_ref, gd_ref, small_ref,
     wa, wi, wd, xt, yt, xs, code_all, bias, kv, kvt, qm, sbuf, pt, pt_r, ott, mt, vcol, cot,
     hid, act, slope, dffn, dpre, datt, datt_r, lobuf, tgbuf,
     part, near_in, far_out, far_in, gown, gxs, gxr, gzs, gzr, dkv0, dqt, dproj, dqp, ctxp, dom0, dom1,
     unit1, hidden, resid, sa, sb,
     sa1, sac, sas, sbc, sbs,
     qkv_own, out_own, code_ref, vec_ref, stat, stat_in, delta, delta_in,
     local_sems, send_sems, recv_sems) = refs
    me_s, me_c, me_t = lax.axis_index("shard"), lax.axis_index("ctx"), lax.axis_index("tp")
    mine = me_t % 2
    other = 1 - mine
    near = {"tp": me_t + 1 - 2 * mine}
    far = {"tp": (me_t + 2) % TP}
    wc = me_c if wctx > 1 else 0
    net = Net(send_sems, recv_sems)

    def shard_at(step):
        return (me_s + step) % shards

    def ctx_at(step):
        return (me_c + step) % ctxs

    line = shards == 4
    steps = [2, 1, 3] if line else list(range(1, shards))
    side = me_s // 2
    is_hub = (me_s + side) % 2 == 1
    partner, other_hub, other_end = me_s + 1 - 2 * (me_s % 2), 2 - side, 3 - 3 * side

    barrier = pltpu.get_barrier_semaphore()
    local = {}

    def fetch(name, source, target):
        local[name] = pltpu.make_async_copy(source, target, local_sems.at[len(local)])
        local[name].start()

    own_a, own_i, own_d = wa.at[me_s, wc], wi.at[me_s, wc], wd.at[me_s, wc]
    if wctx < ctxs:
        fetch("qkv", qkv_ref, own_a)
    else:
        fetch("qkv", qkv_ref, qkv_own)
        fetch("out", out_ref, out_own)
    fetch("x", x_ref, xs.at[0])
    fetch("wi", wi_ref, own_i)
    fetch("wd", wd_ref, own_d)
    peers = [near, far]
    peers += [{"ctx": ctx_at(e)} for e in range(1, ctxs)]
    peers += [{"shard": shard_at(d)} for d in range(1, shards)]
    for peer in peers:
        pl.semaphore_signal(barrier, inc=1, device_id=peer, device_id_type=pl.DeviceIdType.MESH)
    local["qkv"].wait()
    if wctx == ctxs:
        local["out"].wait()
        wa[me_s, wc, :, 0:cols] = qkv_own[1]
        wa[me_s, wc, :, cols:2 * cols] = qkv_own[2]
        wa[me_s, wc, :, 2 * cols:3 * cols] = qkv_own[0]
        wa[me_s, wc, :, 3 * cols:] = jnp.transpose(out_own[...].astype(F32)).astype(BF16)
    local["x"].wait()
    pl.semaphore_wait(barrier, len(peers))

    class Gather:
        def __init__(self, buf, lo, hi, turn=False):
            self.buf, self.span, self.turn = buf, slice(lo, hi), turn and wctx > 1
            self.along, self.across = {}, []

        def piece(self, s, c):
            return self.buf.at[s, c, :, self.span]

        def send_along(self, c):
            reach = {1: me_s != 3, 3: me_s != 0} if line else {}
            own = self.piece(me_s, {"own": wc, "peer": 1 - wc}.get(c, 0))
            for d in steps:
                self.along[c, d] = net.send(own, own, {"shard": shard_at(d)}, reach.get(d))

        def send_across(self, s):
            if wctx > 1:
                piece = self.piece(s, wc)
                self.across.append(net.send(piece, piece, {"ctx": ctx_at(1)}))

        def start(self):
            self.send_along(0 if wctx == 1 else "own")

        def start_across(self):
            self.send_across(me_s)

        def second(self):
            if self.turn:
                self.across[0].wait_recv()
                self.send_along("peer")

        def arrive(self, name, d):
            c = {"own": wc, "peer": 1 - wc}.get(name, 0)
            self.along[name, d].wait_recv()
            s = shard_at(shards - d)
            if line and d == 2:
                piece = self.piece(s, c)
                net.send(piece, piece, {"shard": 3}, me_s == 2, self.along[name, 3].number)
                net.send(piece, piece, {"shard": 0}, me_s == 1, self.along[name, 1].number)
            if name == "own" and not self.turn:
                self.send_across(s)

        def middle(self):
            if line:
                for name, d in list(self.along):
                    if d == 2:
                        self.arrive(name, d)

        def rest(self):
            for name, d in list(self.along):
                if d != 2 or not line:
                    self.arrive(name, d)

        def wait(self):
            for copy in self.across[1 if self.turn else 0:]:
                copy.wait_recv()

    def wait_all(copies):
        for copy in copies:
            copy.wait_recv()

    def whole(buf, lo, hi):
        return buf[:, :, :, lo:hi].reshape(width, hi - lo)

    def sum_start(k, b, value):
        part[k, b] = value.reshape(2, half, width)
        return net.send(part.at[k, b, other], near_in.at[k, b], near)

    def sum_pass(k, b, copy):
        copy.wait_recv()
        far_out[k, b] = (part[k, b, mine] + near_in[k, b]).astype(BF16)
        return net.send(far_out.at[k, b], far_in.at[k, b], far)

    def sum_end(k, b, copy):
        copy.wait_recv()
        return far_out[k, b].astype(F32) + far_in[k, b].astype(F32)

    def share(buf, b, value):
        buf[b, mine] = value
        return net.send(buf.at[b, mine], buf.at[b, mine], near)

    def block(b):
        return slice(b * rows_b, (b + 1) * rows_b)

    def own_rows(b):
        return pl.ds(pl.multiple_of(b * rows_b + mine * half, half), half)

    roles = [other_end, other_hub, partner, me_s] if line else [shard_at(d) for d in range(1, shards)] + [me_s]

    class Sums:
        def __init__(self, k, lo, hi, turn=False):
            self.k, self.span, self.turn = k, slice(lo, hi), turn and wctx > 1
            self.across, self.copies = {}, {}

        def term(self, s, c):
            if c:
                return gxs[self.k, s, :, self.span].astype(F32)
            total = gown[self.k, s, :, self.span]
            if wctx > 1 and not self.turn:
                total = total + gxr[self.k, s, :, self.span].astype(F32)
            return total

        def out_slot(self, c, r):
            return gzs.at[c, self.k, r, :, self.span]

        def in_slot(self, c, r):
            return gzr.at[c, self.k, r, :, self.span]

        def passes(self):
            return (1, 0) if self.turn else (0,)

        def start(self, which=None):
            if wctx == 1 or self.turn:
                return
            for r in range(shards) if which is None else which:
                s = roles[r]
                self.across[r] = net.send(
                    gxs.at[self.k, s, :, self.span], gxr.at[self.k, s, :, self.span], {"ctx": ctx_at(1)}
                )

        def along(self):
            outer = jnp.logical_not(is_hub)
            for r in range(shards - 1):
                if r in self.across:
                    self.across[r].wait_recv()
                for c in self.passes():
                    if line and r < 2:

                        @pl.when(outer)
                        def _():
                            gzs[c, self.k, r, :, self.span] = self.term(roles[r], c).astype(BF16)

                        self.copies[c, r] = net.send(
                            self.out_slot(c, r), self.in_slot(c, r), {"shard": partner}, outer
                        )
                    else:
                        gzs[c, self.k, r, :, self.span] = self.term(roles[r], c).astype(BF16)
                        self.copies[c, r] = net.send(
                            self.out_slot(c, r), self.in_slot(c, r), {"shard": roles[r]}
                        )

        def merge(self):
            if not line:
                return
            for r in range(2):
                for c in self.passes():

                    @pl.when(is_hub)
                    def _():
                        self.copies[c, r].wait_recv()
                        total = self.term(roles[r], c) + gzr[c, self.k, r, :, self.span].astype(F32)
                        gzs[c, self.k, r, :, self.span] = total.astype(BF16)

                    place = self.copies[c, 3].number if r else None
                    copy = net.send(self.out_slot(c, r), self.in_slot(c, 3), {"shard": roles[r]}, is_hub, place)
                    if r == 0:
                        self.copies[c, 3] = copy

        def total(self, c):
            value = self.term(me_s, c)
            for r in (2, 3) if line else range(shards - 1):
                self.copies[c, r].wait_recv()
                value = value + gzr[c, self.k, r, :, self.span].astype(F32)
            return value

        def turned(self):
            if not self.turn:
                return
            gzs[1, self.k, 3, :, self.span] = self.total(1).astype(BF16)
            self.final = net.send(self.out_slot(1, 3), gxr.at[self.k, me_s, :, self.span], {"ctx": ctx_at(1)})

        def end(self, out_ref):
            if shards - 1 in self.across:
                self.across[shards - 1].wait_recv()
            value = self.total(0)
            if self.turn:
                self.final.wait_recv()
                value = value + gxr[self.k, me_s, :, self.span].astype(F32)
            out_ref[:, self.span] = value

    g_down = [Sums(2, *r) for r in DOWN_SUMS]
    g_in = [Sums(1, *r) for r in IN_SUMS]
    g_kv, g_qo = Sums(0, 0, 2 * cols), Sums(0, 2 * cols, width, QO_TURN)

    def each(items, name, *args):
        for item in items:
            getattr(item, name)(*args)

    def grad_product(k, lo, terms):
        for c in range(wctx - 1, -1, -1):
            where = (me_c + c) % wctx if wctx > 1 else 0
            value = 0.0
            for left, right in terms:
                value = value + nn(left[where].reshape(shards * chunk, piece), right)
            n = value.shape[1]
            value = value.reshape(shards, chunk, n)
            if c > 0:
                gxs[k, :, :, lo:lo + n] = value.astype(BF16)
            else:
                gown[k, :, :, lo:lo + n] = value

    def store_transposed(target, value):
        turned = jnp.transpose(value)
        for s in range(shards):
            for c in range(wctx):
                begin = (s * wctx + c) * chunk
                target[c, s] = turned[begin:begin + chunk]

    def exchange(buf, source, axis, at, count, me):
        buf[me] = source
        return [net.send(buf.at[me], buf.at[me], {axis: at(e)}) for e in range(1, count)]

    def exchange_end(buf, state, count):
        wait_all(state)
        total = buf[0]
        for i in range(1, count):
            total = total + buf[i]
        return total

    quarter = piece // TP

    def token_rows(t):
        return pl.ds(pl.multiple_of(t * quarter, quarter), quarter)

    me_rows, far_rows = token_rows(me_t), token_rows((me_t + 2) % TP)
    split = 2 * cols
    w_kv, w_qo = Gather(wa, 0, split), Gather(wa, split, width, QO_FIRST)
    w_in = [Gather(wi, *r) for r in IN_RANGES]
    w_down = [Gather(wd, *r) for r in DOWN_RANGES]
    w_kv.start()
    w_qo.start_across()
    token_in = [
        net.send(xs.at[0, me_rows], xs.at[e, me_rows], {"ctx": ctx_at(e)}) for e in range(1, ctxs)
    ]
    w_kv.start_across()
    w_qo.start()
    seg = seg_ref[...].astype(F32)
    real = valid_ref[...] == 1
    code_ref[...] = jnp.zeros_like(code_ref)
    code_ref[0:1] = jnp.where(real, seg, -1.0)
    code_ref[1:2] = seg
    code_ref[2:3] = jnp.where(real, 1.0, 0.0)
    code_sends = [net.send(code_ref, code_all.at[e], {"ctx": ctx_at(e)}) for e in range(1, ctxs)]
    code_all[0] = code_ref[...]
    for b in range(BLOCKS):
        fetch("cot%d" % b, cot_ref.at[own_rows(b)], cot.at[b])
    vec_ref[...] = jnp.zeros_like(vec_ref)
    vec_ref[0:1, 0:cols] = qv_bias_ref[0:1]
    vec_ref[1:2, cols:2 * cols] = qv_bias_ref[1:2]
    vcol[...] = jnp.transpose(jnp.broadcast_to(code_ref[2:3, :], (LANES, piece)))
    w_qo.second()
    w_kv.middle()
    token_far, token_near = [], []
    for e in range(1, ctxs):
        token_in[e - 1].wait_recv()
        token_far.append(net.send(xs.at[e, me_rows], xs.at[e, me_rows], far))
        token_near.append(net.send(xs.at[e, me_rows], xs.at[e, me_rows], near))

    def column_code(e):
        return jnp.transpose(jnp.broadcast_to(code_all[e][0:1, :], (LANES, piece)))[:, 0:1]

    def store_bias(e):
        allowed = column_code(e) == code_ref[1:2, :]
        if e == 0:
            rows = lax.broadcasted_iota(jnp.int32, (piece, piece), 0)
            lanes = lax.broadcasted_iota(jnp.int32, (piece, piece), 1)
            allowed = allowed | (rows == lanes)
        bias[e] = jnp.where(allowed, 0.0, MASKED)

    store_bias(0)
    w_kv.rest()
    w_qo.middle()
    local["wi"].wait()
    local["wd"].wait()
    for gather in w_in + w_down:
        gather.start()
    for e in range(1, ctxs):
        token_far[e - 1].wait_recv()
        token_near.append(net.send(xs.at[e, far_rows], xs.at[e, far_rows], near))
    for gather in w_in + w_down:
        gather.start_across()
    wait_all(code_sends)
    for e in range(1, ctxs):
        store_bias(e)
    w_kv.wait()

    x = xs[0]

    def project_kv(e):
        kv[e] = (nn(xs[e], whole(wa, 0, split)) + vec_ref[1:2, 0:split]).astype(BF16)
        kvt[e] = jnp.transpose(kv[e])

    lane = lax.broadcasted_iota(jnp.int32, (piece, 256), 1)

    def project_q(e):
        low = (nn(xs[e], whole(wa, split, split + 256)) + vec_ref[0:1, 0:256]).astype(BF16).astype(F32) * 0.125
        for h in range(heads):
            inside = (lane >= h * HEAD_DIM) & (lane < (h + 1) * HEAD_DIM)
            qm[e, h] = jnp.where(inside, low, 0.0).astype(BF16)

    project_kv(0)
    w_qo.rest()
    for gather in w_in + w_down:
        gather.second()
    for gather in w_in:
        gather.middle()
    w_qo.wait()
    project_q(0)
    wait_all(token_near)
    for e in range(1, ctxs):
        project_kv(e)
    each(w_in, "rest")

    ott[0:cols] = jnp.zeros((cols, piece), F32)
    mt[0:cols] = jnp.zeros((cols, piece), F32)
    stat[...] = jnp.zeros_like(stat)
    delta[...] = jnp.zeros_like(delta)
    for h in range(heads):
        top = None
        for e in range(ctxs):
            s = nt(kv[e][:, 0:256], qm[0, h]) + bias[e]
            sbuf[e] = s
            high = jnp.max(s, axis=0, keepdims=True)
            top = high if top is None else jnp.maximum(top, high)
        rows = slice(cols + h * HEAD_DIM, cols + (h + 1) * HEAD_DIM)
        total = jnp.zeros((1, piece), F32)
        mixed = jnp.zeros((HEAD_DIM, piece), F32)
        for e in range(ctxs):
            weights = jnp.exp(sbuf[e] - top)
            total = total + column_sum(weights)
            low = weights.astype(BF16)
            pt[h, e] = low
            mixed = mixed + nn(kvt[e, rows], low)
        inverse = 1.0 / total
        ott[rows] = mixed * inverse
        mt[rows] = jnp.broadcast_to(inverse, (HEAD_DIM, piece))
        stat[h:h + 1] = top
        stat[4 + h:5 + h] = inverse
    stat_sends = [net.send(stat, stat_in.at[e - 1], {"ctx": ctx_at(e)}) for e in range(1, ctxs)]
    ctxp[...] = jnp.transpose(ott[...]).astype(BF16)

    out_bias, gain1, shift1, in_bias = (
        ref[...].reshape(1, -1) for ref in (out_bias_ref, gain1_ref, shift1_ref, in_bias_ref)
    )
    down_bias, gain2, shift2 = (ref[...].reshape(1, -1) for ref in (down_bias_ref, gain2_ref, shift2_ref))
    sa[...] = jnp.zeros_like(sa)
    near_copy, far_copy, share_copy, inverse1, out_copy = {}, {}, {}, {}, {}

    def add_sum(row, value):
        sa[row:row + 1] = sa[row:row + 1] + column_sum(value)

    def stage_a(b):
        near_copy[0, b] = sum_start(0, b, nt(ctxp[block(b)], whole(wa, split, width)))

    def stage_b(b):
        far_copy[0, b] = sum_pass(0, b, near_copy[0, b])

    def stage_c(b):
        attn = sum_end(0, b, far_copy[0, b]) + out_bias
        x_own = xs[0, own_rows(b)].astype(F32)
        valid = vcol[own_rows(b), 0:1]
        unit, inverse1[b] = norm_forward(x_own + attn)
        unit1[b] = unit
        own_hidden = unit * gain1 + shift1
        hidden[b] = own_hidden
        share_copy[0, b] = share(hid, b, own_hidden.astype(BF16))
        add_sum(6, valid * x_own * x_own)
        add_sum(7, valid * attn * attn)
        sa[9:10] = sa[9:10] + column_sum(valid)

    def stage_d(b):
        if b == 0:
            for gather in w_in:
                gather.wait()
        share_copy[0, b].wait_recv()
        pre = nn(hid[b].reshape(rows_b, width), whole(wi, 0, width)) + in_bias
        value, slope[b] = gelu_and_slope(pre)
        act[b] = value.astype(BF16)

    def stage_p(b):
        if b == 0:
            for gather in w_down:
                gather.wait()
        near_copy[1, b] = sum_start(1, b, nt(act[b], whole(wd, 0, width)))

    def stage_e(b):
        far_copy[1, b] = sum_pass(1, b, near_copy[1, b])

    def stage_f(b):
        local["cot%d" % b].wait()
        ffn = sum_end(1, b, far_copy[1, b]) + down_bias
        valid = vcol[own_rows(b), 0:1]
        unit, inverse = norm_forward(hidden[b] + ffn)
        grad = cot[b]
        d_resid2 = norm_backward(grad, unit, inverse, gain2)
        low = d_resid2.astype(BF16)
        share_copy[1, b] = share(dffn, b, low)
        resid[b] = d_resid2
        out_copy[b] = share(lobuf, b, (unit * gain2 + shift2).astype(BF16))
        add_sum(8, valid * ffn * ffn)
        add_sum(3, low.astype(F32))
        add_sum(4, grad * unit)
        add_sum(5, grad)

    ready = set()

    def cotangent_ready(b):
        if b not in ready:
            ready.add(b)
            share_copy[1, b].wait_recv()

    def stage_g(b):
        cotangent_ready(b)
        d_act = nn(dffn[b].reshape(rows_b, width), whole(wd, 0, width))
        dpre[b] = (d_act * slope[b]).astype(BF16)
        near_copy[2, b] = sum_start(2, b, nt(dpre[b], whole(wi, 0, width)))

    def stage_h(b):
        far_copy[2, b] = sum_pass(2, b, near_copy[2, b])

    def stage_i(b):
        d_hidden = resid[b] + sum_end(2, b, far_copy[2, b])
        unit = unit1[b]
        d_resid1 = norm_backward(d_hidden, unit, inverse1[b], gain1)
        low = d_resid1.astype(BF16)
        share_copy[2, b] = share(datt, b, low)
        resid[b] = d_resid1
        add_sum(0, low.astype(F32))
        add_sum(1, d_hidden * unit)
        add_sum(2, d_hidden)

    stages = dict(A=stage_a, B=stage_b, C=stage_c, D=stage_d, E=stage_e, P=stage_p, F=stage_f, G=stage_g, H=stage_h, I=stage_i)

    def down_grads():
        for b in range(BLOCKS):
            cotangent_ready(b)
        store_transposed(yt, dffn[...].reshape(piece, width))
        grad_product(2, 0, [(yt, act[...].reshape(piece, width))])
        each(g_down, "start", (0, 1))
        for item in g_down:
            if item.turn:
                item.along()

    def in_grads():
        each(g_down, "start", range(2, shards))
        store_transposed(yt, hid[...].reshape(piece, width))
        grad_product(1, 0, [(yt, dpre[...].reshape(piece, width))])
        each(g_in, "start")
        for item in g_in:
            if item.turn:
                item.along()

    def remote_probs():
        store_transposed(xt, x)
        for e in range(1, ctxs):
            project_q(e)
            bias[e] = jnp.where(column_code(0) == code_all[e][1:2, :], 0.0, MASKED)
            stat_sends[e - 1].wait_recv()
            for h in range(heads):
                s = nt(kv[0][:, 0:256], qm[e, h]) + bias[e]
                pt_r[h, e - 1] = jnp.exp(s - stat_in[e - 1, h:h + 1]).astype(BF16)

    cross = {}

    def cross_send(j):
        b = 2 * j + me_t // 2
        for e in range(1, ctxs):
            cross[j, e] = net.send(datt.at[b, mine], datt_r.at[e - 1, b, mine], {"ctx": ctx_at(e)})

    def cross_pass(j):
        b = 2 * j + me_t // 2
        for e in range(1, ctxs):
            cross[j, e].wait_recv()
            source = datt_r.at[e - 1, b, mine]
            cross[j, e, "far"] = net.send(source, source, far)
            cross[j, e, "near"] = net.send(source, source, near)

    def cross_last(j):
        b = 2 * j + (me_t // 2 + 1) % 2
        for e in range(1, ctxs):
            cross[j, e, "far"].wait_recv()
            source = datt_r.at[e - 1, b, mine]
            cross[j, e, "last"] = net.send(source, source, near)

    def down_middle():
        for gather in w_down:
            gather.middle()

    def down_rest():
        for gather in w_down:
            gather.rest()

    extras = (down_grads, in_grads, remote_probs, lambda: cross_send(0), lambda: cross_send(1), down_middle, down_rest)
    for name in ORDER:
        for i in range(0, len(name), 2):
            if name[i] == "X":
                extras[int(name[i + 1])]()
            else:
                stages[name[i]](int(name[i + 1]))

    sb[...] = jnp.zeros_like(sb)
    sb[0:1] = column_sum(dpre[...].reshape(piece, width).astype(F32))
    sa_near = net.send(sa, sa1, near)
    for b in range(BLOCKS):
        share_copy[2, b].wait_recv()
    lane = lax.broadcasted_iota(jnp.int32, (piece, LANES), 1)

    def mixed_gradient(e, d_att, scale):
        d_mix = nn(d_att, whole(wa, split, width)).astype(BF16).astype(F32) * jnp.transpose(scale)
        dom0[e] = d_mix[:, 0:256].astype(BF16)
        last = d_mix[:, 256:384]
        dom1[e, 0] = jnp.where(lane < HEAD_DIM, last, 0.0).astype(BF16)
        dom1[e, 1] = jnp.where(lane >= HEAD_DIM, last, 0.0).astype(BF16)
        return d_mix

    d_att_all = datt[...].reshape(piece, width)
    d_mix = mixed_gradient(0, d_att_all, mt[...])
    product = jnp.transpose(d_mix)[cols:] * ott[cols:]
    for h in range(heads):
        delta[h:h + 1] = column_sum(product[h * HEAD_DIM:(h + 1) * HEAD_DIM])
    delta_sends = [net.send(delta, delta_in.at[e - 1], {"ctx": ctx_at(e)}) for e in range(1, ctxs)]
    cross_pass(0)
    for item in g_down:
        if item.turn:
            item.merge()

    def score_gradient(h, keys, queries, probs, deltas):
        if h == 0:
            d_probs = nt(kv[keys][:, 0:256], dom0[queries])
        else:
            d_probs = nt(kv[keys][:, 256:384], dom1[queries, h - 1])
        return (probs.astype(F32) * (d_probs - deltas)).astype(BF16)

    def key_gradient(h, queries, probs, d_scores):
        first = nn(d_scores, qm[queries, h])
        if h == 0:
            dkv0[:, 0:256] = dkv0[:, 0:256] + first + nn(probs, dom0[queries])
        else:
            dkv0[:, 0:256] = dkv0[:, 0:256] + first
            dkv0[:, 256:384] = dkv0[:, 256:384] + nn(probs, dom1[queries, h - 1])

    dkv0[...] = jnp.zeros_like(dkv0)
    dqt[...] = jnp.zeros((2 * cols, piece), F32)
    for e in range(ctxs):
        for h in range(heads):
            d_scores = score_gradient(h, e, 0, pt[h, e], delta[h:h + 1])
            rows = slice(h * HEAD_DIM, (h + 1) * HEAD_DIM)
            dqt[rows] = dqt[rows] + nn(kvt[e, rows], d_scores)
            if e == 0:
                key_gradient(h, 0, pt[h, 0], d_scores)
        if e == 0:
            cross_pass(1)
            cross_last(0)
            for item in g_down:
                if not item.turn:
                    item.along()
    sa_near.wait_recv()
    sa_c = exchange(sac, sa[...] + sa1[...], "ctx", ctx_at, ctxs, me_c)
    cross_last(1)
    each(g_down, "turned")
    for item in g_in:
        if item.turn:
            item.merge()
    dqp[...] = jnp.transpose(dqt[...] * 0.125).astype(BF16)
    store_transposed(yt, d_att_all)
    grad_product(0, split, [(xt, dqp[...]), (yt, ctxp[...])])
    g_qo.start()
    if g_qo.turn:
        g_qo.along()
    for item in g_down:
        if not item.turn:
            item.merge()
    sa_s = exchange(sas, exchange_end(sac, sa_c, ctxs), "shard", shard_at, shards, me_s)
    for e in range(1, ctxs):
        for j in range(BLOCKS // 2):
            cross[j, e, "near"].wait_recv()
            cross[j, e, "last"].wait_recv()
        delta_sends[e - 1].wait_recv()
        for h in range(heads):
            rows = slice(cols + h * HEAD_DIM, cols + (h + 1) * HEAD_DIM)
            mt[rows] = jnp.broadcast_to(stat_in[e - 1, 4 + h:5 + h], (HEAD_DIM, piece))
        mixed_gradient(e, datt_r[e - 1].reshape(piece, width), mt[...])
        for h in range(heads):
            probs = pt_r[h, e - 1]
            d_scores = score_gradient(h, 0, e, probs, delta_in[e - 1, h:h + 1])
            key_gradient(h, e, probs, d_scores)
    for item in g_in:
        if item.turn:
            item.turned()
        else:
            item.along()
    dproj[...] = dkv0[...].astype(BF16)

    def back_tokens(b):
        value = nt(dproj[block(b)], whole(wa, 0, split))
        return value + nt(dqp[block(b), 0:256], whole(wa, split, split + 256))

    for b in range(2):
        near_copy[3, b] = sum_start(3, b, back_tokens(b))
    far_copy[3, 0] = sum_pass(3, 0, near_copy[3, 0])
    grad_product(0, 0, [(xt, dproj[...])])
    g_kv.start()
    far_copy[3, 1] = sum_pass(3, 1, near_copy[3, 1])
    for b in range(2, BLOCKS):
        near_copy[3, b] = sum_start(3, b, back_tokens(b))
    for b in range(2, BLOCKS):
        far_copy[3, b] = sum_pass(3, b, near_copy[3, b])
    sb[1:2, 0:split] = column_sum(dproj[...].astype(F32))
    sb[2:3, 0:split] = column_sum(dqp[...].astype(F32))
    sb_c = exchange(sbc, sb[...], "ctx", ctx_at, ctxs, me_c)
    for item in g_in:
        if not item.turn:
            item.merge()
    if g_qo.turn:
        g_qo.merge()
    else:
        g_qo.along()
    for b in range(BLOCKS):
        share_copy[3, b] = share(tgbuf, b, (resid[b] + sum_end(3, b, far_copy[3, b])).astype(BF16))
    sb_s = exchange(sbs, exchange_end(sbc, sb_c, ctxs), "shard", shard_at, shards, me_s)
    g_kv.along()
    if g_qo.turn:
        g_qo.turned()
    else:
        g_qo.merge()
    each(g_down, "end", gd_ref)
    for b in range(BLOCKS):
        out_copy[b].wait_recv()
        lo_ref[b] = lobuf[b].reshape(rows_b, width)
    small_ref[0:16] = exchange_end(sas, sa_s, shards)
    g_kv.merge()
    each(g_in, "end", gi_ref)
    for b in range(BLOCKS):
        share_copy[3, b].wait_recv()
        tg_ref[b] = tgbuf[b].reshape(rows_b, width)
    small_ref[16:24] = exchange_end(sbs, sb_s, shards)
    g_qo.end(ga_ref)
    g_kv.end(ga_ref)
    net.finish()


def run_layer(dims, copies, *operands):
    shards, ctxs, wctx, piece, width, chunk, heads = dims
    rows_b = piece // BLOCKS
    half = rows_b // 2
    cols = heads * HEAD_DIM
    hidden_cols = operands[4].shape[1]
    vmem = pl.BlockSpec(memory_space=pltpu.VMEM)
    weights = (shards, wctx, chunk, width)
    turned = (wctx, shards, chunk, piece)
    V = pltpu.VMEM
    shared = (BLOCKS, 2, half, width)
    hidden = (BLOCKS, rows_b, hidden_cols)
    scratch = [
        V(weights, BF16), V(weights, BF16), V(weights, BF16),
        V(turned, BF16), V(turned, BF16),
        V((ctxs, piece, width), BF16),
        V((ctxs, 8, piece), F32), V((ctxs, piece, piece), F32),
        V((ctxs, piece, 2 * cols), BF16), V((ctxs, 2 * cols, piece), BF16), V((ctxs, heads, piece, 256), BF16),
        V((ctxs, piece, piece), F32), V((heads, ctxs, piece, piece), BF16), V((heads, ctxs - 1, piece, piece), BF16),
        V((2 * cols, piece), F32), V((2 * cols, piece), F32), V((piece, LANES), F32), V((BLOCKS, half, width), F32),
        V(shared, BF16), V(hidden, BF16), V(hidden, F32),
        V(shared, BF16), V(hidden, BF16), V(shared, BF16), V((ctxs - 1,) + shared, BF16), V(shared, BF16),
        V(shared, BF16),
        V((4, BLOCKS, 2, half, width), F32), V((4, BLOCKS, half, width), F32),
        V((4, BLOCKS, half, width), BF16), V((4, BLOCKS, half, width), BF16),
        V((3, shards, chunk, width), F32), V((3, shards, chunk, width), BF16), V((3, shards, chunk, width), BF16),
        V((wctx, 3, shards, chunk, width), BF16), V((wctx, 3, shards, chunk, width), BF16),
        V((piece, 2 * cols), F32),
        V((2 * cols, piece), F32), V((piece, 2 * cols), BF16), V((piece, 2 * cols), BF16), V((piece, 2 * cols), BF16),
        V((ctxs, piece, 256), BF16), V((ctxs, 2, piece, LANES), BF16),
        V((BLOCKS, half, width), F32), V((BLOCKS, half, width), F32), V((BLOCKS, half, width), F32),
        V((16, width), F32), V((8, width), F32),
        V((16, width), F32), V((ctxs, 16, width), F32), V((shards, 16, width), F32),
        V((ctxs, 8, width), F32), V((shards, 8, width), F32),
        V((3, chunk, cols), BF16), V((cols, chunk), BF16), V((8, piece), F32), V((8, 2 * cols), F32),
        V((8, piece), F32), V((ctxs - 1, 8, piece), F32), V((8, piece), F32), V((ctxs - 1, 8, piece), F32),
        pltpu.SemaphoreType.DMA((BLOCKS + 5,)), pltpu.SemaphoreType.DMA((min(copies, POOL),)),
        pltpu.SemaphoreType.DMA((copies,)),
    ]
    return pl.pallas_call(
        functools.partial(layer_kernel, dims),
        out_shape=(
            jax.ShapeDtypeStruct((BLOCKS, rows_b, width), BF16),
            jax.ShapeDtypeStruct((BLOCKS, rows_b, width), BF16),
            jax.ShapeDtypeStruct((chunk, width), F32),
            jax.ShapeDtypeStruct((chunk, hidden_cols), F32),
            jax.ShapeDtypeStruct((chunk, hidden_cols), F32),
            jax.ShapeDtypeStruct((24, width), F32),
        ),
        in_specs=[pl.BlockSpec(memory_space=pl.ANY)] * 6 + [vmem] * (len(operands) - 6),
        out_specs=(vmem,) * 6,
        scratch_shapes=scratch,
        compiler_params=pltpu.CompilerParams(
            collective_id=0, has_side_effects=True, vmem_limit_bytes=67_043_328
        ),
        name="layer",
    )(*operands)


def finish_kernel(cols, *refs):
    (lo, tg, ga, gi, gd, small,
     lo_out, tg_out, qkv_out, qv_out, out_out, in_out, down_out, v0, v1, v2, v3, v4, v5, v6, rms_out) = refs
    lo_out[...] = lo[...]
    tg_out[...] = tg[...].astype(F32)

    @pl.when(pl.program_id(0) == 0)
    def _():
        qkv_out[0] = ga[:, 2 * cols:3 * cols]
        qkv_out[1] = ga[:, 0:cols]
        qkv_out[2] = ga[:, cols:2 * cols]
        out_out[...] = jnp.transpose(ga[:, 3 * cols:])
        in_out[...] = gi[...]
        down_out[...] = gd[...]
        qv_out[0:1] = small[18:19, 0:cols]
        qv_out[1:2] = small[17:18, cols:2 * cols]
        for row, ref in zip((0, 1, 2, 16, 3, 4, 5), (v0, v1, v2, v3, v4, v5, v6)):
            ref[...] = small[row]
        count = small[9:10, 0:1] * small.shape[1]
        for i in range(3):
            rms_out[0:1, i:i + 1] = jnp.sqrt(jnp.sum(small[6 + i:7 + i], axis=1, keepdims=True) / count)


def run_finish(cols, *operands):
    blocks, rows_b, width = operands[0].shape
    chunk, hidden_cols = operands[3].shape
    shapes = [
        ((blocks, rows_b, width), BF16), ((blocks, rows_b, width), F32), ((3, chunk, cols), F32), ((2, cols), F32),
        ((cols, chunk), F32), ((chunk, hidden_cols), F32), ((chunk, hidden_cols), F32),
        ((width,), F32), ((width,), F32), ((width,), F32), ((hidden_cols,), F32),
        ((width,), F32), ((width,), F32), ((width,), F32), ((1, 3), F32),
    ]
    rows = pl.BlockSpec((1, rows_b, width), lambda i: (i, 0, 0))

    def fixed(shape):
        return pl.BlockSpec(shape, lambda i: (0,) * len(shape))

    return pl.pallas_call(
        functools.partial(finish_kernel, cols),
        grid=(blocks,),
        out_shape=tuple(jax.ShapeDtypeStruct(*shape) for shape in shapes),
        in_specs=[rows, rows] + [fixed(operand.shape) for operand in operands[2:]],
        out_specs=(rows, rows) + tuple(fixed(shape[0]) for shape in shapes[2:]),
        name="finish",
    )(*operands)


def body(
    sizes,
    tokens, segment_ids, valid_mask, qkv_weight, qv_bias, out_weight, out_bias, norm1_gain, norm1_shift,
    in_weight, in_bias, down_weight, down_bias, norm2_gain, norm2_shift, out_cotangent,
):
    shards, ctxs = sizes
    _, piece, width = tokens.shape
    cols = qkv_weight.shape[2]
    heads = cols // HEAD_DIM
    raw = qkv_weight.shape[1] % 16 == 0 and ctxs <= 2
    if raw:
        wctx = ctxs
        parts = [qkv_weight, out_weight, in_weight, down_weight.T]
        chunk = in_weight.shape[0]
    else:
        wctx = 1
        own = jnp.concatenate([qkv_weight[1], qkv_weight[2], qkv_weight[0], out_weight.T], axis=1)
        own, into, down = (
            lax.all_gather(part, "ctx", axis=0, tiled=True) for part in (own, in_weight, down_weight.T)
        )
        parts = [own, out_weight, into, down]
        chunk = own.shape[0]
    dims = (shards, ctxs, wctx, piece, width, chunk, heads)
    vectors = [out_bias, norm1_gain, norm1_shift, in_bias, down_bias, norm2_gain, norm2_shift]
    results = run_layer(
        dims, COPIES.get((shards, ctxs), 320), tokens.reshape(piece, width), out_cotangent.reshape(piece, width), *parts,
        segment_ids, valid_mask, qv_bias, *vectors
    )
    if raw:
        lo, tg, g_qkv, g_qv, g_out, g_in, g_down, *sums, rms = run_finish(cols, *results)
        return (
            lo.reshape(1, piece, width), tg.reshape(1, piece, width), g_qkv, g_qv, g_out, sums[0], sums[1], sums[2],
            g_in, sums[3], g_down.T, sums[4], sums[5], sums[6], rms.reshape(-1),
        )
    lo, tg, ga, gi, gd, small = results
    ga, gi, gd = (lax.psum_scatter(g, "ctx", scatter_dimension=0, tiled=True) for g in (ga, gi, gd))
    g_qkv = jnp.stack([ga[:, 2 * cols:3 * cols], ga[:, 0:cols], ga[:, cols:2 * cols]])
    sums = jnp.sum(small[6:9], axis=1)
    return (
        lo.reshape(1, piece, width),
        tg.reshape(1, piece, width).astype(F32),
        g_qkv,
        jnp.stack([small[18, 0:cols], small[17, cols:2 * cols]]),
        ga[:, 3 * cols:].T,
        small[0], small[1], small[2],
        gi,
        small[16],
        gd.T,
        small[3], small[4], small[5],
        jnp.sqrt(sums / (small[9, 0] * width)),
    )


def solution(mesh):
    sizes = (mesh.shape["shard"], mesh.shape["ctx"])
    return jax.shard_map(
        functools.partial(body, sizes),
        mesh=mesh,
        in_specs=(
            P("shard", "ctx", None), P("shard", "ctx"), P("shard", "ctx"),
            P(None, ("shard", "ctx"), "tp"), P(None, "tp"), P("tp", ("shard", "ctx")),
            P(), P(), P(),
            P(("shard", "ctx"), "tp"), P("tp"), P("tp", ("shard", "ctx")),
            P(), P(), P(),
            P("shard", "ctx", None),
        ),
        out_specs=(
            P("shard", "ctx", None), P("shard", "ctx", None),
            P(None, ("shard", "ctx"), "tp"), P(None, "tp"), P("tp", ("shard", "ctx")),
            P(), P(), P(),
            P(("shard", "ctx"), "tp"), P("tp"), P("tp", ("shard", "ctx")),
            P(), P(), P(), P(),
        ),
        check_vma=False,
    )
```
